256 devices in a mesh: sub: 2 (over core), row: 16 (over x, y), col: 8 (over z).
Axes of the slice: x: 4, y: 4, z: 8, core: 2. Of those that a mesh axis runs over, the one named last changes fastest.
Arguments:
- front: float32 [16384, 16384], P(('sub', 'row'), 'col'), as said below
- child_blocks: float32 [2, 8192, 8192], P('sub', 'row', 'col'), may hold values from -1 to 1
- child_map: int32 [2, 8192], replicated, may hold values from 0 to 16383, as said below
Outputs:
- factored: float32 [16384, 16384], P(('sub', 'row'), 'col')
The draws below stay inside these ranges and needn't reach their ends.
Inputs may be any that keep to these rules, and one draw needn't show every extreme that they name: Each row of child_map is strictly increasing. Call block b the parent indices b * 32 to b * 32 + 31. Of the entries at positions k * 1024 to (k + 1) * 1024 - 1 of a row, exactly 128 lie in blocks whose number modulo 8 is d, for every k and d. Of the entries at positions k * 512 to (k + 1) * 512 - 1, at most 24 lie in blocks whose number modulo 32 is p, for every k and p; for each child some p takes exactly 24 from every k. The front's diagonal dominates the rows of the pivot block by construction.
All inputs are finite; a program needn't handle non-finite values.
Results may differ from the reference program's by a relative error of at most 0.00012.
Values sent between devices are 32-bit elements; how exact they have to be, the bound alone decides.
A program may use at most 128 MiB of HBM per device.

```python
import jax
import jax.numpy as jnp
from jax import lax

CB = 8192
PW = 512
NB = 32
PF = 16384
PR = 32
PC = 8


def draw_front(key, part):
    span_rows = PF // PR
    span_cols = PF // PC
    index = jnp.arange(PF, dtype=jnp.int32)
    nat_row = (index % span_rows // NB * PR + index // span_rows) * NB + index % NB
    nat_col = (index % span_cols // NB * PC + index // span_cols) * NB + index % NB
    key_base = jax.random.fold_in(key, 3)
    key_diag = jax.random.fold_in(key, 5)
    base = jax.random.truncated_normal(key_base, -4.0, 4.0, (PF, PF), jnp.float32)
    row_head = nat_row[:, None] < PW
    col_head = nat_col[None, :] < PW
    scale = jnp.where(col_head, jnp.where(row_head, 0.25, 9.0), 1.0)
    diag_vals = jax.random.uniform(key_diag, (PF,), jnp.float32, 3.0 * PW, 6.0 * PW)
    same = nat_row[:, None] == nat_col[None, :]
    return jnp.where(same, diag_vals[:, None], base * scale).astype(jnp.float32)


def draw_child_map(key, part):
    blocks = PF // NB
    groups = blocks // 16
    half = NB // 2
    quarter = NB // 4
    results = []
    for child in range(2):
        child_key = jax.random.fold_in(key, child + 11)
        key_shift = jax.random.fold_in(child_key, 1)
        key_owner = jax.random.fold_in(child_key, 2)
        key_place = jax.random.fold_in(child_key, 3)
        shift = jax.random.randint(key_shift, (groups, 8), -quarter, quarter + 1)
        first = jnp.arange(groups, dtype=jnp.int32)[:, None] * 16 + jnp.arange(8, dtype=jnp.int32)[None, :]
        second = first + 8
        chosen = jax.random.randint(key_owner, (), 0, PR)
        shift = jnp.where(first % PR == chosen, quarter, jnp.where(second % PR == chosen, -quarter, shift))
        counts = jnp.concatenate([half + shift, half - shift], axis=1).reshape(blocks)
        scores = jax.random.randint(key_place, (blocks, NB), 0, 1 << 20) * NB + jnp.arange(NB, dtype=jnp.int32)[None, :]
        ranks = jnp.argsort(jnp.argsort(scores, axis=1), axis=1)
        keep = (ranks < counts[:, None]).reshape(PF)
        results.append(jnp.nonzero(keep, size=CB)[0].astype(jnp.int32))
    return jnp.stack(results)


def shard_levels(stream_key, dims, pieces, smallest, largest):
    gain = 1.0
    for axis_at, shards_of in pieces:
        heights = jax.random.uniform(jax.random.fold_in(jax.random.fold_in(stream_key, 6), axis_at), (shards_of,), jnp.float32, smallest / len(pieces), largest / len(pieces))
        gain = gain * jnp.repeat(jnp.exp(heights), dims[axis_at] // shards_of).reshape((-1,) + (1,) * (len(dims) - 1 - axis_at))
    return gain


def centred(own_key, extent, spread, bound, cuts=(), held_as=jnp.bfloat16):
    result = spread * jax.random.normal(own_key, extent, jnp.float32)
    if cuts:
        result = result * shard_levels(own_key, extent, cuts, -0.22, 0.18)
    return jnp.clip(result, -bound, bound).astype(held_as)


def setup_inputs(seed: int = 0) -> dict:
    key_list = jax.random.split(jax.random.key(seed), 4)
    front = draw_front(jax.random.fold_in(key_list[3], 71), 0)
    child_blocks = centred(key_list[1], (2, CB, CB), 0.25, 1.0, ((0, 2), (1, 16), (2, 8)), jnp.float32)
    child_map = draw_child_map(jax.random.fold_in(key_list[3], 71), 0)
    return {"front": front, "child_blocks": child_blocks, "child_map": child_map}


def natural_of(stored, groups):
    span = PF // groups
    return (stored % span // NB * groups + stored // span) * NB + stored % NB

def stored_of(natural, groups):
    span = PF // groups
    blocks = natural // NB
    return blocks % groups * span + blocks // groups * NB + natural % NB

def reference(front, child_blocks, child_map):
    index = jnp.arange(PF, dtype=jnp.int32)
    nat_row = natural_of(index, PR)
    nat_col = natural_of(index, PC)
    lower = nat_row[:, None] >= nat_col[None, :]
    assembled = jnp.where(lower, front, jnp.float32(0.0))
    child_index = jnp.arange(CB, dtype=jnp.int32)
    child_lower = child_index[:, None] >= child_index[None, :]
    for child in range(2):
        contribution = jnp.where(child_lower, child_blocks[child], jnp.float32(0.0))
        targets = child_map[child]
        row_pos = stored_of(targets, PR)
        col_pos = stored_of(targets, PC)
        assembled = assembled.at[row_pos[:, None], col_pos[None, :]].add(contribution)
    pivots = jnp.arange(PW, dtype=jnp.int32)
    panel_cols = stored_of(pivots, PC)
    panel = assembled[:, panel_cols]
    corner = panel[stored_of(pivots, PR)]
    pivot = jnp.tril(corner) + jnp.tril(corner, -1).T
    chol = jnp.linalg.cholesky(pivot)
    solved = lax.linalg.triangular_solve(chol, panel, left_side=False, lower=True, transpose_a=True)
    factor_rows = jnp.where(nat_row[:, None] < PW, chol[jnp.clip(nat_row, 0, PW - 1)], solved)
    factor_cols = factor_rows[stored_of(nat_col, PR)]
    update = assembled - jnp.dot(factor_rows.astype(jnp.float32), factor_cols.T.astype(jnp.float32), precision=lax.Precision.HIGHEST, preferred_element_type=jnp.float32)
    update = update.at[:, panel_cols].set(factor_rows)
    return jnp.where(lower, update, jnp.float32(0.0))
```

```python
import functools

import jax
import jax.numpy as jnp
from jax import lax
from jax.experimental import pallas as pl
from jax.experimental.pallas import tpu as pltpu
from jax.sharding import PartitionSpec as P

PW = 512
NB = 32
CAP = 24
F32 = jnp.float32
BF16 = jnp.bfloat16
I32 = jnp.int32
AXES = ("sub", "row", "col")


def iota(shape, dim):
    return lax.broadcasted_iota(I32, shape, dim)


def onehot(cond):
    return jnp.where(cond, F32(1.0), F32(0.0)).astype(BF16)


def split(value):
    high = value.astype(BF16)
    return high, (value - high.astype(F32)).astype(BF16)


def mm(a, b):
    return lax.dot_general(a, b, (((1,), (0,)), ((), ())), preferred_element_type=F32)


def mt(a, b):
    return lax.dot_general(a, b, (((1,), (1,)), ((), ())), preferred_element_type=F32)


def params(mib=None):
    return pltpu.CompilerParams(vmem_limit_bytes=None if mib is None else mib << 20)


VM = pl.BlockSpec(memory_space=pltpu.VMEM)
SM = pl.BlockSpec(memory_space=pltpu.SMEM)


def ranks_of(owner, groups, rows):
    n = owner.shape[1]
    member = jnp.where(owner == iota((rows, n), 0), F32(1.0), F32(0.0))
    upto = onehot(iota((n, n), 0) <= iota((n, n), 1))
    counts = mm(member.astype(BF16), upto)
    return (jnp.sum(counts * member, axis=0, keepdims=True) - 1.0).astype(I32)


def columns_kernel(at_ref, map_ref, x_ref, o_ref):
    rows, cols = x_ref.shape
    row0, col0 = at_ref[0], at_ref[1]
    keep = row0 + iota((rows, cols), 0) >= col0 + iota((rows, cols), 1)
    high, low = split(jnp.where(keep, x_ref[...], F32(0.0)))
    owner = (map_ref[...] >> 5) & 7
    slot = owner * 128 + ranks_of(owner, 8, 16)
    for pair in range(4):
        pick = onehot(slot == pair * 256 + iota((256, cols), 0))
        out = mt(high, pick) + mt(low, pick)
        o_ref[2 * pair] = out[:, :128]
        o_ref[2 * pair + 1] = out[:, 128:]


def rows_kernel(map_ref, x_ref, o_ref, p_ref):
    owner = (map_ref[...] >> 5) & 31
    slot = owner * CAP + ranks_of(owner, 32, 32)
    n = owner.shape[1]
    pick = onehot(slot == iota((32 * CAP, n), 0))
    for pair in range(4):
        high, low = split(jnp.concatenate([x_ref[2 * pair], x_ref[2 * pair + 1]], axis=1))
        out = mm(pick, high) + mm(pick, low)
        o_ref[:, pl.ds(pair * 256, 256)] = out
        if pair == 0:
            p_ref[...] = out[:, :128]


def index_kernel(at_ref, map_ref, slot_ref, col_ref):
    rg, cg = at_ref[0], at_ref[1]
    upto = onehot(iota((512, 512), 0) <= iota((512, 512), 1))
    before64 = onehot(iota((64, 64), 1) < iota((64, 64), 0))
    before32 = onehot(iota((32, 32), 0) < iota((32, 32), 1))
    for child in range(2):
        full = map_ref[child]
        match = onehot(((full >> 5) & 31) == rg)
        counts = mm(match, upto)
        slots = jnp.zeros((NB, 16), F32)
        present = jnp.zeros((64, NB), F32)
        for k in range(16):
            here = full[k : k + 1, :]
            block = here >> 5
            off = jnp.where((here & 31) == iota((NB, 512), 0), F32(1.0), F32(0.0))
            own_rows = onehot(
                jnp.where((block & 31) == rg, block >> 5, -1) == iota((16, 512), 0)
            )
            ranked = (off * counts[k : k + 1, :]).astype(BF16)
            off = off.astype(BF16)
            slots = slots + mt(ranked, own_rows) + F32(k * CAP) * mt(off, own_rows)
            own_cols = onehot(jnp.where((block & 7) == cg, block >> 3, -1) == iota((64, 512), 0))
            present = present + mt(own_cols, off)
        slot_ref[child] = slots.astype(I32) - 1
        pb = present.astype(BF16)
        ahead = jnp.sum(mm(before64, pb), axis=1, keepdims=True)
        place = ahead + mm(pb, before32)
        col_ref[child] = jnp.where(present > 0.5, place.astype(I32), -1)


def natural_lower(rg, cg, rows, cols, col0):
    r, c = iota((rows, cols), 0), col0 + iota((rows, cols), 1)
    nat_row = ((r >> 5) * 32 + rg) * 32 + (r & 31)
    nat_col = ((c >> 5) * 8 + cg) * 32 + (c & 31)
    return nat_row >= nat_col


def row_picker(slots, n):
    parts = [onehot(slots[:, b : b + 1] == iota((NB, n), 1)) for b in range(16)]
    return jnp.concatenate(parts, axis=0)


def panel_kernel(at_ref, slot_ref, col_ref, x_ref, front_ref, o_ref):
    rg, cg = at_ref[0], at_ref[1]
    total = jnp.where(natural_lower(rg, cg, 512, 128, 0), front_ref[...], F32(0.0))
    n = x_ref.shape[1]
    for child in range(2):
        pick = row_picker(slot_ref[child], n)
        high, low = split(x_ref[child])
        high, low = split(mm(pick, high) + mm(pick, low))
        put = onehot(col_ref[child] == iota((128, 128), 0))
        total = total + mm(high, put) + mm(low, put)
    left = iota((64, 128), 1) < 64
    for t in range(4):
        a = total[t * 128 : t * 128 + 64]
        b = total[t * 128 + 64 : t * 128 + 128]
        o_ref[t * 64 : t * 64 + 64, :] = jnp.where(left, a, pltpu.roll(b, 64, 1))


def sweep(w):
    tiles = [w[8 * i : 8 * i + 8, :] for i in range(16)]
    lane = iota((8, 128), 1)
    sub = iota((8, 128), 0)
    for k in range(128):
        own, s = k // 8, k % 8
        row = tiles[own][s : s + 1, :]
        inv = 1.0 / row[:, k : k + 1]
        pivot_row = jnp.where(lane[:1] == k, F32(1.0), row)
        scaled = pivot_row * inv
        for i in range(own, 16):
            t = tiles[i]
            col = t[:, k : k + 1]
            new = jnp.where(lane == k, F32(0.0), t) - col * scaled
            tiles[i] = jnp.where(sub > s, new, t) if i == own else new
    w = jnp.concatenate(tiles, axis=0)
    r, c = iota((128, 128), 0), iota((128, 128), 1)
    diag = jnp.sum(jnp.where(r == c, w, F32(0.0)), axis=1, keepdims=True)
    scale = 1.0 / jnp.sqrt(diag)
    upper = jnp.where(c >= r, w, F32(0.0)) * scale
    inverse = jnp.where(c < r, w, jnp.where(c == r, F32(1.0), F32(0.0))) * scale
    return upper, inverse


def exact(a, b, dims):
    return lax.dot_general(
        a, b, (dims, ((), ())), precision=lax.Precision.HIGHEST, preferred_element_type=F32
    )


def factor_kernel(s_ref, low_ref, inv_ref, w_ref):
    r, c = iota((PW, PW), 0), iota((PW, PW), 1)
    raw = s_ref[...]
    w_ref[:, :PW] = jnp.where(r >= c, raw, F32(0.0)) + jnp.where(r > c, raw, F32(0.0)).T
    w_ref[:, PW:] = jnp.where(r == c, F32(1.0), F32(0.0))

    def step(kb, carry):
        at = pl.multiple_of(kb * 128, 128)
        upper, inverse = sweep(w_ref[pl.ds(at, 128), pl.ds(at, 128)])
        rows = exact(inverse, w_ref[pl.ds(at, 128), :], ((1,), (0,)))
        lanes = iota((128, PW), 1)
        ahead = jnp.where(lanes >= at + 128, rows[:, :PW], F32(0.0))
        w_ref[...] = w_ref[...] - exact(ahead, rows, ((0,), (0,)))
        w_ref[pl.ds(at, 128), :] = jnp.concatenate([ahead, rows[:, PW:]], axis=1)
        w_ref[pl.ds(at, 128), pl.ds(at, 128)] = upper
        return carry

    lax.fori_loop(0, PW // 128, step, 0)
    low_ref[...] = w_ref[:, :PW].T
    turned = w_ref[:, PW:].T
    for c8 in range(8):
        for half in range(2):
            src = (half * 8 + c8) * NB
            inv_ref[(c8 * 2 + half) * NB : (c8 * 2 + half + 1) * NB, :] = turned[src : src + NB, :]


def unpack(pieces, left):
    top, bottom = [], []
    for p in range(4):
        a, b = pieces[2 * p], pieces[2 * p + 1]
        top.append(jnp.where(left, a, pltpu.roll(b, 64, 1)))
        bottom.append(jnp.where(left, pltpu.roll(a, 64, 1), b))
    return jnp.concatenate(
        [jnp.concatenate(top, axis=1), jnp.concatenate(bottom, axis=1)], axis=0
    )


def three(a, b, dot):
    return dot(a[0], b[0]) + (dot(a[0], b[1]) + dot(a[1], b[0]))


def final_kernel(
    at_ref, slot_ref, col_ref, x_ref, front_ref, own_ref, cols_ref, inv_ref, low_ref,
    o_ref, ih, il, fh, fl, yh, yl, panel_ref,
):
    rg, cg = at_ref[0], at_ref[1]
    ct = pl.program_id(0)
    left = iota((64, 128), 1) < 64

    @pl.when(ct == 0)
    def _():
        ih[...], il[...] = split(inv_ref[...])
        inv = ih[...], il[...]
        for t in range(4):
            tile = unpack([own_ref[c, t * 64 : t * 64 + 64, :] for c in range(8)], left)
            rows = three(split(tile), inv, mm)
            if t == 0:
                keep = (iota((128, PW), 0) < NB) & (rg < 16)
                known = jnp.concatenate([low_ref[...], jnp.zeros((128 - NB, PW), F32)], axis=0)
                rows = jnp.where(keep, known, rows)
            fh[t * 128 : t * 128 + 128, :], fl[t * 128 : t * 128 + 128, :] = split(rows)
        lane = iota((PW, 128), 1)
        nat = ((lane >> 5) * 8 + cg) * 32 + (lane & 31)
        pick = onehot((nat == iota((PW, 128), 0)) & (lane < 64))
        panel_ref[...] = mm(fh[...], pick) + mm(fl[...], pick)
        n = x_ref.shape[1]
        for child in range(2):
            pick = row_picker(slot_ref[child], n)
            high, low = split(x_ref[child])
            yh[child], yl[child] = split(mm(pick, high) + mm(pick, low))

    inv = ih[...], il[...]
    parts = []
    for i in range(4):
        tile = unpack([cols_ref[i * 8 + c] for c in range(8)], left)
        parts.append(three(split(tile), inv, mm))
    cols = jnp.concatenate(
        [parts[i][q * NB : q * NB + NB] for q in range(4) for i in range(4)], axis=0
    )
    total = front_ref[...] - three((fh[...], fl[...]), split(cols), mt)
    for child in range(2):
        put = onehot(col_ref[child] == iota((1024, 512), 0))
        total = total + mm(yh[child], put) + mm(yl[child], put)
    total = jnp.where(natural_lower(rg, cg, 512, 512, ct * 512), total, F32(0.0))
    o_ref[...] = total

    @pl.when(ct == 0)
    def _():
        lane = iota((512, 128), 1)
        value = jnp.where(
            natural_lower(rg, cg, 512, 128, 0), panel_ref[...], F32(0.0)
        )
        o_ref[:, :128] = jnp.where(lane < 64, value, total[:, :128])


def body(front, child_blocks, child_map):
    sub, row, cg = lax.axis_index("sub"), lax.axis_index("row"), lax.axis_index("col")
    rg = sub * 16 + row
    at = jnp.stack([rg, cg]).astype(I32)
    own_map = lax.dynamic_index_in_dim(child_map, sub, 0, keepdims=True)
    row_targets = lax.dynamic_slice_in_dim(own_map, row * 512, 512, axis=1)
    col_targets = lax.dynamic_slice_in_dim(own_map, cg * 1024, 1024, axis=1)
    start = jnp.stack([row * 512, cg * 1024]).astype(I32)

    by_column = pl.pallas_call(
        columns_kernel,
        out_shape=jax.ShapeDtypeStruct((8, 512, 128), F32),
        in_specs=[SM, VM, VM],
        out_specs=VM,
        name="columns",
        compiler_params=params(40),
    )(start, col_targets, child_blocks[0])
    moved = lax.all_to_all(by_column, "col", split_axis=0, concat_axis=0, tiled=True)

    slots, cols = pl.pallas_call(
        index_kernel,
        out_shape=(
            jax.ShapeDtypeStruct((2, NB, 16), I32),
            jax.ShapeDtypeStruct((2, 64, NB), I32),
        ),
        in_specs=[SM, VM],
        out_specs=(VM, VM),
        name="index",
        compiler_params=params(40),
        cost_estimate=pl.CostEstimate(flops=10**8, bytes_accessed=10**7, transcendentals=0),
    )(at, child_map.reshape(2, 16, 512))
    cols = cols.reshape(2, 1, 2048)

    packed, packed_panel = pl.pallas_call(
        rows_kernel,
        out_shape=(
            jax.ShapeDtypeStruct((32 * CAP, 1024), F32),
            jax.ShapeDtypeStruct((32 * CAP, 128), F32),
        ),
        in_specs=[VM, VM],
        out_specs=(VM, VM),
        name="rows",
        compiler_params=params(40),
    )(row_targets, moved)
    got_panel = lax.all_to_all(
        packed_panel.reshape(32, CAP, 128), ("sub", "row"), split_axis=0, concat_axis=0, tiled=True
    )
    packed, got_panel = lax.optimization_barrier((packed, got_panel))
    received = lax.all_to_all(
        packed.reshape(32, CAP, 1024), ("sub", "row"), split_axis=0, concat_axis=0, tiled=True
    )

    piece = pl.pallas_call(
        panel_kernel,
        out_shape=jax.ShapeDtypeStruct((256, 128), F32),
        grid=(1,),
        in_specs=[
            SM,
            pl.BlockSpec((2, NB, 16), lambda i: (0, 0, 0)),
            pl.BlockSpec((2, 1, 128), lambda i: (0, 0, 0)),
            pl.BlockSpec((2, 16 * CAP, 128), lambda i: (0, 0, 0)),
            pl.BlockSpec((512, 128), lambda i: (0, 0)),
        ],
        out_specs=pl.BlockSpec((256, 128), lambda i: (0, 0)),
        name="panel",
        compiler_params=params(40),
    )(at, slots, cols, got_panel.reshape(2, 16 * CAP, 128), front)

    head = lax.all_gather(piece[:NB, :64], AXES, axis=0)
    head = head.reshape(32, 8, NB, 2, NB)[:16].transpose(0, 2, 3, 1, 4).reshape(PW, PW)
    own_rows = lax.all_gather(piece, "col", axis=0)
    swaps = [
        ((8 * i + a) * 8 + b, (8 * i + b) * 8 + a)
        for i in range(4)
        for a in range(8)
        for b in range(8)
    ]
    swapped = lax.ppermute(piece, AXES, swaps)
    col_rows = lax.all_gather(swapped, ("sub", "row"), axis=0)

    lower, inverse = pl.pallas_call(
        factor_kernel,
        out_shape=(
            jax.ShapeDtypeStruct((PW, PW), F32),
            jax.ShapeDtypeStruct((PW, PW), F32),
        ),
        in_specs=[VM],
        out_specs=(VM, VM),
        scratch_shapes=[pltpu.VMEM((PW, 2 * PW), F32)],
        name="factor",
        compiler_params=params(40),
        cost_estimate=pl.CostEstimate(flops=3 * 10**10, bytes_accessed=10**8, transcendentals=0),
    )(head)

    return pl.pallas_call(
        final_kernel,
        out_shape=jax.ShapeDtypeStruct((512, 2048), F32),
        grid=(4,),
        in_specs=[
            SM,
            pl.BlockSpec((2, NB, 16), lambda i: (0, 0, 0)),
            pl.BlockSpec((2, 1, 512), lambda i: (0, 0, i)),
            pl.BlockSpec((2, 16 * CAP, 1024), lambda i: (0, 0, 0)),
            pl.BlockSpec((512, 512), lambda i: (0, i)),
            pl.BlockSpec((8, 256, 128), lambda i: (0, 0, 0)),
            pl.BlockSpec((32, 64, 128), lambda i: (0, i, 0)),
            pl.BlockSpec((PW, PW), lambda i: (0, 0)),
            pl.BlockSpec((NB, PW), lambda i: (0, 0)),
        ],
        out_specs=pl.BlockSpec((512, 512), lambda i: (0, i)),
        scratch_shapes=[
            pltpu.VMEM((PW, PW), BF16),
            pltpu.VMEM((PW, PW), BF16),
            pltpu.VMEM((512, PW), BF16),
            pltpu.VMEM((512, PW), BF16),
            pltpu.VMEM((2, 512, 1024), BF16),
            pltpu.VMEM((2, 512, 1024), BF16),
            pltpu.VMEM((512, 128), F32),
        ],
        name="final",
        compiler_params=params(60),
    )(
        at,
        slots,
        cols,
        received.reshape(2, 16 * CAP, 1024),
        front,
        own_rows,
        col_rows,
        inverse,
        lax.dynamic_slice_in_dim(lower, jnp.minimum(rg, 15) * NB, NB, axis=0),
    )


def solution(mesh):
    return jax.shard_map(
        body,
        mesh=mesh,
        in_specs=(P(("sub", "row"), "col"), P("sub", "row", "col"), P()),
        out_specs=P(("sub", "row"), "col"),
        check_vma=False,
    )
```

```python
import functools

import jax
import jax.numpy as jnp
from jax import lax
from jax.experimental import pallas as pl
from jax.experimental.pallas import tpu as pltpu
from jax.sharding import PartitionSpec as P

PW = 512
NB = 32
CAP = 24
F32 = jnp.float32
BF16 = jnp.bfloat16
I32 = jnp.int32
AXES = ("sub", "row", "col")


def iota(shape, dim):
    return lax.broadcasted_iota(I32, shape, dim)


def onehot(cond):
    return jnp.where(cond, F32(1.0), F32(0.0)).astype(BF16)


def split(value):
    high = value.astype(BF16)
    return high, (value - high.astype(F32)).astype(BF16)


def mm(a, b):
    return lax.dot_general(a, b, (((1,), (0,)), ((), ())), preferred_element_type=F32)


def mt(a, b):
    return lax.dot_general(a, b, (((1,), (1,)), ((), ())), preferred_element_type=F32)


def params(mib=None):
    return pltpu.CompilerParams(vmem_limit_bytes=None if mib is None else mib << 20)


VM = pl.BlockSpec(memory_space=pltpu.VMEM)
SM = pl.BlockSpec(memory_space=pltpu.SMEM)


def ranks_of(owner, groups, rows):
    n = owner.shape[1]
    member = jnp.where(owner == iota((rows, n), 0), F32(1.0), F32(0.0))
    upto = onehot(iota((n, n), 0) <= iota((n, n), 1))
    counts = mm(member.astype(BF16), upto)
    return (jnp.sum(counts * member, axis=0, keepdims=True) - 1.0).astype(I32)


def columns_kernel(at_ref, map_ref, x_ref, o_ref):
    rows, cols = x_ref.shape
    row0, col0 = at_ref[0], at_ref[1]
    keep = row0 + iota((rows, cols), 0) >= col0 + iota((rows, cols), 1)
    high, low = split(jnp.where(keep, x_ref[...], F32(0.0)))
    owner = (map_ref[...] >> 5) & 7
    slot = owner * 128 + ranks_of(owner, 8, 16)
    for pair in range(4):
        pick = onehot(slot == pair * 256 + iota((256, cols), 0))
        out = mt(high, pick) + mt(low, pick)
        o_ref[2 * pair] = out[:, :128]
        o_ref[2 * pair + 1] = out[:, 128:]


def rows_kernel(map_ref, x_ref, o_ref):
    owner = (map_ref[...] >> 5) & 31
    slot = owner * CAP + ranks_of(owner, 32, 32)
    n = owner.shape[1]
    pick = onehot(slot == iota((32 * CAP, n), 0))
    for pair in range(4):
        high, low = split(jnp.concatenate([x_ref[2 * pair], x_ref[2 * pair + 1]], axis=1))
        out = mm(pick, high) + mm(pick, low)
        o_ref[:, pl.ds(pair * 256, 256)] = out


def index_kernel(at_ref, map_ref, slot_ref, col_ref):
    rg, cg = at_ref[0], at_ref[1]
    upto = onehot(iota((512, 512), 0) <= iota((512, 512), 1))
    before64 = onehot(iota((64, 64), 1) < iota((64, 64), 0))
    before32 = onehot(iota((32, 32), 0) < iota((32, 32), 1))
    for child in range(2):
        full = map_ref[child]
        match = onehot(((full >> 5) & 31) == rg)
        counts = mm(match, upto)
        slots = jnp.zeros((NB, 16), F32)
        present = jnp.zeros((64, NB), F32)
        for k in range(16):
            here = full[k : k + 1, :]
            block = here >> 5
            off = jnp.where((here & 31) == iota((NB, 512), 0), F32(1.0), F32(0.0))
            own_rows = onehot(
                jnp.where((block & 31) == rg, block >> 5, -1) == iota((16, 512), 0)
            )
            ranked = (off * counts[k : k + 1, :]).astype(BF16)
            off = off.astype(BF16)
            slots = slots + mt(ranked, own_rows) + F32(k * CAP) * mt(off, own_rows)
            own_cols = onehot(jnp.where((block & 7) == cg, block >> 3, -1) == iota((64, 512), 0))
            present = present + mt(own_cols, off)
        slot_ref[child] = slots.astype(I32) - 1
        pb = present.astype(BF16)
        ahead = jnp.sum(mm(before64, pb), axis=1, keepdims=True)
        place = ahead + mm(pb, before32)
        col_ref[child] = jnp.where(present > 0.5, place.astype(I32), -1)


def natural_lower(rg, cg, rows, cols, col0):
    r, c = iota((rows, cols), 0), col0 + iota((rows, cols), 1)
    nat_row = ((r >> 5) * 32 + rg) * 32 + (r & 31)
    nat_col = ((c >> 5) * 8 + cg) * 32 + (c & 31)
    return nat_row >= nat_col


def row_picker(slots, n):
    parts = [onehot(slots[:, b : b + 1] == iota((NB, n), 1)) for b in range(16)]
    return jnp.concatenate(parts, axis=0)


def sweep(w):
    tiles = [w[8 * i : 8 * i + 8, :] for i in range(16)]
    lane = iota((8, 128), 1)
    sub = iota((8, 128), 0)
    for k in range(128):
        own, s = k // 8, k % 8
        row = tiles[own][s : s + 1, :]
        inv = 1.0 / row[:, k : k + 1]
        pivot_row = jnp.where(lane[:1] == k, F32(1.0), row)
        scaled = pivot_row * inv
        for i in range(own, 16):
            t = tiles[i]
            col = t[:, k : k + 1]
            new = jnp.where(lane == k, F32(0.0), t) - col * scaled
            tiles[i] = jnp.where(sub > s, new, t) if i == own else new
    w = jnp.concatenate(tiles, axis=0)
    r, c = iota((128, 128), 0), iota((128, 128), 1)
    diag = jnp.sum(jnp.where(r == c, w, F32(0.0)), axis=1, keepdims=True)
    scale = 1.0 / jnp.sqrt(diag)
    upper = jnp.where(c >= r, w, F32(0.0)) * scale
    inverse = jnp.where(c < r, w, jnp.where(c == r, F32(1.0), F32(0.0))) * scale
    return upper, inverse


def exact(a, b, dims):
    return lax.dot_general(
        a, b, (dims, ((), ())), precision=lax.Precision.HIGHEST, preferred_element_type=F32
    )


def remote(src, dst, send, recv, device):
    return pltpu.make_async_remote_copy(
        src_ref=src, dst_ref=dst, send_sem=send, recv_sem=recv, device_id=device,
        device_id_type=pl.DeviceIdType.MESH,
    )


def panel_kernel(
    cmap_ref, rmap_ref, slot_ref, child_ref, front_ref,
    low_ref, inv_ref, own_ref, cols_ref,
    pan_send, pan_recv, rows_send, rows_recv, piece, swapped, head_send, head_recv, sbuf, w_ref,
    pan_s, pan_r, row_s, row_r, head_s, head_r, own_s, own_r, swap_s, swap_r, piv_s, piv_r,
    fan_s, fan_r, pass_s, loc_s,
):
    sub, row, cg = lax.axis_index("sub"), lax.axis_index("row"), lax.axis_index("col")
    rg = sub * 16 + row
    quarter, place = rg // 8, rg % 8
    mate = quarter * 8 + cg
    mate_id = (mate // 16, mate % 16, place)
    moves = place != cg
    twin = (1 - sub, row, cg)

    def each(first, last, fn):
        def go(q, carry):
            fn(q)
            return carry

        lax.fori_loop(first, last, go, 0)

    def line(q):
        return (cg + q) % 8

    def plane(q):
        p = (rg + q) % 32
        return p, (p // 16, p % 16, cg)

    def chip(q):
        r = (row + q) % 16
        return r, (sub, r, cg)

    barrier = pltpu.get_barrier_semaphore()

    def greet(device):
        pl.semaphore_signal(barrier, inc=1, device_id=device, device_id_type=pl.DeviceIdType.MESH)

    each(1, 8, lambda q: greet((sub, row, line(q))))
    each(1, 32, lambda q: greet(plane(q)[1]))

    @pl.when(moves)
    def _():
        greet(mate_id)

    pl.semaphore_wait(barrier, jnp.where(moves, 39, 38))

    pan_recv[64:, :] = jnp.zeros((64, 512), F32)

    def to_line(q):
        return remote(
            pan_send.at[q], pan_recv.at[pl.ds(0, 64)], pan_s.at[q], pan_r, (sub, row, q)
        )

    @pl.when(cg == 0)
    def _():
        keep = row * 512 + iota((512, 512), 0) >= iota((512, 512), 1)
        high, low = split(jnp.where(keep, child_ref[...], F32(0.0)))
        for q in range(7, -1, -1):
            n = iota((64, 512), 0)
            nat = ((n >> 5) * 8 + q) * NB + (n & 31)
            pick = onehot(cmap_ref[...] == nat)
            out = mt(pick, high) + mt(pick, low)
            if q == 0:
                pan_recv[:64, :] = out
            else:
                pan_send[q] = out
                to_line(q).start()

    owner = (rmap_ref[...] >> 5) & 31
    slot = owner * CAP + ranks_of(owner, 32, 32)
    pick_rows = onehot(slot == iota((32 * CAP, 512), 0))

    @pl.when(cg != 0)
    def _():
        to_line(cg).wait_recv()

    high, low = split(pan_recv[...])
    out = mt(pick_rows, high) + mt(pick_rows, low)
    for p in range(32):
        rows_send[p] = out[p * CAP : p * CAP + CAP, :]

    def to_plane(q):
        p, device = plane(q)
        return remote(rows_send.at[p], rows_recv.at[rg], row_s.at[p], row_r.at[rg], device)

    def from_plane(q):
        p, device = plane(q)
        return remote(rows_send.at[p], rows_recv.at[p], row_s.at[p], row_r.at[p], device)

    each(1, 32, lambda q: to_plane(q).start())
    rows_recv[rg] = rows_send[rg]
    total = jnp.where(natural_lower(rg, cg, 512, 128, 0), front_ref[...], F32(0.0))
    picks = [row_picker(slot_ref[child], 16 * CAP) for child in range(2)]
    each(1, 32, lambda q: from_plane(q).wait_recv())
    for child in range(2):
        got = rows_recv[child * 16 : child * 16 + 16].reshape(16 * CAP, 128)
        high, low = split(got)
        total = total + mm(picks[child], high) + mm(picks[child], low)
    left = iota((64, 128), 1) < 64
    for t in range(4):
        a = total[t * 128 : t * 128 + 64]
        b = total[t * 128 + 64 : t * 128 + 128]
        piece[t * 64 : t * 64 + 64, :] = jnp.where(left, a, pltpu.roll(b, 64, 1))
    head_send[...] = total[:NB, :]

    def head(q, at):
        return remote(
            head_send, head_recv.at[at], head_s.at[q], head_r.at[at], (sub, row, line(q))
        )

    def swap():
        return remote(piece, swapped, swap_s, swap_r, mate_id)

    def own(q, at):
        return remote(piece, own_ref.at[at], own_s.at[q], own_r.at[at], (sub, row, line(q)))

    own_local = pltpu.make_async_copy(piece, own_ref.at[cg], loc_s.at[0])

    @pl.when(sub == 0)
    def _():
        each(1, 8, lambda q: head(q, cg).start())

    @pl.when(moves)
    def _():
        swap().start()

    head_recv[cg] = head_send[...]

    def pivot(q, at):
        return remote(sbuf.at[at], sbuf.at[at], piv_s.at[q], piv_r.at[at], chip(q)[1])

    def pivot_twin(at):
        return remote(sbuf.at[at], sbuf.at[at], piv_s.at[16 + at], piv_r.at[at], (1, row, cg))

    @pl.when(sub == 0)
    def _():
        each(1, 8, lambda q: head(q, line(q)).wait_recv())
        half = iota((NB, 128), 1) < 64
        rows = [
            jnp.where(half, head_recv[2 * p], pltpu.roll(head_recv[2 * p + 1], 64, 1))
            for p in range(4)
        ]
        sbuf[row] = jnp.concatenate(rows, axis=1)
        each(1, 16, lambda q: pivot(q, row).start())
        pivot_twin(row).start()

    @pl.when(moves)
    def _():
        swap().wait_recv()

    @pl.when(jnp.logical_not(moves))
    def _():
        swapped[...] = piece[...]

    def fan(q, at):
        return remote(swapped, cols_ref.at[at], fan_s.at[q], fan_r.at[at], chip(q)[1])

    def hand(at, src):
        return remote(src, cols_ref.at[at], pass_s.at[at % 16], fan_r.at[at], twin)

    def twin_hand(at):
        return remote(swapped, cols_ref.at[at], pass_s.at[at % 16], fan_r.at[at], twin)

    cols_local = pltpu.make_async_copy(swapped, cols_ref.at[rg], loc_s.at[1])
    each(1, 16, lambda q: fan(q, rg).start())
    hand(rg, swapped).start()
    cols_local.start()
    each(1, 8, lambda q: own(q, cg).start())
    own_local.start()

    @pl.when(sub == 0)
    def _():
        def relay(q):
            at = chip(q)[0]
            pivot(q, at).wait_recv()
            pivot_twin(at).start()

        each(1, 16, relay)

    @pl.when(sub == 1)
    def _():
        each(0, 16, lambda q: pivot_twin(q).wait_recv())

    turned = sbuf[...].reshape(PW, PW).T
    for c8 in range(8):
        for half in range(2):
            src = (c8 * 2 + half) * NB
            w_ref[(half * 8 + c8) * NB : (half * 8 + c8 + 1) * NB, :PW] = turned[src : src + NB, :]
    r, c = iota((PW, PW), 0), iota((PW, PW), 1)
    raw = w_ref[:, :PW]
    w_ref[:, :PW] = jnp.where(c >= r, raw, F32(0.0)) + jnp.where(c > r, raw, F32(0.0)).T
    w_ref[:, PW:] = jnp.where(r == c, F32(1.0), F32(0.0))

    def step(kb, carry):
        at = pl.multiple_of(kb * 128, 128)
        upper, inverse = sweep(w_ref[pl.ds(at, 128), pl.ds(at, 128)])
        rows = exact(inverse, w_ref[pl.ds(at, 128), :], ((1,), (0,)))
        lanes = iota((128, PW), 1)
        ahead = jnp.where(lanes >= at + 128, rows[:, :PW], F32(0.0))
        w_ref[...] = w_ref[...] - exact(ahead, rows, ((0,), (0,)))
        w_ref[pl.ds(at, 128), :] = jnp.concatenate([ahead, rows[:, PW:]], axis=1)
        w_ref[pl.ds(at, 128), pl.ds(at, 128)] = upper

        def relay(q):
            @pl.when(q < 16)
            def _():
                r = chip(q)[0]
                fan(q, sub * 16 + r).wait_recv()
                hand(sub * 16 + r, cols_ref.at[sub * 16 + r]).start()

        each(kb * 4 + 1, kb * 4 + 5, relay)
        return carry

    lax.fori_loop(0, PW // 128, step, 0)
    low_ref[...] = w_ref[:, :PW].T
    turned = w_ref[:, PW:].T
    for c8 in range(8):
        for half in range(2):
            src = (half * 8 + c8) * NB
            inv_ref[(c8 * 2 + half) * NB : (c8 * 2 + half + 1) * NB, :] = turned[src : src + NB, :]

    each(0, 16, lambda q: twin_hand((1 - sub) * 16 + q).wait_recv())
    each(0, 16, lambda q: twin_hand(sub * 16 + q).wait_send())
    each(1, 16, lambda q: fan(q, rg).wait_send())
    each(1, 8, lambda q: own(q, line(q)).wait_recv())
    each(1, 8, lambda q: own(q, cg).wait_send())
    own_local.wait()
    cols_local.wait()
    each(1, 32, lambda q: to_plane(q).wait_send())

    @pl.when(cg == 0)
    def _():
        each(1, 8, lambda q: to_line(q).wait_send())

    @pl.when(moves)
    def _():
        swap().wait_send()

    @pl.when(sub == 0)
    def _():
        each(1, 8, lambda q: head(q, cg).wait_send())
        each(1, 16, lambda q: pivot(q, row).wait_send())
        each(0, 16, lambda q: pivot_twin(q).wait_send())


def unpack(pieces, left):
    top, bottom = [], []
    for p in range(4):
        a, b = pieces[2 * p], pieces[2 * p + 1]
        top.append(jnp.where(left, a, pltpu.roll(b, 64, 1)))
        bottom.append(jnp.where(left, pltpu.roll(a, 64, 1), b))
    return jnp.concatenate(
        [jnp.concatenate(top, axis=1), jnp.concatenate(bottom, axis=1)], axis=0
    )


def three(a, b, dot):
    return dot(a[0], b[0]) + (dot(a[0], b[1]) + dot(a[1], b[0]))


def final_kernel(
    at_ref, slot_ref, col_ref, x_ref, front_ref, own_ref, cols_ref, inv_ref, low_ref,
    o_ref, ih, il, fh, fl, yh, yl, panel_ref,
):
    rg, cg = at_ref[0], at_ref[1]
    ct = pl.program_id(0)
    left = iota((64, 128), 1) < 64

    @pl.when(ct == 0)
    def _():
        ih[...], il[...] = split(inv_ref[...])
        inv = ih[...], il[...]
        for t in range(4):
            tile = unpack([own_ref[c, t * 64 : t * 64 + 64, :] for c in range(8)], left)
            rows = three(split(tile), inv, mm)
            if t == 0:
                keep = (iota((128, PW), 0) < NB) & (rg < 16)
                known = jnp.concatenate([low_ref[...], jnp.zeros((128 - NB, PW), F32)], axis=0)
                rows = jnp.where(keep, known, rows)
            fh[t * 128 : t * 128 + 128, :], fl[t * 128 : t * 128 + 128, :] = split(rows)
        lane = iota((PW, 128), 1)
        nat = ((lane >> 5) * 8 + cg) * 32 + (lane & 31)
        pick = onehot((nat == iota((PW, 128), 0)) & (lane < 64))
        panel_ref[...] = mm(fh[...], pick) + mm(fl[...], pick)
        n = x_ref.shape[1]
        for child in range(2):
            pick = row_picker(slot_ref[child], n)
            high, low = split(x_ref[child])
            yh[child], yl[child] = split(mm(pick, high) + mm(pick, low))

    inv = ih[...], il[...]
    parts = []
    for i in range(4):
        tile = unpack([cols_ref[i * 8 + c] for c in range(8)], left)
        parts.append(three(split(tile), inv, mm))
    cols = jnp.concatenate(
        [parts[i][q * NB : q * NB + NB] for q in range(4) for i in range(4)], axis=0
    )
    total = front_ref[...] - three((fh[...], fl[...]), split(cols), mt)
    for child in range(2):
        put = onehot(col_ref[child] == iota((1024, 512), 0))
        total = total + mm(yh[child], put) + mm(yl[child], put)
    total = jnp.where(natural_lower(rg, cg, 512, 512, ct * 512), total, F32(0.0))
    o_ref[...] = total

    @pl.when(ct == 0)
    def _():
        lane = iota((512, 128), 1)
        value = jnp.where(
            natural_lower(rg, cg, 512, 128, 0), panel_ref[...], F32(0.0)
        )
        o_ref[:, :128] = jnp.where(lane < 64, value, total[:, :128])


def body(front, child_blocks, child_map):
    sub, row, cg = lax.axis_index("sub"), lax.axis_index("row"), lax.axis_index("col")
    rg = sub * 16 + row
    at = jnp.stack([rg, cg]).astype(I32)
    own_map = lax.dynamic_index_in_dim(child_map, sub, 0, keepdims=True)
    row_targets = lax.dynamic_slice_in_dim(own_map, row * 512, 512, axis=1)
    col_targets = lax.dynamic_slice_in_dim(own_map, cg * 1024, 1024, axis=1)
    start = jnp.stack([row * 512, cg * 1024]).astype(I32)

    by_column = pl.pallas_call(
        columns_kernel,
        out_shape=jax.ShapeDtypeStruct((8, 512, 128), F32),
        in_specs=[SM, VM, VM],
        out_specs=VM,
        name="columns",
        compiler_params=params(40),
    )(start, col_targets, child_blocks[0])
    moved = lax.all_to_all(by_column, "col", split_axis=0, concat_axis=0, tiled=True)

    slots, cols = pl.pallas_call(
        index_kernel,
        out_shape=(
            jax.ShapeDtypeStruct((2, NB, 16), I32),
            jax.ShapeDtypeStruct((2, 64, NB), I32),
        ),
        in_specs=[SM, VM],
        out_specs=(VM, VM),
        name="index",
        compiler_params=params(40),
        cost_estimate=pl.CostEstimate(flops=10**8, bytes_accessed=10**7, transcendentals=0),
    )(at, child_map.reshape(2, 16, 512))
    cols = cols.reshape(2, 1, 2048)

    DMA = pltpu.SemaphoreType.DMA
    lower, inverse, own_rows, col_rows = pl.pallas_call(
        panel_kernel,
        out_shape=(
            jax.ShapeDtypeStruct((PW, PW), F32),
            jax.ShapeDtypeStruct((PW, PW), F32),
            jax.ShapeDtypeStruct((8, 256, 128), F32),
            jax.ShapeDtypeStruct((32, 256, 128), F32),
        ),
        grid=(1,),
        in_specs=[
            pl.BlockSpec((1, 512), lambda i: (0, 0)),
            pl.BlockSpec((1, 512), lambda i: (0, 0)),
            pl.BlockSpec((2, NB, 16), lambda i: (0, 0, 0)),
            pl.BlockSpec((512, 512), lambda i: (0, 0)),
            pl.BlockSpec((512, 128), lambda i: (0, 0)),
        ],
        out_specs=(
            pl.BlockSpec((PW, PW), lambda i: (0, 0)),
            pl.BlockSpec((PW, PW), lambda i: (0, 0)),
            pl.BlockSpec(memory_space=pl.ANY),
            pl.BlockSpec(memory_space=pl.ANY),
        ),
        scratch_shapes=[
            pltpu.VMEM((8, 64, 512), F32),
            pltpu.VMEM((128, 512), F32),
            pltpu.VMEM((32, CAP, 128), F32),
            pltpu.VMEM((32, CAP, 128), F32),
            pltpu.VMEM((256, 128), F32),
            pltpu.VMEM((256, 128), F32),
            pltpu.VMEM((NB, 128), F32),
            pltpu.VMEM((8, NB, 128), F32),
            pltpu.VMEM((16, NB, PW), F32),
            pltpu.VMEM((PW, 2 * PW), F32),
            DMA((8,)), DMA, DMA((32,)), DMA((32,)), DMA((8,)), DMA((8,)), DMA((8,)), DMA((8,)),
            DMA, DMA, DMA((32,)), DMA((16,)), DMA((16,)), DMA((32,)), DMA((16,)), DMA((2,)),
        ],
        name="panel",
        compiler_params=pltpu.CompilerParams(
            collective_id=1, has_side_effects=True, vmem_limit_bytes=40 << 20
        ),
        cost_estimate=pl.CostEstimate(flops=3 * 10**10, bytes_accessed=10**8, transcendentals=0),
    )(own_map[:, :512], row_targets, slots, child_blocks[0], front)

    packed = pl.pallas_call(
        rows_kernel,
        out_shape=jax.ShapeDtypeStruct((32 * CAP, 1024), F32),
        in_specs=[VM, VM],
        out_specs=VM,
        name="rows",
        compiler_params=params(40),
    )(row_targets, moved)
    received = lax.all_to_all(
        packed.reshape(32, CAP, 1024), ("sub", "row"), split_axis=0, concat_axis=0, tiled=True
    )

    return pl.pallas_call(
        final_kernel,
        out_shape=jax.ShapeDtypeStruct((512, 2048), F32),
        grid=(4,),
        in_specs=[
            SM,
            pl.BlockSpec((2, NB, 16), lambda i: (0, 0, 0)),
            pl.BlockSpec((2, 1, 512), lambda i: (0, 0, i)),
            pl.BlockSpec((2, 16 * CAP, 1024), lambda i: (0, 0, 0)),
            pl.BlockSpec((512, 512), lambda i: (0, i)),
            pl.BlockSpec((8, 256, 128), lambda i: (0, 0, 0)),
            pl.BlockSpec((32, 64, 128), lambda i: (0, i, 0)),
            pl.BlockSpec((PW, PW), lambda i: (0, 0)),
            pl.BlockSpec((NB, PW), lambda i: (0, 0)),
        ],
        out_specs=pl.BlockSpec((512, 512), lambda i: (0, i)),
        scratch_shapes=[
            pltpu.VMEM((PW, PW), BF16),
            pltpu.VMEM((PW, PW), BF16),
            pltpu.VMEM((512, PW), BF16),
            pltpu.VMEM((512, PW), BF16),
            pltpu.VMEM((2, 512, 1024), BF16),
            pltpu.VMEM((2, 512, 1024), BF16),
            pltpu.VMEM((512, 128), F32),
        ],
        name="final",
        compiler_params=params(60),
    )(
        at,
        slots,
        cols,
        received.reshape(2, 16 * CAP, 1024),
        front,
        own_rows,
        col_rows,
        inverse,
        lax.dynamic_slice_in_dim(lower, jnp.minimum(rg, 15) * NB, NB, axis=0),
    )


def solution(mesh):
    return jax.shard_map(
        body,
        mesh=mesh,
        in_specs=(P(("sub", "row"), "col"), P("sub", "row", "col"), P()),
        out_specs=P(("sub", "row"), "col"),
        check_vma=False,
    )
```

```python
import functools

import jax
import jax.numpy as jnp
from jax import lax
from jax.experimental import pallas as pl
from jax.experimental.pallas import tpu as pltpu
from jax.sharding import PartitionSpec as P

PW = 512
NB = 32
CAP = 24
F32 = jnp.float32
BF16 = jnp.bfloat16
I32 = jnp.int32
AXES = ("sub", "row", "col")


def iota(shape, dim):
    return lax.broadcasted_iota(I32, shape, dim)


def onehot(cond):
    return jnp.where(cond, F32(1.0), F32(0.0)).astype(BF16)


def split(value):
    high = value.astype(BF16)
    return high, (value - high.astype(F32)).astype(BF16)


def mm(a, b):
    return lax.dot_general(a, b, (((1,), (0,)), ((), ())), preferred_element_type=F32)


def mt(a, b):
    return lax.dot_general(a, b, (((1,), (1,)), ((), ())), preferred_element_type=F32)


def params(mib=None):
    return pltpu.CompilerParams(vmem_limit_bytes=None if mib is None else mib << 20)


VM = pl.BlockSpec(memory_space=pltpu.VMEM)
SM = pl.BlockSpec(memory_space=pltpu.SMEM)


def ranks_of(owner, groups, rows):
    n = owner.shape[1]
    member = jnp.where(owner == iota((rows, n), 0), F32(1.0), F32(0.0))
    upto = onehot(iota((n, n), 0) <= iota((n, n), 1))
    counts = mm(member.astype(BF16), upto)
    return (jnp.sum(counts * member, axis=0, keepdims=True) - 1.0).astype(I32)


def index_work(rg, cg, map_ref, slot_ref, col_ref):
    upto = onehot(iota((512, 512), 0) <= iota((512, 512), 1))
    before64 = onehot(iota((64, 64), 1) < iota((64, 64), 0))
    before32 = onehot(iota((32, 32), 0) < iota((32, 32), 1))
    for child in range(2):
        full = map_ref[child]
        match = onehot(((full >> 5) & 31) == rg)
        counts = mm(match, upto)
        slots = jnp.zeros((NB, 16), F32)
        present = jnp.zeros((64, NB), F32)
        for k in range(16):
            here = full[k : k + 1, :]
            block = here >> 5
            off = jnp.where((here & 31) == iota((NB, 512), 0), F32(1.0), F32(0.0))
            own_rows = onehot(
                jnp.where((block & 31) == rg, block >> 5, -1) == iota((16, 512), 0)
            )
            ranked = (off * counts[k : k + 1, :]).astype(BF16)
            off = off.astype(BF16)
            slots = slots + mt(ranked, own_rows) + F32(k * CAP) * mt(off, own_rows)
            own_cols = onehot(jnp.where((block & 7) == cg, block >> 3, -1) == iota((64, 512), 0))
            present = present + mt(own_cols, off)
        slot_ref[child] = slots.astype(I32) - 1
        pb = present.astype(BF16)
        ahead = jnp.sum(mm(before64, pb), axis=1, keepdims=True)
        place = ahead + mm(pb, before32)
        col_ref[child] = jnp.where(present > 0.5, place.astype(I32), -1)


def natural_lower(rg, cg, rows, cols, col0):
    r, c = iota((rows, cols), 0), col0 + iota((rows, cols), 1)
    nat_row = ((r >> 5) * 32 + rg) * 32 + (r & 31)
    nat_col = ((c >> 5) * 8 + cg) * 32 + (c & 31)
    return nat_row >= nat_col


def row_picker(slots, n):
    parts = [onehot(slots[:, b : b + 1] == iota((NB, n), 1)) for b in range(16)]
    return jnp.concatenate(parts, axis=0)


def sweep(w):
    tiles = [w[8 * i : 8 * i + 8, :] for i in range(16)]
    lane = iota((8, 128), 1)
    sub = iota((8, 128), 0)
    for k in range(128):
        own, s = k // 8, k % 8
        row = tiles[own][s : s + 1, :]
        inv = 1.0 / row[:, k : k + 1]
        pivot_row = jnp.where(lane[:1] == k, F32(1.0), row)
        scaled = pivot_row * inv
        for i in range(own, 16):
            t = tiles[i]
            col = t[:, k : k + 1]
            new = jnp.where(lane == k, F32(0.0), t) - col * scaled
            tiles[i] = jnp.where(sub > s, new, t) if i == own else new
    w = jnp.concatenate(tiles, axis=0)
    r, c = iota((128, 128), 0), iota((128, 128), 1)
    diag = jnp.sum(jnp.where(r == c, w, F32(0.0)), axis=1, keepdims=True)
    scale = 1.0 / jnp.sqrt(diag)
    upper = jnp.where(c >= r, w, F32(0.0)) * scale
    inverse = jnp.where(c < r, w, jnp.where(c == r, F32(1.0), F32(0.0))) * scale
    return upper, inverse


def exact(a, b, dims):
    return lax.dot_general(
        a, b, (dims, ((), ())), precision=lax.Precision.HIGHEST, preferred_element_type=F32
    )


def remote(src, dst, send, recv, device):
    return pltpu.make_async_remote_copy(
        src_ref=src, dst_ref=dst, send_sem=send, recv_sem=recv, device_id=device,
        device_id_type=pl.DeviceIdType.MESH,
    )


def panel_kernel(
    cmap_ref, rmap_ref, map_ref, child_ref, front_ref,
    low_ref, inv_ref, slot_ref, col_ref, own_ref, cols_ref, got_ref,
    zsend, zrecv, xsend, pan_send, pan_recv, rows_send, rows_recv, piece, swapped, head_send, head_recv, sbuf, w_ref,
    pan_s, pan_r, row_s, row_r, head_s, head_r, own_s, own_r, swap_s, swap_r, piv_s, piv_r,
    fan_s, fan_r, pass_s, loc_s, z_s, z_r, x_s, x_r,
):
    sub, row, cg = lax.axis_index("sub"), lax.axis_index("row"), lax.axis_index("col")
    rg = sub * 16 + row
    quarter, place = rg // 8, rg % 8
    mate = quarter * 8 + cg
    mate_id = (mate // 16, mate % 16, place)
    moves = place != cg
    twin = (1 - sub, row, cg)

    def each(first, last, fn):
        def go(q, carry):
            fn(q)
            return carry

        lax.fori_loop(first, last, go, 0)

    def line(q):
        return (cg + q) % 8

    def plane(q):
        p = (rg + q) % 32
        return p, (p // 16, p % 16, cg)

    def chip(q):
        r = (row + q) % 16
        return r, (sub, r, cg)

    barrier = pltpu.get_barrier_semaphore()

    def greet(device):
        pl.semaphore_signal(barrier, inc=1, device_id=device, device_id_type=pl.DeviceIdType.MESH)

    each(1, 8, lambda q: greet((sub, row, line(q))))
    each(1, 32, lambda q: greet(plane(q)[1]))

    @pl.when(moves)
    def _():
        greet(mate_id)

    pl.semaphore_wait(barrier, jnp.where(moves, 39, 38))

    pan_recv[64:, :] = jnp.zeros((64, 512), F32)

    def to_line(q):
        return remote(
            pan_send.at[q], pan_recv.at[pl.ds(0, 64)], pan_s.at[q], pan_r, (sub, row, q)
        )

    @pl.when(cg == 0)
    def _():
        keep = row * 512 + iota((512, 512), 0) >= iota((512, 512), 1)
        high, low = split(jnp.where(keep, child_ref[:, :512], F32(0.0)))
        for q in range(7, -1, -1):
            n = iota((64, 512), 0)
            nat = ((n >> 5) * 8 + q) * NB + (n & 31)
            pick = onehot(cmap_ref[:, :512] == nat)
            out = mt(pick, high) + mt(pick, low)
            if q == 0:
                pan_recv[:64, :] = out
            else:
                pan_send[q] = out
                to_line(q).start()

    def bulk(h, q, at):
        return remote(
            zsend.at[h, q], zrecv.at[h, at], z_s.at[h, q], z_r.at[h, at], (sub, row, q)
        )

    keep = row * 512 + iota((512, 1024), 0) >= cg * 1024 + iota((512, 1024), 1)
    high, low = split(jnp.where(keep, child_ref[...], F32(0.0)))
    owner = (cmap_ref[...] >> 5) & 7
    slot = owner * 128 + ranks_of(owner, 8, 16)

    def bulk_half(h):
        n = iota((512, 1024), 0)
        pick = onehot(slot == (n >> 6) * 128 + h * 64 + (n & 63))
        out = mt(pick, high) + mt(pick, low)
        for q in range(8):
            zsend[h, q] = out[q * 64 : q * 64 + 64, :]
        zrecv[h, cg] = zsend[h, cg]

    bulk_half(0)
    each(1, 8, lambda q: bulk(0, line(q), cg).start())
    bulk_half(1)
    owner = (rmap_ref[...] >> 5) & 31
    slot = owner * CAP + ranks_of(owner, 32, 32)
    pick_rows = onehot(slot == iota((32 * CAP, 512), 0))
    index_work(rg, cg, map_ref, slot_ref, col_ref)

    @pl.when(cg != 0)
    def _():
        to_line(cg).wait_recv()

    high, low = split(pan_recv[...])
    out = mt(pick_rows, high) + mt(pick_rows, low)
    for p in range(32):
        rows_send[p] = out[p * CAP : p * CAP + CAP, :]

    def to_plane(q):
        p, device = plane(q)
        return remote(rows_send.at[p], rows_recv.at[rg], row_s.at[p], row_r.at[rg], device)

    def from_plane(q):
        p, device = plane(q)
        return remote(rows_send.at[p], rows_recv.at[p], row_s.at[p], row_r.at[p], device)

    each(1, 32, lambda q: to_plane(q).start())
    rows_recv[rg] = rows_send[rg]
    total = jnp.where(natural_lower(rg, cg, 512, 128, 0), front_ref[...], F32(0.0))
    picks = [row_picker(slot_ref[child], 16 * CAP) for child in range(2)]
    each(1, 32, lambda q: from_plane(q).wait_recv())
    for child in range(2):
        got = rows_recv[child * 16 : child * 16 + 16].reshape(16 * CAP, 128)
        high, low = split(got)
        total = total + mm(picks[child], high) + mm(picks[child], low)
    left = iota((64, 128), 1) < 64
    for t in range(4):
        a = total[t * 128 : t * 128 + 64]
        b = total[t * 128 + 64 : t * 128 + 128]
        piece[t * 64 : t * 64 + 64, :] = jnp.where(left, a, pltpu.roll(b, 64, 1))
    head_send[...] = total[:NB, :]

    def head(q, at):
        return remote(
            head_send, head_recv.at[at], head_s.at[q], head_r.at[at], (sub, row, line(q))
        )

    def swap():
        return remote(piece, swapped, swap_s, swap_r, mate_id)

    def own(q, at):
        return remote(piece, own_ref.at[at], own_s.at[q], own_r.at[at], (sub, row, line(q)))

    own_local = pltpu.make_async_copy(piece, own_ref.at[cg], loc_s.at[0])

    @pl.when(sub == 0)
    def _():
        each(1, 8, lambda q: head(q, cg).start())

    @pl.when(moves)
    def _():
        swap().start()

    head_recv[cg] = head_send[...]
    each(1, 8, lambda q: bulk(1, line(q), cg).start())

    def cross(h, q, at):
        p, device = plane(q)
        return remote(xsend.at[h, p], got_ref.at[h, at], x_s.at[h, p], x_r.at[h, at], device)

    def keep_own(h):
        return pltpu.make_async_copy(xsend.at[h, rg], got_ref.at[h, rg], loc_s.at[2 + h])

    def cross_half(h):
        each(1, 8, lambda q: bulk(h, line(q), line(q)).wait_recv())
        high, low = split(zrecv[h].reshape(512, 512))
        out = mt(pick_rows, high) + mt(pick_rows, low)
        for p in range(32):
            xsend[h, p] = out[p * CAP : p * CAP + CAP, :]
        each(1, 32, lambda q: cross(h, q, rg).start())
        keep_own(h).start()

    def pivot(q, at):
        return remote(sbuf.at[at], sbuf.at[at], piv_s.at[q], piv_r.at[at], chip(q)[1])

    def pivot_twin(at):
        return remote(sbuf.at[at], sbuf.at[at], piv_s.at[16 + at], piv_r.at[at], (1, row, cg))

    @pl.when(sub == 0)
    def _():
        each(1, 8, lambda q: head(q, line(q)).wait_recv())
        half = iota((NB, 128), 1) < 64
        rows = [
            jnp.where(half, head_recv[2 * p], pltpu.roll(head_recv[2 * p + 1], 64, 1))
            for p in range(4)
        ]
        sbuf[row] = jnp.concatenate(rows, axis=1)
        each(1, 16, lambda q: pivot(q, row).start())
        pivot_twin(row).start()

    @pl.when(moves)
    def _():
        swap().wait_recv()

    @pl.when(jnp.logical_not(moves))
    def _():
        swapped[...] = piece[...]

    def fan(q, at):
        return remote(swapped, cols_ref.at[at], fan_s.at[q], fan_r.at[at], chip(q)[1])

    def hand(at, src):
        return remote(src, cols_ref.at[at], pass_s.at[at % 16], fan_r.at[at], twin)

    def twin_hand(at):
        return remote(swapped, cols_ref.at[at], pass_s.at[at % 16], fan_r.at[at], twin)

    cols_local = pltpu.make_async_copy(swapped, cols_ref.at[rg], loc_s.at[1])
    each(1, 16, lambda q: fan(q, rg).start())
    hand(rg, swapped).start()
    cols_local.start()
    each(1, 8, lambda q: own(q, cg).start())
    own_local.start()

    @pl.when(sub == 0)
    def _():
        def relay(q):
            at = chip(q)[0]
            pivot(q, at).wait_recv()
            pivot_twin(at).start()

        each(1, 16, relay)

    @pl.when(sub == 1)
    def _():
        each(0, 16, lambda q: pivot_twin(q).wait_recv())

    turned = sbuf[...].reshape(PW, PW).T
    for c8 in range(8):
        for half in range(2):
            src = (c8 * 2 + half) * NB
            w_ref[(half * 8 + c8) * NB : (half * 8 + c8 + 1) * NB, :PW] = turned[src : src + NB, :]
    r, c = iota((PW, PW), 0), iota((PW, PW), 1)
    raw = w_ref[:, :PW]
    w_ref[:, :PW] = jnp.where(c >= r, raw, F32(0.0)) + jnp.where(c > r, raw, F32(0.0)).T
    w_ref[:, PW:] = jnp.where(r == c, F32(1.0), F32(0.0))

    def step(kb, carry):
        at = pl.multiple_of(kb * 128, 128)
        upper, inverse = sweep(w_ref[pl.ds(at, 128), pl.ds(at, 128)])
        rows = exact(inverse, w_ref[pl.ds(at, 128), :], ((1,), (0,)))
        lanes = iota((128, PW), 1)
        ahead = jnp.where(lanes >= at + 128, rows[:, :PW], F32(0.0))
        w_ref[...] = w_ref[...] - exact(ahead, rows, ((0,), (0,)))
        w_ref[pl.ds(at, 128), :] = jnp.concatenate([ahead, rows[:, PW:]], axis=1)
        w_ref[pl.ds(at, 128), pl.ds(at, 128)] = upper

        def relay(q):
            @pl.when(q < 16)
            def _():
                r = chip(q)[0]
                fan(q, sub * 16 + r).wait_recv()
                hand(sub * 16 + r, cols_ref.at[sub * 16 + r]).start()

        each(kb * 4 + 1, kb * 4 + 5, relay)

        @pl.when(kb < 2)
        def _():
            cross_half(kb)

        return carry

    lax.fori_loop(0, PW // 128, step, 0)
    low_ref[...] = w_ref[:, :PW].T
    turned = w_ref[:, PW:].T
    for c8 in range(8):
        for half in range(2):
            src = (half * 8 + c8) * NB
            inv_ref[(c8 * 2 + half) * NB : (c8 * 2 + half + 1) * NB, :] = turned[src : src + NB, :]

    each(0, 16, lambda q: twin_hand((1 - sub) * 16 + q).wait_recv())
    each(0, 16, lambda q: twin_hand(sub * 16 + q).wait_send())
    each(1, 16, lambda q: fan(q, rg).wait_send())
    each(1, 8, lambda q: own(q, line(q)).wait_recv())
    each(1, 8, lambda q: own(q, cg).wait_send())
    own_local.wait()
    cols_local.wait()
    each(1, 32, lambda q: to_plane(q).wait_send())
    for h in range(2):
        each(1, 8, lambda q: bulk(h, line(q), cg).wait_send())
        each(1, 32, lambda q: cross(h, q, plane(q)[0]).wait_recv())
        each(1, 32, lambda q: cross(h, q, rg).wait_send())
        keep_own(h).wait()

    @pl.when(cg == 0)
    def _():
        each(1, 8, lambda q: to_line(q).wait_send())

    @pl.when(moves)
    def _():
        swap().wait_send()

    @pl.when(sub == 0)
    def _():
        each(1, 8, lambda q: head(q, cg).wait_send())
        each(1, 16, lambda q: pivot(q, row).wait_send())
        each(0, 16, lambda q: pivot_twin(q).wait_send())


def unpack(pieces, left):
    top, bottom = [], []
    for p in range(4):
        a, b = pieces[2 * p], pieces[2 * p + 1]
        top.append(jnp.where(left, a, pltpu.roll(b, 64, 1)))
        bottom.append(jnp.where(left, pltpu.roll(a, 64, 1), b))
    return jnp.concatenate(
        [jnp.concatenate(top, axis=1), jnp.concatenate(bottom, axis=1)], axis=0
    )


def three(a, b, dot):
    return dot(a[0], b[0]) + (dot(a[0], b[1]) + dot(a[1], b[0]))


def final_kernel(
    at_ref, slot_ref, col_ref, x_ref, front_ref, own_ref, cols_ref, inv_ref, low_ref,
    o_ref, ih, il, fh, fl, yh, yl, panel_ref,
):
    rg, cg = at_ref[0], at_ref[1]
    ct = pl.program_id(0)
    left = iota((64, 128), 1) < 64

    @pl.when(ct == 0)
    def _():
        ih[...], il[...] = split(inv_ref[...])
        inv = ih[...], il[...]
        for t in range(4):
            tile = unpack([own_ref[c, t * 64 : t * 64 + 64, :] for c in range(8)], left)
            rows = three(split(tile), inv, mm)
            if t == 0:
                keep = (iota((128, PW), 0) < NB) & (rg < 16)
                known = jnp.concatenate([low_ref[...], jnp.zeros((128 - NB, PW), F32)], axis=0)
                rows = jnp.where(keep, known, rows)
            fh[t * 128 : t * 128 + 128, :], fl[t * 128 : t * 128 + 128, :] = split(rows)
        lane = iota((PW, 128), 1)
        nat = ((lane >> 5) * 8 + cg) * 32 + (lane & 31)
        pick = onehot((nat == iota((PW, 128), 0)) & (lane < 64))
        panel_ref[...] = mm(fh[...], pick) + mm(fl[...], pick)
        for child in range(2):
            pick = row_picker(slot_ref[child], 16 * CAP)
            for h in range(2):
                got = x_ref[h, child * 16 : child * 16 + 16].reshape(16 * CAP, 512)
                high, low = split(got)
                at = pl.ds(h * 512, 512)
                yh[child, :, at], yl[child, :, at] = split(mm(pick, high) + mm(pick, low))

    inv = ih[...], il[...]
    parts = []
    for i in range(4):
        tile = unpack([cols_ref[i * 8 + c] for c in range(8)], left)
        parts.append(three(split(tile), inv, mm))
    cols = jnp.concatenate(
        [parts[i][q * NB : q * NB + NB] for q in range(4) for i in range(4)], axis=0
    )
    total = front_ref[...] - three((fh[...], fl[...]), split(cols), mt)
    for child in range(2):
        m = col_ref[child]
        m = jnp.where(m < 0, -1, ((m >> 6) & 1) * 512 + (m >> 7) * 64 + (m & 63))
        put = onehot(m == iota((1024, 512), 0))
        total = total + mm(yh[child], put) + mm(yl[child], put)
    total = jnp.where(natural_lower(rg, cg, 512, 512, ct * 512), total, F32(0.0))
    o_ref[...] = total

    @pl.when(ct == 0)
    def _():
        lane = iota((512, 128), 1)
        value = jnp.where(
            natural_lower(rg, cg, 512, 128, 0), panel_ref[...], F32(0.0)
        )
        o_ref[:, :128] = jnp.where(lane < 64, value, total[:, :128])


def body(front, child_blocks, child_map):
    sub, row, cg = lax.axis_index("sub"), lax.axis_index("row"), lax.axis_index("col")
    rg = sub * 16 + row
    at = jnp.stack([rg, cg]).astype(I32)
    own_map = lax.dynamic_index_in_dim(child_map, sub, 0, keepdims=True)
    row_targets = lax.dynamic_slice_in_dim(own_map, row * 512, 512, axis=1)
    col_targets = lax.dynamic_slice_in_dim(own_map, cg * 1024, 1024, axis=1)

    DMA = pltpu.SemaphoreType.DMA
    lower, inverse, slots, cols, own_rows, col_rows, received = pl.pallas_call(
        panel_kernel,
        out_shape=(
            jax.ShapeDtypeStruct((PW, PW), F32),
            jax.ShapeDtypeStruct((PW, PW), F32),
            jax.ShapeDtypeStruct((2, NB, 16), I32),
            jax.ShapeDtypeStruct((2, 64, NB), I32),
            jax.ShapeDtypeStruct((8, 256, 128), F32),
            jax.ShapeDtypeStruct((32, 256, 128), F32),
            jax.ShapeDtypeStruct((2, 32, CAP, 512), F32),
        ),
        grid=(1,),
        in_specs=[
            pl.BlockSpec((1, 1024), lambda i: (0, 0)),
            pl.BlockSpec((1, 512), lambda i: (0, 0)),
            pl.BlockSpec((2, 16, 512), lambda i: (0, 0, 0)),
            pl.BlockSpec((512, 1024), lambda i: (0, 0)),
            pl.BlockSpec((512, 128), lambda i: (0, 0)),
        ],
        out_specs=(
            pl.BlockSpec((PW, PW), lambda i: (0, 0)),
            pl.BlockSpec((PW, PW), lambda i: (0, 0)),
            pl.BlockSpec((2, NB, 16), lambda i: (0, 0, 0)),
            pl.BlockSpec((2, 64, NB), lambda i: (0, 0, 0)),
            pl.BlockSpec(memory_space=pl.ANY),
            pl.BlockSpec(memory_space=pl.ANY),
            pl.BlockSpec(memory_space=pl.ANY),
        ),
        scratch_shapes=[
            pltpu.VMEM((2, 8, 64, 512), F32),
            pltpu.VMEM((2, 8, 64, 512), F32),
            pltpu.VMEM((2, 32, CAP, 512), F32),
            pltpu.VMEM((8, 64, 512), F32),
            pltpu.VMEM((128, 512), F32),
            pltpu.VMEM((32, CAP, 128), F32),
            pltpu.VMEM((32, CAP, 128), F32),
            pltpu.VMEM((256, 128), F32),
            pltpu.VMEM((256, 128), F32),
            pltpu.VMEM((NB, 128), F32),
            pltpu.VMEM((8, NB, 128), F32),
            pltpu.VMEM((16, NB, PW), F32),
            pltpu.VMEM((PW, 2 * PW), F32),
            DMA((8,)), DMA, DMA((32,)), DMA((32,)), DMA((8,)), DMA((8,)), DMA((8,)), DMA((8,)),
            DMA, DMA, DMA((32,)), DMA((16,)), DMA((16,)), DMA((32,)), DMA((16,)), DMA((4,)),
            DMA((2, 8)), DMA((2, 8)), DMA((2, 32)), DMA((2, 32)),
        ],
        name="panel",
        compiler_params=pltpu.CompilerParams(
            collective_id=1, has_side_effects=True, vmem_limit_bytes=56 << 20
        ),
        cost_estimate=pl.CostEstimate(flops=3 * 10**10, bytes_accessed=10**8, transcendentals=0),
    )(col_targets, row_targets, child_map.reshape(2, 16, 512), child_blocks[0], front)

    cols = cols.reshape(2, 1, 2048)
    return pl.pallas_call(
        final_kernel,
        out_shape=jax.ShapeDtypeStruct((512, 2048), F32),
        grid=(4,),
        in_specs=[
            SM,
            pl.BlockSpec((2, NB, 16), lambda i: (0, 0, 0)),
            pl.BlockSpec((2, 1, 512), lambda i: (0, 0, i)),
            pl.BlockSpec((2, 32, CAP, 512), lambda i: (0, 0, 0, 0)),
            pl.BlockSpec((512, 512), lambda i: (0, i)),
            pl.BlockSpec((8, 256, 128), lambda i: (0, 0, 0)),
            pl.BlockSpec((32, 64, 128), lambda i: (0, i, 0)),
            pl.BlockSpec((PW, PW), lambda i: (0, 0)),
            pl.BlockSpec((NB, PW), lambda i: (0, 0)),
        ],
        out_specs=pl.BlockSpec((512, 512), lambda i: (0, i)),
        scratch_shapes=[
            pltpu.VMEM((PW, PW), BF16),
            pltpu.VMEM((PW, PW), BF16),
            pltpu.VMEM((512, PW), BF16),
            pltpu.VMEM((512, PW), BF16),
            pltpu.VMEM((2, 512, 1024), BF16),
            pltpu.VMEM((2, 512, 1024), BF16),
            pltpu.VMEM((512, 128), F32),
        ],
        name="final",
        compiler_params=params(60),
    )(
        at,
        slots,
        cols,
        received,
        front,
        own_rows,
        col_rows,
        inverse,
        lax.dynamic_slice_in_dim(lower, jnp.minimum(rg, 15) * NB, NB, axis=0),
    )


def solution(mesh):
    return jax.shard_map(
        body,
        mesh=mesh,
        in_specs=(P(("sub", "row"), "col"), P("sub", "row", "col"), P()),
        out_specs=P(("sub", "row"), "col"),
        check_vma=False,
    )
```

```python
import functools

import jax
import jax.numpy as jnp
from jax import lax
from jax.experimental import pallas as pl
from jax.experimental.pallas import tpu as pltpu
from jax.sharding import PartitionSpec as P

PW = 512
NB = 32
CAP = 24
F32 = jnp.float32
BF16 = jnp.bfloat16
I32 = jnp.int32
AXES = ("sub", "row", "col")


def iota(shape, dim):
    return lax.broadcasted_iota(I32, shape, dim)


def onehot(cond):
    return jnp.where(cond, F32(1.0), F32(0.0)).astype(BF16)


def split(value):
    high = value.astype(BF16)
    return high, (value - high.astype(F32)).astype(BF16)


def mm(a, b):
    return lax.dot_general(a, b, (((1,), (0,)), ((), ())), preferred_element_type=F32)


def mt(a, b):
    return lax.dot_general(a, b, (((1,), (1,)), ((), ())), preferred_element_type=F32)


def params(mib=None):
    return pltpu.CompilerParams(vmem_limit_bytes=None if mib is None else mib << 20)


VM = pl.BlockSpec(memory_space=pltpu.VMEM)
SM = pl.BlockSpec(memory_space=pltpu.SMEM)


def ranks_of(owner, groups, rows):
    n = owner.shape[1]
    member = jnp.where(owner == iota((rows, n), 0), F32(1.0), F32(0.0))
    upto = onehot(iota((n, n), 0) <= iota((n, n), 1))
    counts = mm(member.astype(BF16), upto)
    return (jnp.sum(counts * member, axis=0, keepdims=True) - 1.0).astype(I32)


def index_work(rg, cg, map_ref, slot_ref, col_ref, flat_ref):
    upto = onehot(iota((512, 512), 0) <= iota((512, 512), 1))
    before64 = onehot(iota((64, 64), 1) < iota((64, 64), 0))
    before128 = onehot(iota((128, 128), 0) < iota((128, 128), 1))
    for child in range(2):
        chunks = [map_ref[child : child + 1, k * 512 : k * 512 + 512] for k in range(16)]
        match = onehot(((jnp.concatenate(chunks, axis=0) >> 5) & 31) == rg)
        counts = mm(match, upto)
        slots = jnp.zeros((NB, 16), F32)
        present = jnp.zeros((64, 128), F32)
        for k in range(16):
            here = chunks[k]
            block = here >> 5
            off = jnp.where((here & 31) == iota((128, 512), 0), F32(1.0), F32(0.0))
            own_rows = onehot(
                jnp.where((block & 31) == rg, block >> 5, -1) == iota((16, 512), 0)
            )
            ranked = (off[:NB] * counts[k : k + 1, :]).astype(BF16)
            off = off.astype(BF16)
            slots = slots + mt(ranked, own_rows) + F32(k * CAP) * mt(off[:NB], own_rows)
            own_cols = onehot(jnp.where((block & 7) == cg, block >> 3, -1) == iota((64, 512), 0))
            present = present + mt(own_cols, off)
        slot_ref[child] = slots.astype(I32) - 1
        pb = present.astype(BF16)
        ahead = jnp.sum(mm(before64, pb), axis=1, keepdims=True)
        place = ahead + mm(pb, before128)
        flat_ref[...] = jnp.where(present > 0.5, place + 1.0, F32(0.0))
        flat = flat_ref[pl.ds(0, 16, stride=4), :]
        for i in range(1, 4):
            flat = flat + pltpu.roll(flat_ref[pl.ds(i, 16, stride=4), :], NB * i, 1)
        col_ref[child] = flat.astype(I32) - 1


def natural_lower(rg, cg, rows, cols, col0):
    r, c = iota((rows, cols), 0), col0 + iota((rows, cols), 1)
    nat_row = ((r >> 5) * 32 + rg) * 32 + (r & 31)
    nat_col = ((c >> 5) * 8 + cg) * 32 + (c & 31)
    return nat_row >= nat_col


def row_picker(slots, n):
    parts = [onehot(slots[:, b : b + 1] == iota((NB, n), 1)) for b in range(16)]
    return jnp.concatenate(parts, axis=0)


def sweep(w):
    tiles = [w[8 * i : 8 * i + 8, :] for i in range(16)]
    lane = iota((8, 128), 1)
    sub = iota((8, 128), 0)
    for k in range(128):
        own, s = k // 8, k % 8
        row = tiles[own][s : s + 1, :]
        inv = 1.0 / row[:, k : k + 1]
        pivot_row = jnp.where(lane[:1] == k, F32(1.0), row)
        scaled = pivot_row * inv
        for i in range(own, 16):
            t = tiles[i]
            col = t[:, k : k + 1]
            new = jnp.where(lane == k, F32(0.0), t) - col * scaled
            tiles[i] = jnp.where(sub > s, new, t) if i == own else new
    w = jnp.concatenate(tiles, axis=0)
    r, c = iota((128, 128), 0), iota((128, 128), 1)
    diag = jnp.sum(jnp.where(r == c, w, F32(0.0)), axis=1, keepdims=True)
    scale = 1.0 / jnp.sqrt(diag)
    upper = jnp.where(c >= r, w, F32(0.0)) * scale
    inverse = jnp.where(c < r, w, jnp.where(c == r, F32(1.0), F32(0.0))) * scale
    return upper, inverse


def exact(a, b, dims):
    return lax.dot_general(
        a, b, (dims, ((), ())), precision=lax.Precision.HIGHEST, preferred_element_type=F32
    )


def remote(src, dst, send, recv, device):
    return pltpu.make_async_remote_copy(
        src_ref=src, dst_ref=dst, send_sem=send, recv_sem=recv, device_id=device,
        device_id_type=pl.DeviceIdType.MESH,
    )


def panel_kernel(
    map_ref, child_ref, front_ref,
    low_ref, inv_ref, slot_ref, col_ref, own_ref, cols_ref, got_ref,
    zsend, zrecv, xsend, pan_send, pan_recv, rows_send, rows_recv, piece, swapped, head_send, head_recv, sbuf, w_ref,
    pan_s, pan_r, row_s, row_r, head_s, head_r, own_s, own_r, swap_s, swap_r, piv_s, piv_r,
    fan_s, fan_r, pass_s, loc_s, z_s, z_r, x_s, x_r, flat_ref, far_s,
):
    sub, row, cg = lax.axis_index("sub"), lax.axis_index("row"), lax.axis_index("col")
    rg = sub * 16 + row
    quarter, place = rg // 8, rg % 8
    mate = quarter * 8 + cg
    mate_id = (mate // 16, mate % 16, place)
    moves = place != cg
    twin = (1 - sub, row, cg)

    cmap = map_ref[pl.ds(sub, 1), pl.ds(pl.multiple_of(cg * 1024, 1024), 1024)]
    rmap = map_ref[pl.ds(sub, 1), pl.ds(pl.multiple_of(row * 512, 512), 512)]

    def each(first, last, fn):
        def go(q, carry):
            fn(q)
            return carry

        lax.fori_loop(first, last, go, 0)

    def line(q):
        return (cg + q) % 8

    def plane(q):
        p = (rg + q) % 32
        return p, (p // 16, p % 16, cg)

    def chip(q):
        r = (row + q) % 16
        return r, (sub, r, cg)

    barrier = pltpu.get_barrier_semaphore()

    def greet(device):
        pl.semaphore_signal(barrier, inc=1, device_id=device, device_id_type=pl.DeviceIdType.MESH)

    each(1, 8, lambda q: greet((sub, row, line(q))))
    each(1, 32, lambda q: greet(plane(q)[1]))

    @pl.when(moves)
    def _():
        greet(mate_id)

    pl.semaphore_wait(barrier, jnp.where(moves, 39, 38))

    pan_recv[64:, :] = jnp.zeros((64, 512), F32)

    def to_line(q):
        return remote(
            pan_send.at[q], pan_recv.at[pl.ds(0, 64)], pan_s.at[q], pan_r, (sub, row, q)
        )

    @pl.when(cg == 0)
    def _():
        keep = row * 512 + iota((512, 512), 0) >= iota((512, 512), 1)
        high, low = split(jnp.where(keep, child_ref[:, :512], F32(0.0)))
        for q in range(7, -1, -1):
            n = iota((64, 512), 0)
            nat = ((n >> 5) * 8 + q) * NB + (n & 31)
            pick = onehot(cmap[:, :512] == nat)
            out = mt(pick, high) + mt(pick, low)
            if q == 0:
                pan_recv[:64, :] = out
            else:
                pan_send[q] = out
                to_line(q).start()

    def bulk(h, q, at):
        return remote(
            zsend.at[h, q], zrecv.at[h, at], z_s.at[h, q], z_r.at[h, at], (sub, row, q)
        )

    keep = row * 512 + iota((512, 1024), 0) >= cg * 1024 + iota((512, 1024), 1)
    high, low = split(jnp.where(keep, child_ref[...], F32(0.0)))
    owner = (cmap >> 5) & 7
    slot = owner * 128 + ranks_of(owner, 8, 16)

    def bulk_half(h):
        n = iota((512, 1024), 0)
        pick = onehot(slot == (n >> 6) * 128 + h * 64 + (n & 63))
        out = mt(pick, high) + mt(pick, low)
        for q in range(8):
            zsend[h, q] = out[q * 64 : q * 64 + 64, :]
        zrecv[h, cg] = zsend[h, cg]

    last = row // 2
    for c in range(1, 8):

        @pl.when(c > last)
        def _(c=c):
            zrecv[0, c] = jnp.zeros((64, 512), F32)
            zrecv[1, c] = jnp.zeros((64, 512), F32)

    def bulk_out(h):
        @pl.when(cg <= last)
        def _():
            each(1, 8, lambda q: bulk(h, line(q), cg).start())

    def bulk_in(h):
        def one(c):
            @pl.when(c != cg)
            def _():
                bulk(h, c, c).wait_recv()

        each(0, last + 1, one)

    bulk_half(0)
    bulk_out(0)
    bulk_half(1)
    owner = (rmap >> 5) & 31
    slot = owner * CAP + ranks_of(owner, 32, 32)
    pick_rows = onehot(slot == iota((32 * CAP, 512), 0))
    index_work(rg, cg, map_ref, slot_ref, col_ref, flat_ref)

    @pl.when(cg != 0)
    def _():
        to_line(cg).wait_recv()

    high, low = split(pan_recv[...])
    out = mt(pick_rows, high) + mt(pick_rows, low)
    for p in range(32):
        rows_send[p] = out[p * CAP : p * CAP + CAP, :]

    def to_plane(q):
        p, device = plane(q)
        return remote(rows_send.at[p], rows_recv.at[rg], row_s.at[p], row_r.at[rg], device)

    def from_plane(q):
        p, device = plane(q)
        return remote(rows_send.at[p], rows_recv.at[p], row_s.at[p], row_r.at[p], device)

    each(1, 32, lambda q: to_plane(q).start())
    rows_recv[rg] = rows_send[rg]
    total = jnp.where(natural_lower(rg, cg, 512, 128, 0), front_ref[...], F32(0.0))
    picks = [row_picker(slot_ref[child], 16 * CAP) for child in range(2)]
    each(1, 32, lambda q: from_plane(q).wait_recv())
    for child in range(2):
        got = rows_recv[child * 16 : child * 16 + 16].reshape(16 * CAP, 128)
        high, low = split(got)
        total = total + mm(picks[child], high) + mm(picks[child], low)
    left = iota((64, 128), 1) < 64
    for t in range(4):
        a = total[t * 128 : t * 128 + 64]
        b = total[t * 128 + 64 : t * 128 + 128]
        piece[t * 64 : t * 64 + 64, :] = jnp.where(left, a, pltpu.roll(b, 64, 1))
    head_send[...] = total[:NB, :]

    def head(q, at):
        return remote(
            head_send, head_recv.at[at], head_s.at[q], head_r.at[at], (sub, row, line(q))
        )

    def swap():
        return remote(piece, swapped, swap_s, swap_r, mate_id)

    def own_up(t, at, src):
        return remote(src, own_ref.at[at], own_s.at[t], own_r.at[at], (sub, row, line(1)))

    def own_down(t, at, src):
        return remote(src, own_ref.at[at], own_s.at[4 + t], own_r.at[at], (sub, row, line(7)))

    def ring(t):
        @pl.when(t < 4)
        def _():
            at = (cg + 8 - t) % 8
            own_up(t, at, own_ref.at[at]).wait_recv()
            own_up(t, at, own_ref.at[at]).start()

        @pl.when(t < 3)
        def _():
            at = (cg + t) % 8
            own_down(t, at, own_ref.at[at]).wait_recv()
            own_down(t, at, own_ref.at[at]).start()

    own_local = pltpu.make_async_copy(piece, own_ref.at[cg], loc_s.at[0])

    @pl.when(sub == 0)
    def _():
        each(1, 8, lambda q: head(q, cg).start())

    @pl.when(moves)
    def _():
        swap().start()

    head_recv[cg] = head_send[...]
    bulk_out(1)

    def cross(h, p, at, level):
        lanes = pl.ds(0, 128 * (level + 1))
        return remote(
            xsend.at[h, p, :, lanes], got_ref.at[h, at, :, lanes], x_s.at[h, p], x_r.at[h, at],
            (p // 16, p % 16, cg),
        )

    def by_level(fn):
        for level in range(4):

            @pl.when(row // 4 == level)
            def _(level=level):
                each(1, 32, lambda q: fn(plane(q)[0], level))

    def cross_out(h):
        by_level(lambda p, level: cross(h, p, rg, level).start())

    def cross_in(h):
        for level in range(4):

            def one(j):
                p = j // 4 * 16 + level * 4 + j % 4

                @pl.when(p != rg)
                def _():
                    cross(h, p, p, level).wait_recv()

            each(0, 8, one)

    def keep_own(h):
        return pltpu.make_async_copy(xsend.at[h, rg], got_ref.at[h, rg], loc_s.at[2 + h])

    def cross_half(h):
        bulk_in(h)
        high, low = split(zrecv[h].reshape(512, 512))
        out = mt(pick_rows, high) + mt(pick_rows, low)
        for p in range(32):
            xsend[h, p] = out[p * CAP : p * CAP + CAP, :]
        cross_out(h)
        keep_own(h).start()

    def pivot(q, at):
        return remote(sbuf.at[at], sbuf.at[at], piv_s.at[q], piv_r.at[at], chip(q)[1])

    def pivot_twin(at):
        return remote(sbuf.at[at], sbuf.at[at], piv_s.at[16 + at], piv_r.at[at], (1, row, cg))

    @pl.when(sub == 0)
    def _():
        each(1, 8, lambda q: head(q, line(q)).wait_recv())
        half = iota((NB, 128), 1) < 64
        rows = [
            jnp.where(half, head_recv[2 * p], pltpu.roll(head_recv[2 * p + 1], 64, 1))
            for p in range(4)
        ]
        sbuf[row] = jnp.concatenate(rows, axis=1)
        each(1, 16, lambda q: pivot(q, row).start())
        pivot_twin(row).start()

    @pl.when(moves)
    def _():
        swap().wait_recv()

    @pl.when(jnp.logical_not(moves))
    def _():
        swapped[...] = piece[...]

    gx, gy = row // 4, row % 4

    def xmate(j):
        return (gx + j) % 4 * 4 + gy

    def ymate(j):
        return gx * 4 + (gy + j) % 4

    def fan(k, at, to):
        return remote(swapped, cols_ref.at[at], fan_s.at[k], fan_r.at[0, at], (sub, to, cg))

    def far(half, k, at, to):
        part = cols_ref.at[at, pl.ds(half * 128, 128)]
        return remote(part, part, far_s.at[half, k], fan_r.at[half, at], (sub, to, cg))

    def hand(at, src):
        return remote(src, cols_ref.at[at], pass_s.at[at % 16], fan_r.at[0, at], twin)

    def near(j):
        x, y = xmate(j), ymate(j)
        fan(j, sub * 16 + x, x).wait_recv()
        each(1, 4, lambda i: far(0, j * 4 + i, sub * 16 + x, ymate(i)).start())
        hand(sub * 16 + x, cols_ref.at[sub * 16 + x]).start()
        fan(4 + j, sub * 16 + y, y).wait_recv()
        each(1, 4, lambda i: far(1, j * 4 + i, sub * 16 + y, xmate(i)).start())
        hand(sub * 16 + y, cols_ref.at[sub * 16 + y]).start()

    def corner(i, j):
        at = sub * 16 + (gx + i) % 4 * 4 + (gy + j) % 4
        far(0, 0, at, 0).wait_recv()
        far(1, 0, at, 0).wait_recv()
        hand(at, cols_ref.at[at]).start()

    cols_local = pltpu.make_async_copy(swapped, cols_ref.at[rg], loc_s.at[1])

    def fan_out(j):
        fan(j, rg, xmate(j)).start()
        fan(4 + j, rg, ymate(j)).start()

    each(1, 4, fan_out)
    hand(rg, swapped).start()
    cols_local.start()
    own_up(0, cg, piece).start()
    own_down(0, cg, piece).start()
    own_local.start()

    @pl.when(sub == 0)
    def _():
        def relay(q):
            at = chip(q)[0]
            pivot(q, at).wait_recv()
            pivot_twin(at).start()

        each(1, 16, relay)

    @pl.when(sub == 1)
    def _():
        each(0, 16, lambda q: pivot_twin(q).wait_recv())

    turned = sbuf[...].reshape(PW, PW).T
    for c8 in range(8):
        for half in range(2):
            src = (c8 * 2 + half) * NB
            w_ref[(half * 8 + c8) * NB : (half * 8 + c8 + 1) * NB, :PW] = turned[src : src + NB, :]
    r, c = iota((PW, PW), 0), iota((PW, PW), 1)
    raw = w_ref[:, :PW]
    w_ref[:, :PW] = jnp.where(c >= r, raw, F32(0.0)) + jnp.where(c > r, raw, F32(0.0)).T
    w_ref[:, PW:] = jnp.where(r == c, F32(1.0), F32(0.0))

    def step(kb, carry):
        at = pl.multiple_of(kb * 128, 128)
        upper, inverse = sweep(w_ref[pl.ds(at, 128), pl.ds(at, 128)])
        rows = exact(inverse, w_ref[pl.ds(at, 128), :], ((1,), (0,)))
        lanes = iota((128, PW), 1)
        ahead = jnp.where(lanes >= at + 128, rows[:, :PW], F32(0.0))
        w_ref[...] = w_ref[...] - exact(ahead, rows, ((0,), (0,)))
        w_ref[pl.ds(at, 128), :] = jnp.concatenate([ahead, rows[:, PW:]], axis=1)
        w_ref[pl.ds(at, 128), pl.ds(at, 128)] = upper

        ring(kb + 1)

        @pl.when(kb == 0)
        def _():
            each(1, 4, near)

        @pl.when(kb > 0)
        def _():
            each(1, 4, lambda j: corner(kb, j))

        @pl.when(kb < 2)
        def _():
            cross_half(kb)

        return carry

    lax.fori_loop(0, PW // 128, step, 0)
    w_ref[:, :PW] = w_ref[:, :PW].T
    low_ref[...] = w_ref[pl.ds(pl.multiple_of(jnp.minimum(rg, 15) * NB, NB), NB), :PW]
    turned = w_ref[:, PW:].T
    for c8 in range(8):
        for half in range(2):
            src = (half * 8 + c8) * NB
            inv_ref[(c8 * 2 + half) * NB : (c8 * 2 + half + 1) * NB, :] = turned[src : src + NB, :]

    each(0, 16, lambda q: hand((1 - sub) * 16 + q, swapped).wait_recv())
    each(0, 16, lambda q: hand(sub * 16 + q, swapped).wait_send())

    def sent(j):
        fan(j, rg, xmate(j)).wait_send()
        fan(4 + j, rg, ymate(j)).wait_send()
        each(1, 4, lambda i: far(0, j * 4 + i, rg, ymate(i)).wait_send())
        each(1, 4, lambda i: far(1, j * 4 + i, rg, xmate(i)).wait_send())

    each(1, 4, sent)
    own_up(0, line(4), piece).wait_recv()
    own_down(0, line(3), piece).wait_recv()
    each(0, 4, lambda t: own_up(t, cg, piece).wait_send())
    each(0, 3, lambda t: own_down(t, cg, piece).wait_send())
    own_local.wait()
    cols_local.wait()
    each(1, 32, lambda q: to_plane(q).wait_send())
    for h in range(2):

        @pl.when(cg <= last)
        def _(h=h):
            each(1, 8, lambda q: bulk(h, line(q), cg).wait_send())

        cross_in(h)
        by_level(lambda p, level: cross(h, p, rg, level).wait_send())
        keep_own(h).wait()

    @pl.when(cg == 0)
    def _():
        each(1, 8, lambda q: to_line(q).wait_send())

    @pl.when(moves)
    def _():
        swap().wait_send()

    @pl.when(sub == 0)
    def _():
        each(1, 8, lambda q: head(q, cg).wait_send())
        each(1, 16, lambda q: pivot(q, row).wait_send())
        each(0, 16, lambda q: pivot_twin(q).wait_send())


def unpack(pieces, left):
    top, bottom = [], []
    for p in range(4):
        a, b = pieces[2 * p], pieces[2 * p + 1]
        top.append(jnp.where(left, a, pltpu.roll(b, 64, 1)))
        bottom.append(jnp.where(left, pltpu.roll(a, 64, 1), b))
    return jnp.concatenate(
        [jnp.concatenate(top, axis=1), jnp.concatenate(bottom, axis=1)], axis=0
    )


def three(a, b, dot):
    return dot(a[0], b[0]) + (dot(a[0], b[1]) + dot(a[1], b[0]))


def final_kernel(
    at_ref, slot_ref, col_ref, x_ref, front_ref, own_ref, cols_ref, inv_ref, low_ref,
    o_ref, ih, il, fh, fl, yh, yl, panel_ref,
):
    rg, cg = at_ref[0], at_ref[1]
    ct = pl.program_id(0)
    left = iota((64, 128), 1) < 64

    @pl.when(ct == 0)
    def _():
        ih[...], il[...] = split(inv_ref[...])
        inv = ih[...], il[...]
        for t in range(4):
            tile = unpack([own_ref[c, t * 64 : t * 64 + 64, :] for c in range(8)], left)
            rows = three(split(tile), inv, mm)
            if t == 0:
                keep = (iota((128, PW), 0) < NB) & (rg < 16)
                known = jnp.concatenate([low_ref[...], jnp.zeros((128 - NB, PW), F32)], axis=0)
                rows = jnp.where(keep, known, rows)
            fh[t * 128 : t * 128 + 128, :], fl[t * 128 : t * 128 + 128, :] = split(rows)
        lane = iota((PW, 128), 1)
        nat = ((lane >> 5) * 8 + cg) * 32 + (lane & 31)
        pick = onehot((nat == iota((PW, 128), 0)) & (lane < 64))
        panel_ref[...] = mm(fh[...], pick) + mm(fl[...], pick)
        for child in range(2):
            pick = row_picker(slot_ref[child], 16 * CAP)
            for h in range(2):
                got = x_ref[h, child * 16 : child * 16 + 16].reshape(16 * CAP, 512)
                r, lane = iota(got.shape, 0), iota(got.shape, 1)
                limit = jnp.where(r < 4 * CAP, 128, jnp.where(r < 8 * CAP, 256, 384))
                got = jnp.where((lane < limit) | (r >= 12 * CAP), got, F32(0.0))
                high, low = split(got)
                at = pl.ds(h * 512, 512)
                yh[child, :, at], yl[child, :, at] = split(mm(pick, high) + mm(pick, low))

    inv = ih[...], il[...]
    parts = []
    for i in range(4):
        tile = unpack([cols_ref[i * 8 + c] for c in range(8)], left)
        parts.append(three(split(tile), inv, mm))
    cols = split(
        jnp.concatenate(
            [parts[i][q * NB : q * NB + NB] for q in range(4) for i in range(4)], axis=0
        )
    )
    for v in range(4):

        @pl.when(ct == v)
        def _(v=v):
            top = v * 128
            down = pl.ds(top, 512 - top)
            total = front_ref[down, :] - three((fh[down, :], fl[down, :]), cols, mt)
            for child in range(2):
                m = jnp.concatenate(
                    [col_ref[child, v * 4 + j : v * 4 + j + 1, :] for j in range(4)], axis=1
                )
                m = jnp.where(m < 0, -1, ((m >> 6) & 1) * 512 + (m >> 7) * 64 + (m & 63))
                put = onehot(m == iota((1024, 512), 0))
                total = total + mm(yh[child, down, :], put) + mm(yl[child, down, :], put)
            r, c = top + iota(total.shape, 0), v * 512 + iota(total.shape, 1)
            nat_row = ((r >> 5) * 32 + rg) * 32 + (r & 31)
            nat_col = ((c >> 5) * 8 + cg) * 32 + (c & 31)
            total = jnp.where(nat_row >= nat_col, total, F32(0.0))
            if v == 0:
                lane = iota((512, 128), 1)
                value = jnp.where(natural_lower(rg, cg, 512, 128, 0), panel_ref[...], F32(0.0))
                o_ref[:, :128] = jnp.where(lane < 64, value, total[:, :128])
                o_ref[:, 128:] = total[:, 128:]
            else:
                o_ref[:top, :] = jnp.zeros((top, 512), F32)
                o_ref[down, :] = total


def body(front, child_blocks, child_map):
    sub, row, cg = lax.axis_index("sub"), lax.axis_index("row"), lax.axis_index("col")
    rg = sub * 16 + row
    at = jnp.stack([rg, cg]).astype(I32)
    DMA = pltpu.SemaphoreType.DMA
    lower, inverse, slots, cols, own_rows, col_rows, received = pl.pallas_call(
        panel_kernel,
        out_shape=(
            jax.ShapeDtypeStruct((NB, PW), F32),
            jax.ShapeDtypeStruct((PW, PW), F32),
            jax.ShapeDtypeStruct((2, NB, 16), I32),
            jax.ShapeDtypeStruct((2, 16, 128), I32),
            jax.ShapeDtypeStruct((8, 256, 128), F32),
            jax.ShapeDtypeStruct((32, 256, 128), F32),
            jax.ShapeDtypeStruct((2, 32, CAP, 512), F32),
        ),
        grid=(1,),
        in_specs=[
            pl.BlockSpec((2, 8192), lambda i: (0, 0)),
            pl.BlockSpec((512, 1024), lambda i: (0, 0)),
            pl.BlockSpec((512, 128), lambda i: (0, 0)),
        ],
        out_specs=(
            pl.BlockSpec((NB, PW), lambda i: (0, 0)),
            pl.BlockSpec((PW, PW), lambda i: (0, 0)),
            pl.BlockSpec((2, NB, 16), lambda i: (0, 0, 0)),
            pl.BlockSpec((2, 16, 128), lambda i: (0, 0, 0)),
            pl.BlockSpec(memory_space=pl.ANY),
            pl.BlockSpec(memory_space=pl.ANY),
            pl.BlockSpec(memory_space=pl.ANY),
        ),
        scratch_shapes=[
            pltpu.VMEM((2, 8, 64, 512), F32),
            pltpu.VMEM((2, 8, 64, 512), F32),
            pltpu.VMEM((2, 32, CAP, 512), F32),
            pltpu.VMEM((8, 64, 512), F32),
            pltpu.VMEM((128, 512), F32),
            pltpu.VMEM((32, CAP, 128), F32),
            pltpu.VMEM((32, CAP, 128), F32),
            pltpu.VMEM((256, 128), F32),
            pltpu.VMEM((256, 128), F32),
            pltpu.VMEM((NB, 128), F32),
            pltpu.VMEM((8, NB, 128), F32),
            pltpu.VMEM((16, NB, PW), F32),
            pltpu.VMEM((PW, 2 * PW), F32),
            DMA((8,)), DMA, DMA((32,)), DMA((32,)), DMA((8,)), DMA((8,)), DMA((8,)), DMA((8,)),
            DMA, DMA, DMA((32,)), DMA((16,)), DMA((8,)), DMA((2, 32)), DMA((16,)), DMA((4,)),
            DMA((2, 8)), DMA((2, 8)), DMA((2, 32)), DMA((2, 32)),
            pltpu.VMEM((64, 128), F32), DMA((2, 16)),
        ],
        name="panel",
        compiler_params=pltpu.CompilerParams(
            collective_id=1, has_side_effects=True, vmem_limit_bytes=56 << 20
        ),
        cost_estimate=pl.CostEstimate(flops=3 * 10**10, bytes_accessed=10**8, transcendentals=0),
    )(child_map, child_blocks[0], front)

    return pl.pallas_call(
        final_kernel,
        out_shape=jax.ShapeDtypeStruct((512, 2048), F32),
        grid=(4,),
        in_specs=[
            SM,
            pl.BlockSpec((2, NB, 16), lambda i: (0, 0, 0)),
            pl.BlockSpec((2, 16, 128), lambda i: (0, 0, 0)),
            pl.BlockSpec((2, 32, CAP, 512), lambda i: (0, 0, 0, 0)),
            pl.BlockSpec((512, 512), lambda i: (0, i)),
            pl.BlockSpec((8, 256, 128), lambda i: (0, 0, 0)),
            pl.BlockSpec((32, 64, 128), lambda i: (0, i, 0)),
            pl.BlockSpec((PW, PW), lambda i: (0, 0)),
            pl.BlockSpec((NB, PW), lambda i: (0, 0)),
        ],
        out_specs=pl.BlockSpec((512, 512), lambda i: (0, i)),
        scratch_shapes=[
            pltpu.VMEM((PW, PW), BF16),
            pltpu.VMEM((PW, PW), BF16),
            pltpu.VMEM((512, PW), BF16),
            pltpu.VMEM((512, PW), BF16),
            pltpu.VMEM((2, 512, 1024), BF16),
            pltpu.VMEM((2, 512, 1024), BF16),
            pltpu.VMEM((512, 128), F32),
        ],
        name="final",
        compiler_params=params(60),
    )(
        at,
        slots,
        cols,
        received,
        front,
        own_rows,
        col_rows,
        inverse,
        lower,
    )


def solution(mesh):
    return jax.shard_map(
        body,
        mesh=mesh,
        in_specs=(P(("sub", "row"), "col"), P("sub", "row", "col"), P()),
        out_specs=P(("sub", "row"), "col"),
        check_vma=False,
    )
```

```python
import functools

import jax
import jax.numpy as jnp
from jax import lax
from jax.experimental import pallas as pl
from jax.experimental.pallas import tpu as pltpu
from jax.sharding import PartitionSpec as P

PW = 512
NB = 32
CAP = 24
F32 = jnp.float32
BF16 = jnp.bfloat16
I32 = jnp.int32
AXES = ("sub", "row", "col")


def iota(shape, dim):
    return lax.broadcasted_iota(I32, shape, dim)


def onehot(cond):
    return jnp.where(cond, F32(1.0), F32(0.0)).astype(BF16)


def split(value):
    high = value.astype(BF16)
    return high, (value - high.astype(F32)).astype(BF16)


def mm(a, b):
    return lax.dot_general(a, b, (((1,), (0,)), ((), ())), preferred_element_type=F32)


def mt(a, b):
    return lax.dot_general(a, b, (((1,), (1,)), ((), ())), preferred_element_type=F32)


def params(mib=None):
    return pltpu.CompilerParams(vmem_limit_bytes=None if mib is None else mib << 20)


VM = pl.BlockSpec(memory_space=pltpu.VMEM)
SM = pl.BlockSpec(memory_space=pltpu.SMEM)


def ranks_of(owner, groups, rows):
    n = owner.shape[1]
    member = jnp.where(owner == iota((rows, n), 0), F32(1.0), F32(0.0))
    upto = onehot(iota((n, n), 0) <= iota((n, n), 1))
    counts = mm(member.astype(BF16), upto)
    return (jnp.sum(counts * member, axis=0, keepdims=True) - 1.0).astype(I32)


def index_work(rg, cg, map_ref, slot_ref, col_ref, flat_ref):
    upto = onehot(iota((512, 512), 0) <= iota((512, 512), 1))
    before64 = onehot(iota((64, 64), 1) < iota((64, 64), 0))
    before128 = onehot(iota((128, 128), 0) < iota((128, 128), 1))
    for child in range(2):
        chunks = [map_ref[child : child + 1, k * 512 : k * 512 + 512] for k in range(16)]
        match = onehot(((jnp.concatenate(chunks, axis=0) >> 5) & 31) == rg)
        counts = mm(match, upto)
        slots = jnp.zeros((NB, 16), F32)
        present = jnp.zeros((64, 128), F32)
        for k in range(16):
            here = chunks[k]
            block = here >> 5
            off = jnp.where((here & 31) == iota((128, 512), 0), F32(1.0), F32(0.0))
            own_rows = onehot(
                jnp.where((block & 31) == rg, block >> 5, -1) == iota((16, 512), 0)
            )
            ranked = (off[:NB] * counts[k : k + 1, :]).astype(BF16)
            off = off.astype(BF16)
            slots = slots + mt(ranked, own_rows) + F32(k * CAP) * mt(off[:NB], own_rows)
            own_cols = onehot(jnp.where((block & 7) == cg, block >> 3, -1) == iota((64, 512), 0))
            present = present + mt(own_cols, off)
        slot_ref[child] = slots.astype(I32) - 1
        pb = present.astype(BF16)
        ahead = jnp.sum(mm(before64, pb), axis=1, keepdims=True)
        place = ahead + mm(pb, before128)
        flat_ref[...] = jnp.where(present > 0.5, place + 1.0, F32(0.0))
        flat = flat_ref[pl.ds(0, 16, stride=4), :]
        for i in range(1, 4):
            flat = flat + pltpu.roll(flat_ref[pl.ds(i, 16, stride=4), :], NB * i, 1)
        col_ref[child] = flat.astype(I32) - 1


def natural_lower(rg, cg, rows, cols, col0):
    r, c = iota((rows, cols), 0), col0 + iota((rows, cols), 1)
    nat_row = ((r >> 5) * 32 + rg) * 32 + (r & 31)
    nat_col = ((c >> 5) * 8 + cg) * 32 + (c & 31)
    return nat_row >= nat_col


def row_picker(slots, n):
    parts = [onehot(slots[:, b : b + 1] == iota((NB, n), 1)) for b in range(16)]
    return jnp.concatenate(parts, axis=0)


GROUP = 8


def sweep(w):
    lane = iota((1, 128), 1)
    below = w
    done = []
    for k0 in range(0, 128, GROUP):
        n = 128 - k0
        column = [jnp.broadcast_to(below[:, k0 + j : k0 + j + 1], (n, 128)) for j in range(GROUP)]
        row = [below[j : j + 1, :] for j in range(GROUP)]
        scaled = []
        for j in range(GROUP):
            inv = 1.0 / column[j][j : j + 1, :]
            scaled.append(jnp.where(lane == k0 + j, F32(1.0), row[j]) * inv)
            for i in range(j + 1, GROUP):
                ratio = column[i][j : j + 1, :] * inv
                kept = jnp.where(lane == k0 + j, F32(0.0), row[i])
                row[i] = kept - column[j][i : i + 1, :] * scaled[j]
                column[i] = column[i] - column[j] * ratio
        done.extend(row)
        if n > GROUP:
            inside = (lane >= k0) & (lane < k0 + GROUP)
            rest = jnp.where(inside, F32(0.0), below[GROUP:])
            for j in range(GROUP):
                part = jnp.where((lane > k0 + j) & inside, F32(0.0), scaled[j])
                rest = rest - column[j][GROUP:] * part
            below = rest
    w = jnp.concatenate(done, axis=0)
    r, c = iota((128, 128), 0), iota((128, 128), 1)
    diag = jnp.sum(jnp.where(r == c, w, F32(0.0)), axis=1, keepdims=True)
    scale = 1.0 / jnp.sqrt(diag)
    upper = jnp.where(c >= r, w, F32(0.0)) * scale
    inverse = jnp.where(c < r, w, jnp.where(c == r, F32(1.0), F32(0.0))) * scale
    return upper, inverse


def exact(a, b, dims):
    return lax.dot_general(
        a, b, (dims, ((), ())), precision=lax.Precision.HIGHEST, preferred_element_type=F32
    )


def remote(src, dst, send, recv, device):
    return pltpu.make_async_remote_copy(
        src_ref=src, dst_ref=dst, send_sem=send, recv_sem=recv, device_id=device,
        device_id_type=pl.DeviceIdType.MESH,
    )


def panel_kernel(
    map_ref, child_ref, front_ref,
    low_ref, inv_ref, slot_ref, col_ref, own_ref, cols_ref, got_ref,
    zsend, zrecv, xsend, pan_send, pan_recv, rows_send, rows_recv, piece, swapped, head_send, head_recv, sbuf, w_ref,
    pan_s, pan_r, row_s, row_r, head_s, head_r, own_s, own_r, swap_s, swap_r, piv_s, piv_r,
    fan_s, fan_r, pass_s, loc_s, z_s, z_r, x_s, x_r, flat_ref, far_s,
):
    sub, row, cg = lax.axis_index("sub"), lax.axis_index("row"), lax.axis_index("col")
    rg = sub * 16 + row
    quarter, place = rg // 8, rg % 8
    mate = quarter * 8 + cg
    mate_id = (mate // 16, mate % 16, place)
    moves = place != cg
    twin = (1 - sub, row, cg)

    cmap = map_ref[pl.ds(sub, 1), pl.ds(pl.multiple_of(cg * 1024, 1024), 1024)]
    rmap = map_ref[pl.ds(sub, 1), pl.ds(pl.multiple_of(row * 512, 512), 512)]

    def each(first, last, fn):
        def go(q, carry):
            fn(q)
            return carry

        lax.fori_loop(first, last, go, 0)

    def line(q):
        return (cg + q) % 8

    def plane(q):
        p = (rg + q) % 32
        return p, (p // 16, p % 16, cg)

    def chip(q):
        r = (row + q) % 16
        return r, (sub, r, cg)

    barrier = pltpu.get_barrier_semaphore()

    def greet(device):
        pl.semaphore_signal(barrier, inc=1, device_id=device, device_id_type=pl.DeviceIdType.MESH)

    each(1, 8, lambda q: greet((sub, row, line(q))))
    each(1, 32, lambda q: greet(plane(q)[1]))

    @pl.when(moves)
    def _():
        greet(mate_id)

    pl.semaphore_wait(barrier, jnp.where(moves, 39, 38))

    pan_recv[64:, :] = jnp.zeros((64, 512), F32)

    def to_line(q):
        return remote(
            pan_send.at[q], pan_recv.at[pl.ds(0, 64)], pan_s.at[q], pan_r, (sub, row, q)
        )

    @pl.when(cg == 0)
    def _():
        keep = row * 512 + iota((512, 512), 0) >= iota((512, 512), 1)
        high, low = split(jnp.where(keep, child_ref[:, :512], F32(0.0)))
        n = iota((512, 512), 0)
        nat = (((n >> 5) & 1) * 8 + (n >> 6)) * NB + (n & 31)
        pick = onehot(cmap[:, :512] == nat)
        out = mt(pick, high) + mt(pick, low)
        for q in range(1, 8):
            pan_send[q] = out[q * 64 : q * 64 + 64, :]
            to_line(q).start()
        pan_recv[:64, :] = out[:64, :]

    def bulk(h, q, at):
        return remote(
            zsend.at[h, q], zrecv.at[h, at], z_s.at[h, q], z_r.at[h, at], (sub, row, q)
        )

    keep = row * 512 + iota((512, 1024), 0) >= cg * 1024 + iota((512, 1024), 1)
    high, low = split(jnp.where(keep, child_ref[...], F32(0.0)))
    owner = (cmap >> 5) & 7
    slot = owner * 128 + ranks_of(owner, 8, 16)

    def bulk_half(h):
        n = iota((512, 1024), 0)
        pick = onehot(slot == (n >> 6) * 128 + h * 64 + (n & 63))
        out = mt(pick, high) + mt(pick, low)
        for q in range(8):
            zsend[h, q] = out[q * 64 : q * 64 + 64, :]
        zrecv[h, cg] = zsend[h, cg]

    last = row // 2
    for c in range(1, 8):

        @pl.when(c > last)
        def _(c=c):
            zrecv[0, c] = jnp.zeros((64, 512), F32)
            zrecv[1, c] = jnp.zeros((64, 512), F32)

    def bulk_out(h):
        @pl.when(cg <= last)
        def _():
            each(1, 8, lambda q: bulk(h, line(q), cg).start())

    def bulk_in(h):
        def one(c):
            @pl.when(c != cg)
            def _():
                bulk(h, c, c).wait_recv()

        each(0, last + 1, one)

    bulk_half(0)
    bulk_half(1)
    owner = (rmap >> 5) & 31
    slot = owner * CAP + ranks_of(owner, 32, 32)
    pick_rows = onehot(slot == iota((32 * CAP, 512), 0))
    index_work(rg, cg, map_ref, slot_ref, col_ref, flat_ref)

    @pl.when(cg != 0)
    def _():
        to_line(cg).wait_recv()

    bulk_out(0)

    high, low = split(pan_recv[...])
    out = mt(pick_rows, high) + mt(pick_rows, low)
    for p in range(32):
        rows_send[p] = out[p * CAP : p * CAP + CAP, :]

    def to_plane(q):
        p, device = plane(q)
        return remote(rows_send.at[p], rows_recv.at[rg], row_s.at[p], row_r.at[rg], device)

    def from_plane(q):
        p, device = plane(q)
        return remote(rows_send.at[p], rows_recv.at[p], row_s.at[p], row_r.at[p], device)

    each(1, 32, lambda q: to_plane(q).start())
    rows_recv[rg] = rows_send[rg]
    total = jnp.where(natural_lower(rg, cg, 512, 128, 0), front_ref[...], F32(0.0))
    picks = [row_picker(slot_ref[child], 16 * CAP) for child in range(2)]
    each(1, 32, lambda q: from_plane(q).wait_recv())
    for child in range(2):
        got = rows_recv[child * 16 : child * 16 + 16].reshape(16 * CAP, 128)
        high, low = split(got)
        total = total + mm(picks[child], high) + mm(picks[child], low)
    left = iota((64, 128), 1) < 64
    for t in range(4):
        a = total[t * 128 : t * 128 + 64]
        b = total[t * 128 + 64 : t * 128 + 128]
        piece[t * 64 : t * 64 + 64, :] = jnp.where(left, a, pltpu.roll(b, 64, 1))
    head_send[...] = total[:NB, :]

    def head(q, at):
        return remote(
            head_send, head_recv.at[at], head_s.at[q], head_r.at[at], (sub, row, line(q))
        )

    def swap():
        return remote(piece, swapped, swap_s, swap_r, mate_id)

    def own_up(t, at, src):
        return remote(src, own_ref.at[at], own_s.at[t], own_r.at[at], (sub, row, line(1)))

    def own_down(t, at, src):
        return remote(src, own_ref.at[at], own_s.at[4 + t], own_r.at[at], (sub, row, line(7)))

    def ring(t):
        @pl.when(t < 4)
        def _():
            at = (cg + 8 - t) % 8
            own_up(t, at, own_ref.at[at]).wait_recv()
            own_up(t, at, own_ref.at[at]).start()

        @pl.when(t < 3)
        def _():
            at = (cg + t) % 8
            own_down(t, at, own_ref.at[at]).wait_recv()
            own_down(t, at, own_ref.at[at]).start()

    own_local = pltpu.make_async_copy(piece, own_ref.at[cg], loc_s.at[0])

    @pl.when(sub == 0)
    def _():
        each(1, 8, lambda q: head(q, cg).start())

    @pl.when(moves)
    def _():
        swap().start()

    head_recv[cg] = head_send[...]

    def cross(h, p, at, level):
        lanes = pl.ds(0, 128 * (level + 1))
        return remote(
            xsend.at[h, p, :, lanes], got_ref.at[h, at, :, lanes], x_s.at[h, p], x_r.at[h, at],
            (p // 16, p % 16, cg),
        )

    def by_level(fn):
        for level in range(4):

            @pl.when(row // 4 == level)
            def _(level=level):
                each(1, 32, lambda q: fn(plane(q)[0], level))

    def cross_out(h):
        by_level(lambda p, level: cross(h, p, rg, level).start())

    def cross_in(h):
        for level in range(4):

            def one(j):
                p = j // 4 * 16 + level * 4 + j % 4

                @pl.when(p != rg)
                def _():
                    cross(h, p, p, level).wait_recv()

            each(0, 8, one)

    def keep_own(h):
        return pltpu.make_async_copy(xsend.at[h, rg], got_ref.at[h, rg], loc_s.at[2 + h])

    def cross_half(h):
        bulk_in(h)
        high, low = split(zrecv[h].reshape(512, 512))
        out = mt(pick_rows, high) + mt(pick_rows, low)
        for p in range(32):
            xsend[h, p] = out[p * CAP : p * CAP + CAP, :]
        cross_out(h)
        keep_own(h).start()

    def pivot(q, at):
        return remote(sbuf.at[at], sbuf.at[at], piv_s.at[q], piv_r.at[at], chip(q)[1])

    def pivot_twin(at):
        return remote(sbuf.at[at], sbuf.at[at], piv_s.at[16 + at], piv_r.at[at], (1, row, cg))

    @pl.when(sub == 0)
    def _():
        each(1, 8, lambda q: head(q, line(q)).wait_recv())
        half = iota((NB, 128), 1) < 64
        rows = [
            jnp.where(half, head_recv[2 * p], pltpu.roll(head_recv[2 * p + 1], 64, 1))
            for p in range(4)
        ]
        sbuf[row] = jnp.concatenate(rows, axis=1)
        each(1, 16, lambda q: pivot(q, row).start())
        pivot_twin(row).start()

    bulk_out(1)

    @pl.when(moves)
    def _():
        swap().wait_recv()

    @pl.when(jnp.logical_not(moves))
    def _():
        swapped[...] = piece[...]

    gx, gy = row // 4, row % 4

    def xmate(j):
        return (gx + j) % 4 * 4 + gy

    def ymate(j):
        return gx * 4 + (gy + j) % 4

    def fan(k, at, to):
        return remote(swapped, cols_ref.at[at], fan_s.at[k], fan_r.at[0, at], (sub, to, cg))

    def far(half, k, at, to):
        part = cols_ref.at[at, pl.ds(half * 128, 128)]
        return remote(part, part, far_s.at[half, k], fan_r.at[half, at], (sub, to, cg))

    def hand(at, src):
        return remote(src, cols_ref.at[at], pass_s.at[at % 16], fan_r.at[0, at], twin)

    def near(j):
        x, y = xmate(j), ymate(j)
        fan(j, sub * 16 + x, x).wait_recv()
        each(1, 4, lambda i: far(0, j * 4 + i, sub * 16 + x, ymate(i)).start())
        hand(sub * 16 + x, cols_ref.at[sub * 16 + x]).start()
        fan(4 + j, sub * 16 + y, y).wait_recv()
        each(1, 4, lambda i: far(1, j * 4 + i, sub * 16 + y, xmate(i)).start())
        hand(sub * 16 + y, cols_ref.at[sub * 16 + y]).start()

    def corner(i, j):
        at = sub * 16 + (gx + i) % 4 * 4 + (gy + j) % 4
        far(0, 0, at, 0).wait_recv()
        far(1, 0, at, 0).wait_recv()
        hand(at, cols_ref.at[at]).start()

    cols_local = pltpu.make_async_copy(swapped, cols_ref.at[rg], loc_s.at[1])

    def fan_out(j):
        fan(j, rg, xmate(j)).start()
        fan(4 + j, rg, ymate(j)).start()

    each(1, 4, fan_out)
    hand(rg, swapped).start()
    cols_local.start()
    own_up(0, cg, piece).start()
    own_down(0, cg, piece).start()
    own_local.start()

    cross_half(0)

    @pl.when(sub == 0)
    def _():
        def relay(q):
            at = chip(q)[0]
            pivot(q, at).wait_recv()
            pivot_twin(at).start()

        each(1, 16, relay)

    @pl.when(sub == 1)
    def _():
        each(0, 16, lambda q: pivot_twin(q).wait_recv())

    turned = sbuf[...].reshape(PW, PW).T
    for c8 in range(8):
        for half in range(2):
            src = (c8 * 2 + half) * NB
            w_ref[(half * 8 + c8) * NB : (half * 8 + c8 + 1) * NB, :PW] = turned[src : src + NB, :]
    r, c = iota((PW, PW), 0), iota((PW, PW), 1)
    raw = w_ref[:, :PW]
    w_ref[:, :PW] = jnp.where(c >= r, raw, F32(0.0)) + jnp.where(c > r, raw, F32(0.0)).T
    w_ref[:, PW:] = jnp.where(r == c, F32(1.0), F32(0.0))

    def step(kb, carry):
        at = pl.multiple_of(kb * 128, 128)
        upper, inverse = sweep(w_ref[pl.ds(at, 128), pl.ds(at, 128)])
        rows = exact(inverse, w_ref[pl.ds(at, 128), :], ((1,), (0,)))
        lanes = iota((128, PW), 1)
        ahead = jnp.where(lanes >= at + 128, rows[:, :PW], F32(0.0))
        w_ref[...] = w_ref[...] - exact(ahead, rows, ((0,), (0,)))
        w_ref[pl.ds(at, 128), :] = jnp.concatenate([ahead, rows[:, PW:]], axis=1)
        w_ref[pl.ds(at, 128), pl.ds(at, 128)] = upper

        ring(kb + 1)

        @pl.when(kb == 0)
        def _():
            each(1, 4, near)

        @pl.when(kb > 0)
        def _():
            each(1, 4, lambda j: corner(kb, j))

        @pl.when(kb == 1)
        def _():
            cross_half(1)

        return carry

    lax.fori_loop(0, PW // 128, step, 0)
    w_ref[:, :PW] = w_ref[:, :PW].T
    low_ref[...] = w_ref[pl.ds(pl.multiple_of(jnp.minimum(rg, 15) * NB, NB), NB), :PW]
    turned = w_ref[:, PW:].T
    for c8 in range(8):
        for half in range(2):
            src = (half * 8 + c8) * NB
            inv_ref[(c8 * 2 + half) * NB : (c8 * 2 + half + 1) * NB, :] = turned[src : src + NB, :]

    each(0, 16, lambda q: hand((1 - sub) * 16 + q, swapped).wait_recv())
    each(0, 16, lambda q: hand(sub * 16 + q, swapped).wait_send())

    def sent(j):
        fan(j, rg, xmate(j)).wait_send()
        fan(4 + j, rg, ymate(j)).wait_send()
        each(1, 4, lambda i: far(0, j * 4 + i, rg, ymate(i)).wait_send())
        each(1, 4, lambda i: far(1, j * 4 + i, rg, xmate(i)).wait_send())

    each(1, 4, sent)
    own_up(0, line(4), piece).wait_recv()
    own_down(0, line(3), piece).wait_recv()
    each(0, 4, lambda t: own_up(t, cg, piece).wait_send())
    each(0, 3, lambda t: own_down(t, cg, piece).wait_send())
    own_local.wait()
    cols_local.wait()
    each(1, 32, lambda q: to_plane(q).wait_send())
    for h in range(2):

        @pl.when(cg <= last)
        def _(h=h):
            each(1, 8, lambda q: bulk(h, line(q), cg).wait_send())

        cross_in(h)
        by_level(lambda p, level: cross(h, p, rg, level).wait_send())
        keep_own(h).wait()

    @pl.when(cg == 0)
    def _():
        each(1, 8, lambda q: to_line(q).wait_send())

    @pl.when(moves)
    def _():
        swap().wait_send()

    @pl.when(sub == 0)
    def _():
        each(1, 8, lambda q: head(q, cg).wait_send())
        each(1, 16, lambda q: pivot(q, row).wait_send())
        each(0, 16, lambda q: pivot_twin(q).wait_send())


def unpack(pieces, left):
    top, bottom = [], []
    for p in range(4):
        a, b = pieces[2 * p], pieces[2 * p + 1]
        top.append(jnp.where(left, a, pltpu.roll(b, 64, 1)))
        bottom.append(jnp.where(left, pltpu.roll(a, 64, 1), b))
    return jnp.concatenate(
        [jnp.concatenate(top, axis=1), jnp.concatenate(bottom, axis=1)], axis=0
    )


def three(a, b, dot):
    return dot(a[0], b[0]) + (dot(a[0], b[1]) + dot(a[1], b[0]))


def final_kernel(
    at_ref, slot_ref, col_ref, x_ref, front_ref, own_ref, cols_ref, inv_ref, low_ref,
    o_ref, ih, il, fh, fl, yh, yl, panel_ref,
):
    rg, cg = at_ref[0], at_ref[1]
    ct = pl.program_id(0)
    left = iota((64, 128), 1) < 64

    @pl.when(ct == 0)
    def _():
        ih[...], il[...] = split(inv_ref[...])
        inv = ih[...], il[...]
        for t in range(4):
            tile = unpack([own_ref[c, t * 64 : t * 64 + 64, :] for c in range(8)], left)
            rows = three(split(tile), inv, mm)
            if t == 0:
                keep = (iota((128, PW), 0) < NB) & (rg < 16)
                known = jnp.concatenate([low_ref[...], jnp.zeros((128 - NB, PW), F32)], axis=0)
                rows = jnp.where(keep, known, rows)
            fh[t * 128 : t * 128 + 128, :], fl[t * 128 : t * 128 + 128, :] = split(rows)
        lane = iota((PW, 128), 1)
        nat = ((lane >> 5) * 8 + cg) * 32 + (lane & 31)
        pick = onehot((nat == iota((PW, 128), 0)) & (lane < 64))
        panel_ref[...] = mm(fh[...], pick) + mm(fl[...], pick)
        for child in range(2):
            pick = row_picker(slot_ref[child], 16 * CAP)
            for h in range(2):
                got = x_ref[h, child * 16 : child * 16 + 16].reshape(16 * CAP, 512)
                r, lane = iota(got.shape, 0), iota(got.shape, 1)
                limit = jnp.where(r < 4 * CAP, 128, jnp.where(r < 8 * CAP, 256, 384))
                got = jnp.where((lane < limit) | (r >= 12 * CAP), got, F32(0.0))
                high, low = split(got)
                at = pl.ds(h * 512, 512)
                yh[child, :, at], yl[child, :, at] = split(mm(pick, high) + mm(pick, low))

    inv = ih[...], il[...]
    parts = []
    for i in range(4):
        tile = unpack([cols_ref[i * 8 + c] for c in range(8)], left)
        parts.append(three(split(tile), inv, mm))
    cols = split(
        jnp.concatenate(
            [parts[i][q * NB : q * NB + NB] for q in range(4) for i in range(4)], axis=0
        )
    )
    for v in range(4):

        @pl.when(ct == v)
        def _(v=v):
            top = v * 128
            down = pl.ds(top, 512 - top)
            total = front_ref[down, :] - three((fh[down, :], fl[down, :]), cols, mt)
            for child in range(2):
                m = jnp.concatenate(
                    [col_ref[child, v * 4 + j : v * 4 + j + 1, :] for j in range(4)], axis=1
                )
                m = jnp.where(m < 0, -1, ((m >> 6) & 1) * 512 + (m >> 7) * 64 + (m & 63))
                put = onehot(m == iota((1024, 512), 0))
                total = total + mm(yh[child, down, :], put) + mm(yl[child, down, :], put)
            r, c = top + iota(total.shape, 0), v * 512 + iota(total.shape, 1)
            nat_row = ((r >> 5) * 32 + rg) * 32 + (r & 31)
            nat_col = ((c >> 5) * 8 + cg) * 32 + (c & 31)
            total = jnp.where(nat_row >= nat_col, total, F32(0.0))
            if v == 0:
                lane = iota((512, 128), 1)
                value = jnp.where(natural_lower(rg, cg, 512, 128, 0), panel_ref[...], F32(0.0))
                o_ref[:, :128] = jnp.where(lane < 64, value, total[:, :128])
                o_ref[:, 128:] = total[:, 128:]
            else:
                o_ref[:top, :] = jnp.zeros((top, 512), F32)
                o_ref[down, :] = total


def body(front, child_blocks, child_map):
    sub, row, cg = lax.axis_index("sub"), lax.axis_index("row"), lax.axis_index("col")
    rg = sub * 16 + row
    at = jnp.stack([rg, cg]).astype(I32)
    DMA = pltpu.SemaphoreType.DMA
    lower, inverse, slots, cols, own_rows, col_rows, received = pl.pallas_call(
        panel_kernel,
        out_shape=(
            jax.ShapeDtypeStruct((NB, PW), F32),
            jax.ShapeDtypeStruct((PW, PW), F32),
            jax.ShapeDtypeStruct((2, NB, 16), I32),
            jax.ShapeDtypeStruct((2, 16, 128), I32),
            jax.ShapeDtypeStruct((8, 256, 128), F32),
            jax.ShapeDtypeStruct((32, 256, 128), F32),
            jax.ShapeDtypeStruct((2, 32, CAP, 512), F32),
        ),
        grid=(1,),
        in_specs=[
            pl.BlockSpec((2, 8192), lambda i: (0, 0)),
            pl.BlockSpec((512, 1024), lambda i: (0, 0)),
            pl.BlockSpec((512, 128), lambda i: (0, 0)),
        ],
        out_specs=(
            pl.BlockSpec((NB, PW), lambda i: (0, 0)),
            pl.BlockSpec((PW, PW), lambda i: (0, 0)),
            pl.BlockSpec((2, NB, 16), lambda i: (0, 0, 0)),
            pl.BlockSpec((2, 16, 128), lambda i: (0, 0, 0)),
            pl.BlockSpec(memory_space=pl.ANY),
            pl.BlockSpec(memory_space=pl.ANY),
            pl.BlockSpec(memory_space=pl.ANY),
        ),
        scratch_shapes=[
            pltpu.VMEM((2, 8, 64, 512), F32),
            pltpu.VMEM((2, 8, 64, 512), F32),
            pltpu.VMEM((2, 32, CAP, 512), F32),
            pltpu.VMEM((8, 64, 512), F32),
            pltpu.VMEM((128, 512), F32),
            pltpu.VMEM((32, CAP, 128), F32),
            pltpu.VMEM((32, CAP, 128), F32),
            pltpu.VMEM((256, 128), F32),
            pltpu.VMEM((256, 128), F32),
            pltpu.VMEM((NB, 128), F32),
            pltpu.VMEM((8, NB, 128), F32),
            pltpu.VMEM((16, NB, PW), F32),
            pltpu.VMEM((PW, 2 * PW), F32),
            DMA((8,)), DMA, DMA((32,)), DMA((32,)), DMA((8,)), DMA((8,)), DMA((8,)), DMA((8,)),
            DMA, DMA, DMA((32,)), DMA((16,)), DMA((8,)), DMA((2, 32)), DMA((16,)), DMA((4,)),
            DMA((2, 8)), DMA((2, 8)), DMA((2, 32)), DMA((2, 32)),
            pltpu.VMEM((64, 128), F32), DMA((2, 16)),
        ],
        name="panel",
        compiler_params=pltpu.CompilerParams(
            collective_id=1, has_side_effects=True, vmem_limit_bytes=56 << 20
        ),
        cost_estimate=pl.CostEstimate(flops=3 * 10**10, bytes_accessed=10**8, transcendentals=0),
    )(child_map, child_blocks[0], front)

    return pl.pallas_call(
        final_kernel,
        out_shape=jax.ShapeDtypeStruct((512, 2048), F32),
        grid=(4,),
        in_specs=[
            SM,
            pl.BlockSpec((2, NB, 16), lambda i: (0, 0, 0)),
            pl.BlockSpec((2, 16, 128), lambda i: (0, 0, 0)),
            pl.BlockSpec((2, 32, CAP, 512), lambda i: (0, 0, 0, 0)),
            pl.BlockSpec((512, 512), lambda i: (0, i)),
            pl.BlockSpec((8, 256, 128), lambda i: (0, 0, 0)),
            pl.BlockSpec((32, 64, 128), lambda i: (0, i, 0)),
            pl.BlockSpec((PW, PW), lambda i: (0, 0)),
            pl.BlockSpec((NB, PW), lambda i: (0, 0)),
        ],
        out_specs=pl.BlockSpec((512, 512), lambda i: (0, i)),
        scratch_shapes=[
            pltpu.VMEM((PW, PW), BF16),
            pltpu.VMEM((PW, PW), BF16),
            pltpu.VMEM((512, PW), BF16),
            pltpu.VMEM((512, PW), BF16),
            pltpu.VMEM((2, 512, 1024), BF16),
            pltpu.VMEM((2, 512, 1024), BF16),
            pltpu.VMEM((512, 128), F32),
        ],
        name="final",
        compiler_params=params(60),
    )(
        at,
        slots,
        cols,
        received,
        front,
        own_rows,
        col_rows,
        inverse,
        lower,
    )


def solution(mesh):
    return jax.shard_map(
        body,
        mesh=mesh,
        in_specs=(P(("sub", "row"), "col"), P("sub", "row", "col"), P()),
        out_specs=P(("sub", "row"), "col"),
        check_vma=False,
    )
```

```python
import functools

import jax
import jax.numpy as jnp
from jax import lax
from jax.experimental import pallas as pl
from jax.experimental.pallas import tpu as pltpu
from jax.sharding import PartitionSpec as P

PW = 512
NB = 32
CAP = 24
F32 = jnp.float32
BF16 = jnp.bfloat16
I32 = jnp.int32
AXES = ("sub", "row", "col")


def iota(shape, dim):
    return lax.broadcasted_iota(I32, shape, dim)


def onehot(cond):
    return jnp.where(cond, F32(1.0), F32(0.0)).astype(BF16)


def split(value):
    high = value.astype(BF16)
    return high, (value - high.astype(F32)).astype(BF16)


def mm(a, b):
    return lax.dot_general(a, b, (((1,), (0,)), ((), ())), preferred_element_type=F32)


def mt(a, b):
    return lax.dot_general(a, b, (((1,), (1,)), ((), ())), preferred_element_type=F32)


def params(mib=None):
    return pltpu.CompilerParams(vmem_limit_bytes=None if mib is None else mib << 20)


VM = pl.BlockSpec(memory_space=pltpu.VMEM)
SM = pl.BlockSpec(memory_space=pltpu.SMEM)


def ranks_of(owner, groups, rows):
    n = owner.shape[1]
    member = jnp.where(owner == iota((rows, n), 0), F32(1.0), F32(0.0))
    upto = onehot(iota((n, n), 0) <= iota((n, n), 1))
    counts = mm(member.astype(BF16), upto)
    return (jnp.sum(counts * member, axis=0, keepdims=True) - 1.0).astype(I32)


def index_work(rg, cg, map_ref, slot_ref, col_ref, flat_ref):
    upto = onehot(iota((512, 512), 0) <= iota((512, 512), 1))
    before64 = onehot(iota((64, 64), 1) < iota((64, 64), 0))
    before128 = onehot(iota((128, 128), 0) < iota((128, 128), 1))
    for child in range(2):
        chunks = [map_ref[child : child + 1, k * 512 : k * 512 + 512] for k in range(16)]
        match = onehot(((jnp.concatenate(chunks, axis=0) >> 5) & 31) == rg)
        counts = mm(match, upto)
        slots = jnp.zeros((NB, 16), F32)
        present = jnp.zeros((64, 128), F32)
        for k in range(16):
            here = chunks[k]
            block = here >> 5
            off = jnp.where((here & 31) == iota((128, 512), 0), F32(1.0), F32(0.0))
            own_rows = onehot(
                jnp.where((block & 31) == rg, block >> 5, -1) == iota((16, 512), 0)
            )
            ranked = (off[:NB] * counts[k : k + 1, :]).astype(BF16)
            off = off.astype(BF16)
            slots = slots + mt(ranked, own_rows) + F32(k * CAP) * mt(off[:NB], own_rows)
            own_cols = onehot(jnp.where((block & 7) == cg, block >> 3, -1) == iota((64, 512), 0))
            present = present + mt(own_cols, off)
        slot_ref[child] = slots.astype(I32) - 1
        pb = present.astype(BF16)
        ahead = jnp.sum(mm(before64, pb), axis=1, keepdims=True)
        place = ahead + mm(pb, before128)
        flat_ref[...] = jnp.where(present > 0.5, place + 1.0, F32(0.0))
        flat = flat_ref[pl.ds(0, 16, stride=4), :]
        for i in range(1, 4):
            flat = flat + pltpu.roll(flat_ref[pl.ds(i, 16, stride=4), :], NB * i, 1)
        col_ref[child] = flat.astype(I32) - 1


def natural_lower(rg, cg, rows, cols, col0):
    r, c = iota((rows, cols), 0), col0 + iota((rows, cols), 1)
    nat_row = ((r >> 5) * 32 + rg) * 32 + (r & 31)
    nat_col = ((c >> 5) * 8 + cg) * 32 + (c & 31)
    return nat_row >= nat_col


def row_picker(slots, n):
    parts = [onehot(slots[:, b : b + 1] == iota((NB, n), 1)) for b in range(16)]
    return jnp.concatenate(parts, axis=0)


GROUP = 8


def sweep(w):
    lane = iota((1, 128), 1)
    below = w
    done = []
    for k0 in range(0, 128, GROUP):
        n = 128 - k0
        column = [jnp.broadcast_to(below[:, k0 + j : k0 + j + 1], (n, 128)) for j in range(GROUP)]
        row = [below[j : j + 1, :] for j in range(GROUP)]
        scaled = []
        for j in range(GROUP):
            inv = 1.0 / column[j][j : j + 1, :]
            scaled.append(jnp.where(lane == k0 + j, F32(1.0), row[j]) * inv)
            for i in range(j + 1, GROUP):
                ratio = column[i][j : j + 1, :] * inv
                kept = jnp.where(lane == k0 + j, F32(0.0), row[i])
                row[i] = kept - column[j][i : i + 1, :] * scaled[j]
                column[i] = column[i] - column[j] * ratio
        done.extend(row)
        if n > GROUP:
            inside = (lane >= k0) & (lane < k0 + GROUP)
            rest = jnp.where(inside, F32(0.0), below[GROUP:])
            for j in range(GROUP):
                part = jnp.where((lane > k0 + j) & inside, F32(0.0), scaled[j])
                rest = rest - column[j][GROUP:] * part
            below = rest
    w = jnp.concatenate(done, axis=0)
    r, c = iota((128, 128), 0), iota((128, 128), 1)
    diag = jnp.sum(jnp.where(r == c, w, F32(0.0)), axis=1, keepdims=True)
    scale = 1.0 / jnp.sqrt(diag)
    upper = jnp.where(c >= r, w, F32(0.0)) * scale
    inverse = jnp.where(c < r, w, jnp.where(c == r, F32(1.0), F32(0.0))) * scale
    return upper, inverse


def exact(a, b, dims):
    return lax.dot_general(
        a, b, (dims, ((), ())), precision=lax.Precision.HIGHEST, preferred_element_type=F32
    )


def unpack(pieces, left):
    top, bottom = [], []
    for p in range(4):
        a, b = pieces[2 * p], pieces[2 * p + 1]
        top.append(jnp.where(left, a, pltpu.roll(b, 64, 1)))
        bottom.append(jnp.where(left, pltpu.roll(a, 64, 1), b))
    return jnp.concatenate(
        [jnp.concatenate(top, axis=1), jnp.concatenate(bottom, axis=1)], axis=0
    )


def three(a, b, dot):
    return dot(a[0], b[0]) + (dot(a[0], b[1]) + dot(a[1], b[0]))


def remote(src, dst, send, recv, device):
    return pltpu.make_async_remote_copy(
        src_ref=src, dst_ref=dst, send_sem=send, recv_sem=recv, device_id=device,
        device_id_type=pl.DeviceIdType.MESH,
    )


def panel_kernel(
    map_ref, child_ref, front_ref,
    slot_ref, col_ref, acc_ref, panel_ref, got_ref,
    own_ref, cols_ref, inv_ref, ih, il, fh, fl,
    zsend, zrecv, xsend, pan_send, pan_recv, rows_send, rows_recv, piece, swapped, head_send, head_recv, sbuf, w_ref,
    pan_s, pan_r, row_s, row_r, head_s, head_r, own_s, own_r, swap_s, swap_r, piv_s, piv_r,
    fan_s, fan_r, pass_s, loc_s, z_s, z_r, x_s, x_r, flat_ref, far_s,
):
    sub, row, cg = lax.axis_index("sub"), lax.axis_index("row"), lax.axis_index("col")
    rg = sub * 16 + row
    quarter, place = rg // 8, rg % 8
    mate = quarter * 8 + cg
    mate_id = (mate // 16, mate % 16, place)
    moves = place != cg
    twin = (1 - sub, row, cg)

    cmap = map_ref[pl.ds(sub, 1), pl.ds(pl.multiple_of(cg * 1024, 1024), 1024)]
    rmap = map_ref[pl.ds(sub, 1), pl.ds(pl.multiple_of(row * 512, 512), 512)]

    def each(first, last, fn):
        def go(q, carry):
            fn(q)
            return carry

        lax.fori_loop(first, last, go, 0)

    def line(q):
        return (cg + q) % 8

    def plane(q):
        p = (rg + q) % 32
        return p, (p // 16, p % 16, cg)

    def chip(q):
        r = (row + q) % 16
        return r, (sub, r, cg)

    barrier = pltpu.get_barrier_semaphore()

    def greet(device):
        pl.semaphore_signal(barrier, inc=1, device_id=device, device_id_type=pl.DeviceIdType.MESH)

    each(1, 8, lambda q: greet((sub, row, line(q))))
    each(1, 32, lambda q: greet(plane(q)[1]))

    @pl.when(moves)
    def _():
        greet(mate_id)

    pl.semaphore_wait(barrier, jnp.where(moves, 39, 38))

    pan_recv[64:, :] = jnp.zeros((64, 512), F32)

    def to_line(q):
        return remote(
            pan_send.at[q], pan_recv.at[pl.ds(0, 64)], pan_s.at[q], pan_r, (sub, row, q)
        )

    @pl.when(cg == 0)
    def _():
        keep = row * 512 + iota((512, 512), 0) >= iota((512, 512), 1)
        high, low = split(jnp.where(keep, child_ref[:, :512], F32(0.0)))
        n = iota((512, 512), 0)
        nat = (((n >> 5) & 1) * 8 + (n >> 6)) * NB + (n & 31)
        pick = onehot(cmap[:, :512] == nat)
        out = mt(pick, high) + mt(pick, low)
        for q in range(1, 8):
            pan_send[q] = out[q * 64 : q * 64 + 64, :]
            to_line(q).start()
        pan_recv[:64, :] = out[:64, :]

    def bulk(h, q, at):
        return remote(
            zsend.at[h, q], zrecv.at[h, at], z_s.at[h, q], z_r.at[h, at], (sub, row, q)
        )

    keep = row * 512 + iota((512, 1024), 0) >= cg * 1024 + iota((512, 1024), 1)
    high, low = split(jnp.where(keep, child_ref[...], F32(0.0)))
    owner = (cmap >> 5) & 7
    slot = owner * 128 + ranks_of(owner, 8, 16)

    def bulk_half(h):
        n = iota((512, 1024), 0)
        pick = onehot(slot == (n >> 6) * 128 + h * 64 + (n & 63))
        out = mt(pick, high) + mt(pick, low)
        for q in range(8):
            zsend[h, q] = out[q * 64 : q * 64 + 64, :]
        zrecv[h, cg] = zsend[h, cg]

    last = row // 2
    for c in range(1, 8):

        @pl.when(c > last)
        def _(c=c):
            zrecv[0, c] = jnp.zeros((64, 512), F32)
            zrecv[1, c] = jnp.zeros((64, 512), F32)

    def bulk_out(h):
        @pl.when(cg <= last)
        def _():
            each(1, 8, lambda q: bulk(h, line(q), cg).start())

    def bulk_in(h):
        def one(c):
            @pl.when(c != cg)
            def _():
                bulk(h, c, c).wait_recv()

        each(0, last + 1, one)

    bulk_half(0)
    bulk_half(1)
    owner = (rmap >> 5) & 31
    slot = owner * CAP + ranks_of(owner, 32, 32)
    pick_rows = onehot(slot == iota((32 * CAP, 512), 0))
    index_work(rg, cg, map_ref, slot_ref, col_ref, flat_ref)

    @pl.when(cg != 0)
    def _():
        to_line(cg).wait_recv()

    bulk_out(0)

    high, low = split(pan_recv[...])
    out = mt(pick_rows, high) + mt(pick_rows, low)
    for p in range(32):
        rows_send[p] = out[p * CAP : p * CAP + CAP, :]

    def to_plane(q):
        p, device = plane(q)
        return remote(rows_send.at[p], rows_recv.at[rg], row_s.at[p], row_r.at[rg], device)

    def from_plane(q):
        p, device = plane(q)
        return remote(rows_send.at[p], rows_recv.at[p], row_s.at[p], row_r.at[p], device)

    each(1, 32, lambda q: to_plane(q).start())
    rows_recv[rg] = rows_send[rg]
    total = jnp.where(natural_lower(rg, cg, 512, 128, 0), front_ref[...], F32(0.0))
    picks = [row_picker(slot_ref[child], 16 * CAP) for child in range(2)]
    each(1, 32, lambda q: from_plane(q).wait_recv())
    for child in range(2):
        got = rows_recv[child * 16 : child * 16 + 16].reshape(16 * CAP, 128)
        high, low = split(got)
        total = total + mm(picks[child], high) + mm(picks[child], low)
    left = iota((64, 128), 1) < 64
    for t in range(4):
        a = total[t * 128 : t * 128 + 64]
        b = total[t * 128 + 64 : t * 128 + 128]
        piece[t * 64 : t * 64 + 64, :] = jnp.where(left, a, pltpu.roll(b, 64, 1))
    head_send[...] = total[:NB, :]

    def head(q, at):
        return remote(
            head_send, head_recv.at[at], head_s.at[q], head_r.at[at], (sub, row, line(q))
        )

    def swap():
        return remote(piece, swapped, swap_s, swap_r, mate_id)

    def own_up(t, at, src):
        return remote(src, own_ref.at[at], own_s.at[t], own_r.at[at], (sub, row, line(1)))

    def own_down(t, at, src):
        return remote(src, own_ref.at[at], own_s.at[4 + t], own_r.at[at], (sub, row, line(7)))

    def ring(t):
        @pl.when(t < 4)
        def _():
            at = (cg + 8 - t) % 8
            own_up(t, at, own_ref.at[at]).wait_recv()
            own_up(t, at, own_ref.at[at]).start()

        @pl.when(t < 3)
        def _():
            at = (cg + t) % 8
            own_down(t, at, own_ref.at[at]).wait_recv()
            own_down(t, at, own_ref.at[at]).start()

    own_local = pltpu.make_async_copy(piece, own_ref.at[cg], loc_s.at[0])

    @pl.when(sub == 0)
    def _():
        each(1, 8, lambda q: head(q, cg).start())

    @pl.when(moves)
    def _():
        swap().start()

    head_recv[cg] = head_send[...]

    def cross(h, p, at, level):
        lanes = pl.ds(0, 128 * (level + 1))
        return remote(
            xsend.at[h, p, :, lanes], got_ref.at[h, at, :, lanes], x_s.at[h, p], x_r.at[h, at],
            (p // 16, p % 16, cg),
        )

    def by_level(fn):
        for level in range(4):

            @pl.when(row // 4 == level)
            def _(level=level):
                each(1, 32, lambda q: fn(plane(q)[0], level))

    def cross_out(h):
        by_level(lambda p, level: cross(h, p, rg, level).start())

    def cross_in(h):
        for level in range(4):

            def one(j):
                p = j // 4 * 16 + level * 4 + j % 4

                @pl.when(p != rg)
                def _():
                    cross(h, p, p, level).wait_recv()

            each(0, 8, one)

    def keep_own(h):
        return pltpu.make_async_copy(xsend.at[h, rg], got_ref.at[h, rg], loc_s.at[2 + h])

    def cross_half(h):
        bulk_in(h)
        high, low = split(zrecv[h].reshape(512, 512))
        out = mt(pick_rows, high) + mt(pick_rows, low)
        for p in range(32):
            xsend[h, p] = out[p * CAP : p * CAP + CAP, :]
        cross_out(h)
        keep_own(h).start()

    def pivot(q, at):
        return remote(sbuf.at[at], sbuf.at[at], piv_s.at[q], piv_r.at[at], chip(q)[1])

    def pivot_twin(at):
        return remote(sbuf.at[at], sbuf.at[at], piv_s.at[16 + at], piv_r.at[at], (1, row, cg))

    @pl.when(sub == 0)
    def _():
        each(1, 8, lambda q: head(q, line(q)).wait_recv())
        half = iota((NB, 128), 1) < 64
        rows = [
            jnp.where(half, head_recv[2 * p], pltpu.roll(head_recv[2 * p + 1], 64, 1))
            for p in range(4)
        ]
        sbuf[row] = jnp.concatenate(rows, axis=1)
        each(1, 16, lambda q: pivot(q, row).start())
        pivot_twin(row).start()

    bulk_out(1)

    @pl.when(moves)
    def _():
        swap().wait_recv()

    @pl.when(jnp.logical_not(moves))
    def _():
        swapped[...] = piece[...]

    gx, gy = row // 4, row % 4

    def xmate(j):
        return (gx + j) % 4 * 4 + gy

    def ymate(j):
        return gx * 4 + (gy + j) % 4

    def fan(k, at, to):
        return remote(swapped, cols_ref.at[at], fan_s.at[k], fan_r.at[0, at], (sub, to, cg))

    def far(half, k, at, to):
        part = cols_ref.at[at, pl.ds(half * 128, 128)]
        return remote(part, part, far_s.at[half, k], fan_r.at[half, at], (sub, to, cg))

    def hand(at, src):
        return remote(src, cols_ref.at[at], pass_s.at[at % 16], fan_r.at[0, at], twin)

    def near(j):
        x, y = xmate(j), ymate(j)
        fan(j, sub * 16 + x, x).wait_recv()
        each(1, 4, lambda i: far(0, j * 4 + i, sub * 16 + x, ymate(i)).start())
        hand(sub * 16 + x, cols_ref.at[sub * 16 + x]).start()
        fan(4 + j, sub * 16 + y, y).wait_recv()
        each(1, 4, lambda i: far(1, j * 4 + i, sub * 16 + y, xmate(i)).start())
        hand(sub * 16 + y, cols_ref.at[sub * 16 + y]).start()

    def corner(i, j):
        at = sub * 16 + (gx + i) % 4 * 4 + (gy + j) % 4
        far(0, 0, at, 0).wait_recv()
        far(1, 0, at, 0).wait_recv()
        hand(at, cols_ref.at[at]).start()

    cols_local = pltpu.make_async_copy(swapped, cols_ref.at[rg], loc_s.at[1])

    def fan_out(j):
        fan(j, rg, xmate(j)).start()
        fan(4 + j, rg, ymate(j)).start()

    each(1, 4, fan_out)
    hand(rg, swapped).start()
    cols_local.start()
    own_up(0, cg, piece).start()
    own_down(0, cg, piece).start()
    own_local.start()

    cross_half(0)

    @pl.when(sub == 0)
    def _():
        def relay(q):
            at = chip(q)[0]
            pivot(q, at).wait_recv()
            pivot_twin(at).start()

        each(1, 16, relay)

    @pl.when(sub == 1)
    def _():
        each(0, 16, lambda q: pivot_twin(q).wait_recv())

    turned = sbuf[...].reshape(PW, PW).T
    for c8 in range(8):
        for half in range(2):
            src = (c8 * 2 + half) * NB
            w_ref[(half * 8 + c8) * NB : (half * 8 + c8 + 1) * NB, :PW] = turned[src : src + NB, :]
    r, c = iota((PW, PW), 0), iota((PW, PW), 1)
    raw = w_ref[:, :PW]
    w_ref[:, :PW] = jnp.where(c >= r, raw, F32(0.0)) + jnp.where(c > r, raw, F32(0.0)).T
    w_ref[:, PW:] = jnp.where(r == c, F32(1.0), F32(0.0))

    def step(kb, carry):
        at = pl.multiple_of(kb * 128, 128)
        upper, inverse = sweep(w_ref[pl.ds(at, 128), pl.ds(at, 128)])
        rows = exact(inverse, w_ref[pl.ds(at, 128), :], ((1,), (0,)))
        lanes = iota((128, PW), 1)
        ahead = jnp.where(lanes >= at + 128, rows[:, :PW], F32(0.0))
        w_ref[...] = w_ref[...] - exact(ahead, rows, ((0,), (0,)))
        w_ref[pl.ds(at, 128), :] = jnp.concatenate([ahead, rows[:, PW:]], axis=1)
        w_ref[pl.ds(at, 128), pl.ds(at, 128)] = upper

        ring(kb + 1)

        @pl.when(kb == 0)
        def _():
            each(1, 4, near)

        @pl.when(kb > 0)
        def _():
            each(1, 4, lambda j: corner(kb, j))

        @pl.when(kb == 1)
        def _():
            cross_half(1)

        return carry

    lax.fori_loop(0, PW // 128, step, 0)
    turned = w_ref[:, PW:].T
    for c8 in range(8):
        for half in range(2):
            src = (half * 8 + c8) * NB
            inv_ref[(c8 * 2 + half) * NB : (c8 * 2 + half + 1) * NB, :] = turned[src : src + NB, :]
    ih[...], il[...] = split(inv_ref[...])
    w_ref[:, :PW] = w_ref[:, :PW].T
    known = w_ref[pl.ds(pl.multiple_of(jnp.minimum(rg, 15) * NB, NB), NB), :PW]

    own_up(0, line(4), piece).wait_recv()
    own_down(0, line(3), piece).wait_recv()
    own_local.wait()
    for t in range(4):
        tile = unpack([own_ref[c, t * 64 : t * 64 + 64, :] for c in range(8)], left)
        rows = three(split(tile), (ih[...], il[...]), mm)
        if t == 0:
            keep = (iota((128, PW), 0) < NB) & (rg < 16)
            rows = jnp.where(
                keep, jnp.concatenate([known, jnp.zeros((128 - NB, PW), F32)], axis=0), rows
            )
        fh[t * 128 : t * 128 + 128, :], fl[t * 128 : t * 128 + 128, :] = split(rows)
    lane = iota((PW, 128), 1)
    nat = ((lane >> 5) * 8 + cg) * 32 + (lane & 31)
    pick = onehot((nat == iota((PW, 128), 0)) & (lane < 64))
    panel_ref[...] = mm(fh[...], pick) + mm(fl[...], pick)

    each(0, 16, lambda q: hand((1 - sub) * 16 + q, swapped).wait_recv())
    cols_local.wait()
    for v in range(4):
        parts = []
        for i in range(4):
            tile = unpack(
                [cols_ref[i * 8 + c, v * 64 : v * 64 + 64, :] for c in range(8)], left
            )
            parts.append(three(split(tile), (ih[...], il[...]), mm))
        cols = split(
            jnp.concatenate(
                [parts[i][q * NB : q * NB + NB] for q in range(4) for i in range(4)], axis=0
            )
        )
        down = pl.ds(v * 128, 512 - v * 128)
        acc_ref[down, pl.ds(v * 512, 512)] = three((fh[down, :], fl[down, :]), cols, mt)

    each(0, 16, lambda q: hand(sub * 16 + q, swapped).wait_send())

    def sent(j):
        fan(j, rg, xmate(j)).wait_send()
        fan(4 + j, rg, ymate(j)).wait_send()
        each(1, 4, lambda i: far(0, j * 4 + i, rg, ymate(i)).wait_send())
        each(1, 4, lambda i: far(1, j * 4 + i, rg, xmate(i)).wait_send())

    each(1, 4, sent)
    each(0, 4, lambda t: own_up(t, cg, piece).wait_send())
    each(0, 3, lambda t: own_down(t, cg, piece).wait_send())
    each(1, 32, lambda q: to_plane(q).wait_send())
    for h in range(2):

        @pl.when(cg <= last)
        def _(h=h):
            each(1, 8, lambda q: bulk(h, line(q), cg).wait_send())

        cross_in(h)
        by_level(lambda p, level: cross(h, p, rg, level).wait_send())
        keep_own(h).wait()

    @pl.when(cg == 0)
    def _():
        each(1, 8, lambda q: to_line(q).wait_send())

    @pl.when(moves)
    def _():
        swap().wait_send()

    @pl.when(sub == 0)
    def _():
        each(1, 8, lambda q: head(q, cg).wait_send())
        each(1, 16, lambda q: pivot(q, row).wait_send())
        each(0, 16, lambda q: pivot_twin(q).wait_send())


def final_kernel(
    at_ref, slot_ref, col_ref, x_ref, front_ref, acc_ref, panel_ref, o_ref, yh, yl,
):
    rg, cg = at_ref[0], at_ref[1]
    ct = pl.program_id(0)

    @pl.when(ct == 0)
    def _():
        for child in range(2):
            pick = row_picker(slot_ref[child], 16 * CAP)
            for h in range(2):
                got = x_ref[h, child * 16 : child * 16 + 16].reshape(16 * CAP, 512)
                r, lane = iota(got.shape, 0), iota(got.shape, 1)
                limit = jnp.where(r < 4 * CAP, 128, jnp.where(r < 8 * CAP, 256, 384))
                got = jnp.where((lane < limit) | (r >= 12 * CAP), got, F32(0.0))
                high, low = split(got)
                at = pl.ds(h * 512, 512)
                yh[child, :, at], yl[child, :, at] = split(mm(pick, high) + mm(pick, low))

    for v in range(4):

        @pl.when(ct == v)
        def _(v=v):
            top = v * 128
            down = pl.ds(top, 512 - top)
            total = front_ref[down, :] - acc_ref[down, :]
            for child in range(2):
                m = jnp.concatenate(
                    [col_ref[child, v * 4 + j : v * 4 + j + 1, :] for j in range(4)], axis=1
                )
                m = jnp.where(m < 0, -1, ((m >> 6) & 1) * 512 + (m >> 7) * 64 + (m & 63))
                put = onehot(m == iota((1024, 512), 0))
                total = total + mm(yh[child, down, :], put) + mm(yl[child, down, :], put)
            r, c = top + iota(total.shape, 0), v * 512 + iota(total.shape, 1)
            nat_row = ((r >> 5) * 32 + rg) * 32 + (r & 31)
            nat_col = ((c >> 5) * 8 + cg) * 32 + (c & 31)
            total = jnp.where(nat_row >= nat_col, total, F32(0.0))
            if v == 0:
                lane = iota((512, 128), 1)
                value = jnp.where(natural_lower(rg, cg, 512, 128, 0), panel_ref[...], F32(0.0))
                o_ref[:, :128] = jnp.where(lane < 64, value, total[:, :128])
                o_ref[:, 128:] = total[:, 128:]
            else:
                o_ref[:top, :] = jnp.zeros((top, 512), F32)
                o_ref[down, :] = total


def body(front, child_blocks, child_map):
    sub, row, cg = lax.axis_index("sub"), lax.axis_index("row"), lax.axis_index("col")
    rg = sub * 16 + row
    at = jnp.stack([rg, cg]).astype(I32)
    DMA = pltpu.SemaphoreType.DMA
    slots, cols, product, panel, received = pl.pallas_call(
        panel_kernel,
        out_shape=(
            jax.ShapeDtypeStruct((2, NB, 16), I32),
            jax.ShapeDtypeStruct((2, 16, 128), I32),
            jax.ShapeDtypeStruct((512, 2048), F32),
            jax.ShapeDtypeStruct((512, 128), F32),
            jax.ShapeDtypeStruct((2, 32, CAP, 512), F32),
        ),
        grid=(1,),
        in_specs=[
            pl.BlockSpec((2, 8192), lambda i: (0, 0)),
            pl.BlockSpec((512, 1024), lambda i: (0, 0)),
            pl.BlockSpec((512, 128), lambda i: (0, 0)),
        ],
        out_specs=(
            pl.BlockSpec((2, NB, 16), lambda i: (0, 0, 0)),
            pl.BlockSpec((2, 16, 128), lambda i: (0, 0, 0)),
            pl.BlockSpec((512, 2048), lambda i: (0, 0)),
            pl.BlockSpec((512, 128), lambda i: (0, 0)),
            pl.BlockSpec(memory_space=pl.ANY),
        ),
        scratch_shapes=[
            pltpu.VMEM((8, 256, 128), F32),
            pltpu.VMEM((32, 256, 128), F32),
            pltpu.VMEM((PW, PW), F32),
            pltpu.VMEM((PW, PW), BF16),
            pltpu.VMEM((PW, PW), BF16),
            pltpu.VMEM((512, PW), BF16),
            pltpu.VMEM((512, PW), BF16),
            pltpu.VMEM((2, 8, 64, 512), F32),
            pltpu.VMEM((2, 8, 64, 512), F32),
            pltpu.VMEM((2, 32, CAP, 512), F32),
            pltpu.VMEM((8, 64, 512), F32),
            pltpu.VMEM((128, 512), F32),
            pltpu.VMEM((32, CAP, 128), F32),
            pltpu.VMEM((32, CAP, 128), F32),
            pltpu.VMEM((256, 128), F32),
            pltpu.VMEM((256, 128), F32),
            pltpu.VMEM((NB, 128), F32),
            pltpu.VMEM((8, NB, 128), F32),
            pltpu.VMEM((16, NB, PW), F32),
            pltpu.VMEM((PW, 2 * PW), F32),
            DMA((8,)), DMA, DMA((32,)), DMA((32,)), DMA((8,)), DMA((8,)), DMA((8,)), DMA((8,)),
            DMA, DMA, DMA((32,)), DMA((16,)), DMA((8,)), DMA((2, 32)), DMA((16,)), DMA((4,)),
            DMA((2, 8)), DMA((2, 8)), DMA((2, 32)), DMA((2, 32)),
            pltpu.VMEM((64, 128), F32), DMA((2, 16)),
        ],
        name="panel",
        compiler_params=pltpu.CompilerParams(
            collective_id=1, has_side_effects=True, vmem_limit_bytes=56 << 20
        ),
        cost_estimate=pl.CostEstimate(flops=3 * 10**10, bytes_accessed=10**8, transcendentals=0),
    )(child_map, child_blocks[0], front)

    return pl.pallas_call(
        final_kernel,
        out_shape=jax.ShapeDtypeStruct((512, 2048), F32),
        grid=(4,),
        in_specs=[
            SM,
            pl.BlockSpec((2, NB, 16), lambda i: (0, 0, 0)),
            pl.BlockSpec((2, 16, 128), lambda i: (0, 0, 0)),
            pl.BlockSpec((2, 32, CAP, 512), lambda i: (0, 0, 0, 0)),
            pl.BlockSpec((512, 512), lambda i: (0, i)),
            pl.BlockSpec((512, 512), lambda i: (0, i)),
            pl.BlockSpec((512, 128), lambda i: (0, 0)),
        ],
        out_specs=pl.BlockSpec((512, 512), lambda i: (0, i)),
        scratch_shapes=[
            pltpu.VMEM((2, 512, 1024), BF16),
            pltpu.VMEM((2, 512, 1024), BF16),
        ],
        name="final",
        compiler_params=params(60),
    )(
        at,
        slots,
        cols,
        received,
        front,
        product,
        panel,
    )


def solution(mesh):
    return jax.shard_map(
        body,
        mesh=mesh,
        in_specs=(P(("sub", "row"), "col"), P("sub", "row", "col"), P()),
        out_specs=P(("sub", "row"), "col"),
        check_vma=False,
    )
```

```python
import functools

import jax
import jax.numpy as jnp
from jax import lax
from jax.experimental import pallas as pl
from jax.experimental.pallas import tpu as pltpu
from jax.sharding import PartitionSpec as P

PW = 512
NB = 32
CAP = 24
F32 = jnp.float32
BF16 = jnp.bfloat16
I32 = jnp.int32
AXES = ("sub", "row", "col")


def iota(shape, dim):
    return lax.broadcasted_iota(I32, shape, dim)


def onehot(cond):
    return jnp.where(cond, F32(1.0), F32(0.0)).astype(BF16)


def split(value):
    high = value.astype(BF16)
    return high, (value - high.astype(F32)).astype(BF16)


def mm(a, b):
    return lax.dot_general(a, b, (((1,), (0,)), ((), ())), preferred_element_type=F32)


def mt(a, b):
    return lax.dot_general(a, b, (((1,), (1,)), ((), ())), preferred_element_type=F32)


def params(mib=None):
    return pltpu.CompilerParams(vmem_limit_bytes=None if mib is None else mib << 20)


VM = pl.BlockSpec(memory_space=pltpu.VMEM)
SM = pl.BlockSpec(memory_space=pltpu.SMEM)


def ranks_of(owner, groups, rows):
    n = owner.shape[1]
    member = jnp.where(owner == iota((rows, n), 0), F32(1.0), F32(0.0))
    upto = onehot(iota((n, n), 0) <= iota((n, n), 1))
    counts = mm(member.astype(BF16), upto)
    return (jnp.sum(counts * member, axis=0, keepdims=True) - 1.0).astype(I32)


def index_work(rg, cg, map_ref, slot_ref, col_ref, flat_ref):
    upto = onehot(iota((512, 512), 0) <= iota((512, 512), 1))
    before64 = onehot(iota((64, 64), 1) < iota((64, 64), 0))
    before128 = onehot(iota((128, 128), 0) < iota((128, 128), 1))
    for child in range(2):
        chunks = [map_ref[child : child + 1, k * 512 : k * 512 + 512] for k in range(16)]
        match = onehot(((jnp.concatenate(chunks, axis=0) >> 5) & 31) == rg)
        counts = mm(match, upto)
        slots = jnp.zeros((NB, 16), F32)
        present = jnp.zeros((64, 128), F32)
        for k in range(16):
            here = chunks[k]
            block = here >> 5
            off = jnp.where((here & 31) == iota((128, 512), 0), F32(1.0), F32(0.0))
            own_rows = onehot(
                jnp.where((block & 31) == rg, block >> 5, -1) == iota((16, 512), 0)
            )
            ranked = (off[:NB] * counts[k : k + 1, :]).astype(BF16)
            off = off.astype(BF16)
            slots = slots + mt(ranked, own_rows) + F32(k * CAP) * mt(off[:NB], own_rows)
            own_cols = onehot(jnp.where((block & 7) == cg, block >> 3, -1) == iota((64, 512), 0))
            present = present + mt(own_cols, off)
        slot_ref[child] = slots.astype(I32) - 1
        pb = present.astype(BF16)
        ahead = jnp.sum(mm(before64, pb), axis=1, keepdims=True)
        place = ahead + mm(pb, before128)
        flat_ref[...] = jnp.where(present > 0.5, place + 1.0, F32(0.0))
        flat = flat_ref[pl.ds(0, 16, stride=4), :]
        for i in range(1, 4):
            flat = flat + pltpu.roll(flat_ref[pl.ds(i, 16, stride=4), :], NB * i, 1)
        col_ref[child] = flat.astype(I32) - 1


def natural_lower(rg, cg, rows, cols, col0):
    r, c = iota((rows, cols), 0), col0 + iota((rows, cols), 1)
    nat_row = ((r >> 5) * 32 + rg) * 32 + (r & 31)
    nat_col = ((c >> 5) * 8 + cg) * 32 + (c & 31)
    return nat_row >= nat_col


def row_picker(slots, n):
    parts = [onehot(slots[:, b : b + 1] == iota((NB, n), 1)) for b in range(16)]
    return jnp.concatenate(parts, axis=0)


GROUP = 8


def sweep(w):
    lane = iota((1, 128), 1)
    below = w
    done = []
    for k0 in range(0, 128, GROUP):
        n = 128 - k0
        column = [jnp.broadcast_to(below[:, k0 + j : k0 + j + 1], (n, 128)) for j in range(GROUP)]
        row = [below[j : j + 1, :] for j in range(GROUP)]
        scaled = []
        for j in range(GROUP):
            inv = 1.0 / column[j][j : j + 1, :]
            scaled.append(jnp.where(lane == k0 + j, F32(1.0), row[j]) * inv)
            for i in range(j + 1, GROUP):
                ratio = column[i][j : j + 1, :] * inv
                kept = jnp.where(lane == k0 + j, F32(0.0), row[i])
                row[i] = kept - column[j][i : i + 1, :] * scaled[j]
                column[i] = column[i] - column[j] * ratio
        done.extend(row)
        if n > GROUP:
            inside = (lane >= k0) & (lane < k0 + GROUP)
            rest = jnp.where(inside, F32(0.0), below[GROUP:])
            for j in range(GROUP):
                part = jnp.where((lane > k0 + j) & inside, F32(0.0), scaled[j])
                rest = rest - column[j][GROUP:] * part
            below = rest
    w = jnp.concatenate(done, axis=0)
    r, c = iota((128, 128), 0), iota((128, 128), 1)
    diag = jnp.sum(jnp.where(r == c, w, F32(0.0)), axis=1, keepdims=True)
    scale = 1.0 / jnp.sqrt(diag)
    upper = jnp.where(c >= r, w, F32(0.0)) * scale
    inverse = jnp.where(c < r, w, jnp.where(c == r, F32(1.0), F32(0.0))) * scale
    return upper, inverse


def exact(a, b, dims):
    return lax.dot_general(
        a, b, (dims, ((), ())), precision=lax.Precision.HIGHEST, preferred_element_type=F32
    )


def unpack(pieces, left):
    top, bottom = [], []
    for p in range(4):
        a, b = pieces[2 * p], pieces[2 * p + 1]
        top.append(jnp.where(left, a, pltpu.roll(b, 64, 1)))
        bottom.append(jnp.where(left, pltpu.roll(a, 64, 1), b))
    return jnp.concatenate(
        [jnp.concatenate(top, axis=1), jnp.concatenate(bottom, axis=1)], axis=0
    )


def three(a, b, dot):
    return dot(a[0], b[0]) + (dot(a[0], b[1]) + dot(a[1], b[0]))


def remote(src, dst, send, recv, device):
    return pltpu.make_async_remote_copy(
        src_ref=src, dst_ref=dst, send_sem=send, recv_sem=recv, device_id=device,
        device_id_type=pl.DeviceIdType.MESH,
    )


def panel_kernel(
    map_ref, child_ref, front_ref,
    slot_ref, col_ref, acc_ref, panel_ref, got_ref,
    own_ref, cols_ref, inv_ref, ih, il, fh, fl,
    zsend, zrecv, xsend, pan_send, pan_recv, rows_send, rows_recv, piece, swapped, head_send, head_recv, sbuf, w_ref,
    pan_s, pan_r, row_s, row_r, head_s, head_r, own_s, own_r, swap_s, swap_r, piv_s, piv_r,
    fan_s, fan_r, pass_s, loc_s, z_s, z_r, x_s, x_r, flat_ref, far_s,
):
    sub, row, cg = lax.axis_index("sub"), lax.axis_index("row"), lax.axis_index("col")
    rg = sub * 16 + row
    quarter, place = rg // 8, rg % 8
    mate = quarter * 8 + cg
    mate_id = (mate // 16, mate % 16, place)
    moves = place != cg
    twin = (1 - sub, row, cg)

    cmap = map_ref[pl.ds(sub, 1), pl.ds(pl.multiple_of(cg * 1024, 1024), 1024)]
    rmap = map_ref[pl.ds(sub, 1), pl.ds(pl.multiple_of(row * 512, 512), 512)]

    def each(first, last, fn):
        def go(q, carry):
            fn(q)
            return carry

        lax.fori_loop(first, last, go, 0)

    def line(q):
        return (cg + q) % 8

    def plane(q):
        p = (rg + q) % 32
        return p, (p // 16, p % 16, cg)

    def chip(q):
        r = (row + q) % 16
        return r, (sub, r, cg)

    barrier = pltpu.get_barrier_semaphore()

    def greet(device):
        pl.semaphore_signal(barrier, inc=1, device_id=device, device_id_type=pl.DeviceIdType.MESH)

    each(1, 8, lambda q: greet((sub, row, line(q))))
    each(1, 32, lambda q: greet(plane(q)[1]))

    @pl.when(moves)
    def _():
        greet(mate_id)

    pl.semaphore_wait(barrier, jnp.where(moves, 39, 38))

    pan_recv[64:, :] = jnp.zeros((64, 512), F32)

    def to_line(q):
        return remote(
            pan_send.at[q], pan_recv.at[pl.ds(0, 64)], pan_s.at[q], pan_r, (sub, row, q)
        )

    @pl.when(cg == 0)
    def _():
        keep = row * 512 + iota((512, 512), 0) >= iota((512, 512), 1)
        high, low = split(jnp.where(keep, child_ref[:, :512], F32(0.0)))
        n = iota((512, 512), 0)
        nat = (((n >> 5) & 1) * 8 + (n >> 6)) * NB + (n & 31)
        pick = onehot(cmap[:, :512] == nat)
        out = mt(pick, high) + mt(pick, low)
        for q in range(1, 8):
            pan_send[q] = out[q * 64 : q * 64 + 64, :]
            to_line(q).start()
        pan_recv[:64, :] = out[:64, :]

    def bulk(h, q, at):
        return remote(
            zsend.at[h, q], zrecv.at[h, at], z_s.at[h, q], z_r.at[h, at], (sub, row, q)
        )

    keep = row * 512 + iota((512, 1024), 0) >= cg * 1024 + iota((512, 1024), 1)
    high, low = split(jnp.where(keep, child_ref[...], F32(0.0)))
    owner = (cmap >> 5) & 7
    slot = owner * 128 + ranks_of(owner, 8, 16)

    def bulk_half(h):
        n = iota((512, 1024), 0)
        pick = onehot(slot == (n >> 6) * 128 + h * 64 + (n & 63))
        out = mt(pick, high) + mt(pick, low)
        for q in range(8):
            zsend[h, q] = out[q * 64 : q * 64 + 64, :]
        zrecv[h, cg] = zsend[h, cg]

    last = row // 2
    for c in range(1, 8):

        @pl.when(c > last)
        def _(c=c):
            zrecv[0, c] = jnp.zeros((64, 512), F32)
            zrecv[1, c] = jnp.zeros((64, 512), F32)

    def bulk_out(h):
        @pl.when(cg <= last)
        def _():
            each(1, 8, lambda q: bulk(h, line(q), cg).start())

    def bulk_in(h):
        def one(c):
            @pl.when(c != cg)
            def _():
                bulk(h, c, c).wait_recv()

        each(0, last + 1, one)

    bulk_half(0)
    bulk_half(1)
    owner = (rmap >> 5) & 31
    slot = owner * CAP + ranks_of(owner, 32, 32)
    pick_rows = onehot(slot == iota((32 * CAP, 512), 0))
    index_work(rg, cg, map_ref, slot_ref, col_ref, flat_ref)

    @pl.when(cg != 0)
    def _():
        to_line(cg).wait_recv()

    bulk_out(0)

    high, low = split(pan_recv[...])
    out = mt(pick_rows, high) + mt(pick_rows, low)
    for p in range(32):
        rows_send[p] = out[p * CAP : p * CAP + CAP, :]

    def to_plane(q):
        p, device = plane(q)
        return remote(rows_send.at[p], rows_recv.at[rg], row_s.at[p], row_r.at[rg], device)

    def from_plane(q):
        p, device = plane(q)
        return remote(rows_send.at[p], rows_recv.at[p], row_s.at[p], row_r.at[p], device)

    each(1, 32, lambda q: to_plane(q).start())
    rows_recv[rg] = rows_send[rg]
    total = jnp.where(natural_lower(rg, cg, 512, 128, 0), front_ref[...], F32(0.0))
    picks = [row_picker(slot_ref[child], 16 * CAP) for child in range(2)]
    each(1, 32, lambda q: from_plane(q).wait_recv())
    for child in range(2):
        got = rows_recv[child * 16 : child * 16 + 16].reshape(16 * CAP, 128)
        high, low = split(got)
        total = total + mm(picks[child], high) + mm(picks[child], low)
    left = iota((64, 128), 1) < 64
    for t in range(4):
        a = total[t * 128 : t * 128 + 64]
        b = total[t * 128 + 64 : t * 128 + 128]
        piece[t * 64 : t * 64 + 64, :] = jnp.where(left, a, pltpu.roll(b, 64, 1))
    head_send[...] = total[:NB, :]

    def head(q, at):
        return remote(
            head_send, head_recv.at[at], head_s.at[q], head_r.at[at], (sub, row, line(q))
        )

    def swap():
        return remote(piece, swapped, swap_s, swap_r, mate_id)

    def own_up(t, at, src):
        return remote(src, own_ref.at[at], own_s.at[t], own_r.at[at], (sub, row, line(1)))

    def own_down(t, at, src):
        return remote(src, own_ref.at[at], own_s.at[4 + t], own_r.at[at], (sub, row, line(7)))

    def ring(t):
        @pl.when(t < 4)
        def _():
            at = (cg + 8 - t) % 8
            own_up(t, at, own_ref.at[at]).wait_recv()
            own_up(t, at, own_ref.at[at]).start()

        @pl.when(t < 3)
        def _():
            at = (cg + t) % 8
            own_down(t, at, own_ref.at[at]).wait_recv()
            own_down(t, at, own_ref.at[at]).start()

    own_local = pltpu.make_async_copy(piece, own_ref.at[cg], loc_s.at[0])

    @pl.when(sub == 0)
    def _():
        each(1, 8, lambda q: head(q, cg).start())

    @pl.when(moves)
    def _():
        swap().start()

    head_recv[cg] = head_send[...]

    def cross(h, p, at, level):
        lanes = pl.ds(0, 128 * (level + 1))
        return remote(
            xsend.at[h, p, :, lanes], got_ref.at[h, at, :, lanes], x_s.at[h, p], x_r.at[h, at],
            (p // 16, p % 16, cg),
        )

    def by_level(fn):
        for level in range(4):

            @pl.when(row // 4 == level)
            def _(level=level):
                each(1, 32, lambda q: fn(plane(q)[0], level))

    def cross_out(h):
        by_level(lambda p, level: cross(h, p, rg, level).start())

    def cross_in(h):
        for level in range(4):

            def one(j):
                p = j // 4 * 16 + level * 4 + j % 4

                @pl.when(p != rg)
                def _():
                    cross(h, p, p, level).wait_recv()

            each(0, 8, one)

    def keep_own(h):
        return pltpu.make_async_copy(xsend.at[h, rg], got_ref.at[h, rg], loc_s.at[2 + h])

    def cross_half(h):
        bulk_in(h)
        high, low = split(zrecv[h].reshape(512, 512))
        out = mt(pick_rows, high) + mt(pick_rows, low)
        for p in range(32):
            xsend[h, p] = out[p * CAP : p * CAP + CAP, :]
        cross_out(h)
        keep_own(h).start()

    def pivot(q, at):
        return remote(sbuf.at[at], sbuf.at[at], piv_s.at[q], piv_r.at[at], chip(q)[1])

    def pivot_twin(at):
        return remote(sbuf.at[at], sbuf.at[at], piv_s.at[16 + at], piv_r.at[at], (1, row, cg))

    @pl.when(sub == 0)
    def _():
        each(1, 8, lambda q: head(q, line(q)).wait_recv())
        half = iota((NB, 128), 1) < 64
        rows = [
            jnp.where(half, head_recv[2 * p], pltpu.roll(head_recv[2 * p + 1], 64, 1))
            for p in range(4)
        ]
        sbuf[row] = jnp.concatenate(rows, axis=1)
        each(1, 16, lambda q: pivot(q, row).start())
        pivot_twin(row).start()

    bulk_out(1)

    @pl.when(moves)
    def _():
        swap().wait_recv()

    @pl.when(jnp.logical_not(moves))
    def _():
        swapped[...] = piece[...]

    gx, gy = row // 4, row % 4

    def xmate(j):
        return (gx + j) % 4 * 4 + gy

    def ymate(j):
        return gx * 4 + (gy + j) % 4

    def fan(k, at, to):
        return remote(swapped, cols_ref.at[at], fan_s.at[k], fan_r.at[0, at], (sub, to, cg))

    def far(half, k, at, to):
        part = cols_ref.at[at, pl.ds(half * 128, 128)]
        return remote(part, part, far_s.at[half, k], fan_r.at[half, at], (sub, to, cg))

    def hand(at, src):
        return remote(src, cols_ref.at[at], pass_s.at[at % 16], fan_r.at[0, at], twin)

    def near(j):
        x, y = xmate(j), ymate(j)
        fan(j, sub * 16 + x, x).wait_recv()
        each(1, 4, lambda i: far(0, j * 4 + i, sub * 16 + x, ymate(i)).start())
        hand(sub * 16 + x, cols_ref.at[sub * 16 + x]).start()
        fan(4 + j, sub * 16 + y, y).wait_recv()
        each(1, 4, lambda i: far(1, j * 4 + i, sub * 16 + y, xmate(i)).start())
        hand(sub * 16 + y, cols_ref.at[sub * 16 + y]).start()

    def corner(i, j):
        at = sub * 16 + (gx + i) % 4 * 4 + (gy + j) % 4
        far(0, 0, at, 0).wait_recv()
        far(1, 0, at, 0).wait_recv()
        hand(at, cols_ref.at[at]).start()

    cols_local = pltpu.make_async_copy(swapped, cols_ref.at[rg], loc_s.at[1])

    def fan_out(j):
        fan(j, rg, xmate(j)).start()
        fan(4 + j, rg, ymate(j)).start()

    each(1, 4, fan_out)
    hand(rg, swapped).start()
    cols_local.start()
    own_up(0, cg, piece).start()
    own_down(0, cg, piece).start()
    own_local.start()

    cross_half(0)

    @pl.when(sub == 0)
    def _():
        def relay(q):
            at = chip(q)[0]
            pivot(q, at).wait_recv()
            pivot_twin(at).start()

        each(1, 16, relay)

    @pl.when(sub == 1)
    def _():
        each(0, 16, lambda q: pivot_twin(q).wait_recv())

    turned = sbuf[...].reshape(PW, PW).T
    for c8 in range(8):
        for half in range(2):
            src = (c8 * 2 + half) * NB
            w_ref[(half * 8 + c8) * NB : (half * 8 + c8 + 1) * NB, :PW] = turned[src : src + NB, :]
    r, c = iota((PW, PW), 0), iota((PW, PW), 1)
    raw = w_ref[:, :PW]
    w_ref[:, :PW] = jnp.where(c >= r, raw, F32(0.0)) + jnp.where(c > r, raw, F32(0.0)).T
    w_ref[:, PW:] = jnp.where(r == c, F32(1.0), F32(0.0))

    def step(kb, carry):
        at = pl.multiple_of(kb * 128, 128)
        upper, inverse = sweep(w_ref[pl.ds(at, 128), pl.ds(at, 128)])
        rows = exact(inverse, w_ref[pl.ds(at, 128), :], ((1,), (0,)))
        lanes = iota((128, PW), 1)
        ahead = jnp.where(lanes >= at + 128, rows[:, :PW], F32(0.0))

        @pl.when(kb < 3)
        def _():
            w_ref[...] = w_ref[...] - exact(ahead, rows, ((0,), (0,)))

        w_ref[pl.ds(at, 128), :] = jnp.concatenate([ahead, rows[:, PW:]], axis=1)
        w_ref[pl.ds(at, 128), pl.ds(at, 128)] = upper

        ring(kb + 1)

        @pl.when(kb == 0)
        def _():
            each(1, 4, near)

        @pl.when(kb > 0)
        def _():
            each(1, 4, lambda j: corner(kb, j))

        @pl.when(kb == 1)
        def _():
            cross_half(1)

        return carry

    lax.fori_loop(0, PW // 128, step, 0)
    turned = w_ref[:, PW:].T
    for c8 in range(8):
        for half in range(2):
            src = (half * 8 + c8) * NB
            inv_ref[(c8 * 2 + half) * NB : (c8 * 2 + half + 1) * NB, :] = turned[src : src + NB, :]
    ih[...], il[...] = split(inv_ref[...])
    w_ref[:, :PW] = w_ref[:, :PW].T
    known = w_ref[pl.ds(pl.multiple_of(jnp.minimum(rg, 15) * NB, NB), NB), :PW]

    own_up(0, line(4), piece).wait_recv()
    own_down(0, line(3), piece).wait_recv()
    own_local.wait()
    for t in range(4):
        tile = unpack([own_ref[c, t * 64 : t * 64 + 64, :] for c in range(8)], left)
        rows = three(split(tile), (ih[...], il[...]), mm)
        if t == 0:
            keep = (iota((128, PW), 0) < NB) & (rg < 16)
            rows = jnp.where(
                keep, jnp.concatenate([known, jnp.zeros((128 - NB, PW), F32)], axis=0), rows
            )
        fh[t * 128 : t * 128 + 128, :], fl[t * 128 : t * 128 + 128, :] = split(rows)
    lane = iota((PW, 128), 1)
    nat = ((lane >> 5) * 8 + cg) * 32 + (lane & 31)
    pick = onehot((nat == iota((PW, 128), 0)) & (lane < 64))
    panel_ref[...] = mm(fh[...], pick) + mm(fl[...], pick)

    each(0, 16, lambda q: hand((1 - sub) * 16 + q, swapped).wait_recv())
    cols_local.wait()
    for v in range(4):
        parts = []
        for i in range(4):
            tile = unpack(
                [cols_ref[i * 8 + c, v * 64 : v * 64 + 64, :] for c in range(8)], left
            )
            parts.append(three(split(tile), (ih[...], il[...]), mm))
        cols = split(
            jnp.concatenate(
                [parts[i][q * NB : q * NB + NB] for q in range(4) for i in range(4)], axis=0
            )
        )
        down = pl.ds(v * 128, 512 - v * 128)
        acc_ref[down, pl.ds(v * 512, 512)] = three((fh[down, :], fl[down, :]), cols, mt)

    each(0, 16, lambda q: hand(sub * 16 + q, swapped).wait_send())

    def sent(j):
        fan(j, rg, xmate(j)).wait_send()
        fan(4 + j, rg, ymate(j)).wait_send()
        each(1, 4, lambda i: far(0, j * 4 + i, rg, ymate(i)).wait_send())
        each(1, 4, lambda i: far(1, j * 4 + i, rg, xmate(i)).wait_send())

    each(1, 4, sent)
    each(0, 4, lambda t: own_up(t, cg, piece).wait_send())
    each(0, 3, lambda t: own_down(t, cg, piece).wait_send())
    each(1, 32, lambda q: to_plane(q).wait_send())
    for h in range(2):

        @pl.when(cg <= last)
        def _(h=h):
            each(1, 8, lambda q: bulk(h, line(q), cg).wait_send())

        cross_in(h)
        by_level(lambda p, level: cross(h, p, rg, level).wait_send())
        keep_own(h).wait()

    @pl.when(cg == 0)
    def _():
        each(1, 8, lambda q: to_line(q).wait_send())

    @pl.when(moves)
    def _():
        swap().wait_send()

    @pl.when(sub == 0)
    def _():
        each(1, 8, lambda q: head(q, cg).wait_send())
        each(1, 16, lambda q: pivot(q, row).wait_send())
        each(0, 16, lambda q: pivot_twin(q).wait_send())


def final_kernel(
    at_ref, slot_ref, col_ref, x_ref, front_ref, acc_ref, panel_ref, o_ref, yh, yl,
):
    rg, cg = at_ref[0], at_ref[1]
    ct = pl.program_id(0)

    @pl.when(ct == 0)
    def _():
        for child in range(2):
            pick = row_picker(slot_ref[child], 16 * CAP)
            for h in range(2):
                got = x_ref[h, child * 16 : child * 16 + 16].reshape(16 * CAP, 512)
                r, lane = iota(got.shape, 0), iota(got.shape, 1)
                limit = jnp.where(r < 4 * CAP, 128, jnp.where(r < 8 * CAP, 256, 384))
                got = jnp.where((lane < limit) | (r >= 12 * CAP), got, F32(0.0))
                high, low = split(got)
                at = pl.ds(h * 512, 512)
                yh[child, :, at], yl[child, :, at] = split(mm(pick, high) + mm(pick, low))

    for v in range(4):

        @pl.when(ct == v)
        def _(v=v):
            top = v * 128
            down = pl.ds(top, 512 - top)
            total = front_ref[down, :] - acc_ref[down, :]
            for child in range(2):
                m = jnp.concatenate(
                    [col_ref[child, v * 4 + j : v * 4 + j + 1, :] for j in range(4)], axis=1
                )
                m = jnp.where(m < 0, -1, ((m >> 6) & 1) * 512 + (m >> 7) * 64 + (m & 63))
                put = onehot(m == iota((1024, 512), 0))
                total = total + mm(yh[child, down, :], put) + mm(yl[child, down, :], put)
            r, c = top + iota(total.shape, 0), v * 512 + iota(total.shape, 1)
            nat_row = ((r >> 5) * 32 + rg) * 32 + (r & 31)
            nat_col = ((c >> 5) * 8 + cg) * 32 + (c & 31)
            total = jnp.where(nat_row >= nat_col, total, F32(0.0))
            if v == 0:
                lane = iota((512, 128), 1)
                value = jnp.where(natural_lower(rg, cg, 512, 128, 0), panel_ref[...], F32(0.0))
                o_ref[:, :128] = jnp.where(lane < 64, value, total[:, :128])
                o_ref[:, 128:] = total[:, 128:]
            else:
                o_ref[:top, :] = jnp.zeros((top, 512), F32)
                o_ref[down, :] = total


def body(front, child_blocks, child_map):
    sub, row, cg = lax.axis_index("sub"), lax.axis_index("row"), lax.axis_index("col")
    rg = sub * 16 + row
    at = jnp.stack([rg, cg]).astype(I32)
    DMA = pltpu.SemaphoreType.DMA
    slots, cols, product, panel, received = pl.pallas_call(
        panel_kernel,
        out_shape=(
            jax.ShapeDtypeStruct((2, NB, 16), I32),
            jax.ShapeDtypeStruct((2, 16, 128), I32),
            jax.ShapeDtypeStruct((512, 2048), F32),
            jax.ShapeDtypeStruct((512, 128), F32),
            jax.ShapeDtypeStruct((2, 32, CAP, 512), F32),
        ),
        grid=(1,),
        in_specs=[
            pl.BlockSpec((2, 8192), lambda i: (0, 0)),
            pl.BlockSpec((512, 1024), lambda i: (0, 0)),
            pl.BlockSpec((512, 128), lambda i: (0, 0)),
        ],
        out_specs=(
            pl.BlockSpec((2, NB, 16), lambda i: (0, 0, 0)),
            pl.BlockSpec((2, 16, 128), lambda i: (0, 0, 0)),
            pl.BlockSpec((512, 2048), lambda i: (0, 0)),
            pl.BlockSpec((512, 128), lambda i: (0, 0)),
            pl.BlockSpec(memory_space=pl.ANY),
        ),
        scratch_shapes=[
            pltpu.VMEM((8, 256, 128), F32),
            pltpu.VMEM((32, 256, 128), F32),
            pltpu.VMEM((PW, PW), F32),
            pltpu.VMEM((PW, PW), BF16),
            pltpu.VMEM((PW, PW), BF16),
            pltpu.VMEM((512, PW), BF16),
            pltpu.VMEM((512, PW), BF16),
            pltpu.VMEM((2, 8, 64, 512), F32),
            pltpu.VMEM((2, 8, 64, 512), F32),
            pltpu.VMEM((2, 32, CAP, 512), F32),
            pltpu.VMEM((8, 64, 512), F32),
            pltpu.VMEM((128, 512), F32),
            pltpu.VMEM((32, CAP, 128), F32),
            pltpu.VMEM((32, CAP, 128), F32),
            pltpu.VMEM((256, 128), F32),
            pltpu.VMEM((256, 128), F32),
            pltpu.VMEM((NB, 128), F32),
            pltpu.VMEM((8, NB, 128), F32),
            pltpu.VMEM((16, NB, PW), F32),
            pltpu.VMEM((PW, 2 * PW), F32),
            DMA((8,)), DMA, DMA((32,)), DMA((32,)), DMA((8,)), DMA((8,)), DMA((8,)), DMA((8,)),
            DMA, DMA, DMA((32,)), DMA((16,)), DMA((8,)), DMA((2, 32)), DMA((16,)), DMA((4,)),
            DMA((2, 8)), DMA((2, 8)), DMA((2, 32)), DMA((2, 32)),
            pltpu.VMEM((64, 128), F32), DMA((2, 16)),
        ],
        name="panel",
        compiler_params=pltpu.CompilerParams(
            collective_id=1, has_side_effects=True, vmem_limit_bytes=56 << 20
        ),
        cost_estimate=pl.CostEstimate(flops=3 * 10**10, bytes_accessed=10**8, transcendentals=0),
    )(child_map, child_blocks[0], front)

    return pl.pallas_call(
        final_kernel,
        out_shape=jax.ShapeDtypeStruct((512, 2048), F32),
        grid=(4,),
        in_specs=[
            SM,
            pl.BlockSpec((2, NB, 16), lambda i: (0, 0, 0)),
            pl.BlockSpec((2, 16, 128), lambda i: (0, 0, 0)),
            pl.BlockSpec((2, 32, CAP, 512), lambda i: (0, 0, 0, 0)),
            pl.BlockSpec((512, 512), lambda i: (0, i)),
            pl.BlockSpec((512, 512), lambda i: (0, i)),
            pl.BlockSpec((512, 128), lambda i: (0, 0)),
        ],
        out_specs=pl.BlockSpec((512, 512), lambda i: (0, i)),
        scratch_shapes=[
            pltpu.VMEM((2, 512, 1024), BF16),
            pltpu.VMEM((2, 512, 1024), BF16),
        ],
        name="final",
        compiler_params=params(60),
    )(
        at,
        slots,
        cols,
        received,
        front,
        product,
        panel,
    )


def solution(mesh):
    return jax.shard_map(
        body,
        mesh=mesh,
        in_specs=(P(("sub", "row"), "col"), P("sub", "row", "col"), P()),
        out_specs=P(("sub", "row"), "col"),
        check_vma=False,
    )
```

```python
import functools

import jax
import jax.numpy as jnp
from jax import lax
from jax.experimental import pallas as pl
from jax.experimental.pallas import tpu as pltpu
from jax.sharding import PartitionSpec as P

PW = 512
NB = 32
CAP = 24
F32 = jnp.float32
BF16 = jnp.bfloat16
I32 = jnp.int32
AXES = ("sub", "row", "col")


def iota(shape, dim):
    return lax.broadcasted_iota(I32, shape, dim)


def onehot(cond):
    return jnp.where(cond, F32(1.0), F32(0.0)).astype(BF16)


def split(value):
    high = value.astype(BF16)
    return high, (value - high.astype(F32)).astype(BF16)


def mm(a, b):
    return lax.dot_general(a, b, (((1,), (0,)), ((), ())), preferred_element_type=F32)


def mt(a, b):
    return lax.dot_general(a, b, (((1,), (1,)), ((), ())), preferred_element_type=F32)


def params(mib=None):
    return pltpu.CompilerParams(vmem_limit_bytes=None if mib is None else mib << 20)


VM = pl.BlockSpec(memory_space=pltpu.VMEM)
SM = pl.BlockSpec(memory_space=pltpu.SMEM)


def ranks_of(owner, groups, rows):
    n = owner.shape[1]
    member = jnp.where(owner == iota((rows, n), 0), F32(1.0), F32(0.0))
    upto = onehot(iota((n, n), 0) <= iota((n, n), 1))
    counts = mm(member.astype(BF16), upto)
    return (jnp.sum(counts * member, axis=0, keepdims=True) - 1.0).astype(I32)


def index_work(rg, cg, map_ref, slot_ref, col_ref, flat_ref):
    upto = onehot(iota((512, 512), 0) <= iota((512, 512), 1))
    before64 = onehot(iota((64, 64), 1) < iota((64, 64), 0))
    before128 = onehot(iota((128, 128), 0) < iota((128, 128), 1))
    for child in range(2):
        chunks = [map_ref[child : child + 1, k * 512 : k * 512 + 512] for k in range(16)]
        match = onehot(((jnp.concatenate(chunks, axis=0) >> 5) & 31) == rg)
        counts = mm(match, upto)
        slots = jnp.zeros((NB, 16), F32)
        present = jnp.zeros((64, 128), F32)
        for k in range(16):
            here = chunks[k]
            block = here >> 5
            off = jnp.where((here & 31) == iota((128, 512), 0), F32(1.0), F32(0.0))
            own_rows = onehot(
                jnp.where((block & 31) == rg, block >> 5, -1) == iota((16, 512), 0)
            )
            ranked = (off[:NB] * counts[k : k + 1, :]).astype(BF16)
            off = off.astype(BF16)
            slots = slots + mt(ranked, own_rows) + F32(k * CAP) * mt(off[:NB], own_rows)
            own_cols = onehot(jnp.where((block & 7) == cg, block >> 3, -1) == iota((64, 512), 0))
            present = present + mt(own_cols, off)
        slot_ref[child] = slots.astype(I32) - 1
        pb = present.astype(BF16)
        ahead = jnp.sum(mm(before64, pb), axis=1, keepdims=True)
        place = ahead + mm(pb, before128)
        flat_ref[...] = jnp.where(present > 0.5, place + 1.0, F32(0.0))
        flat = flat_ref[pl.ds(0, 16, stride=4), :]
        for i in range(1, 4):
            flat = flat + pltpu.roll(flat_ref[pl.ds(i, 16, stride=4), :], NB * i, 1)
        col_ref[child] = flat.astype(I32) - 1


def natural_lower(rg, cg, rows, cols, col0):
    r, c = iota((rows, cols), 0), col0 + iota((rows, cols), 1)
    nat_row = ((r >> 5) * 32 + rg) * 32 + (r & 31)
    nat_col = ((c >> 5) * 8 + cg) * 32 + (c & 31)
    return nat_row >= nat_col


def row_picker(slots, n):
    parts = [onehot(slots[:, b : b + 1] == iota((NB, n), 1)) for b in range(16)]
    return jnp.concatenate(parts, axis=0)


GROUP = 8


def sweep(w):
    lane = iota((1, 128), 1)
    below = w
    done = []
    for k0 in range(0, 128, GROUP):
        n = 128 - k0
        column = [jnp.broadcast_to(below[:, k0 + j : k0 + j + 1], (n, 128)) for j in range(GROUP)]
        row = [below[j : j + 1, :] for j in range(GROUP)]
        scaled = []
        for j in range(GROUP):
            inv = 1.0 / column[j][j : j + 1, :]
            scaled.append(jnp.where(lane == k0 + j, F32(1.0), row[j]) * inv)
            for i in range(j + 1, GROUP):
                ratio = column[i][j : j + 1, :] * inv
                kept = jnp.where(lane == k0 + j, F32(0.0), row[i])
                row[i] = kept - column[j][i : i + 1, :] * scaled[j]
                column[i] = column[i] - column[j] * ratio
        done.extend(row)
        if n > GROUP:
            inside = (lane >= k0) & (lane < k0 + GROUP)
            rest = jnp.where(inside, F32(0.0), below[GROUP:])
            for j in range(GROUP):
                part = jnp.where((lane > k0 + j) & inside, F32(0.0), scaled[j])
                rest = rest - column[j][GROUP:] * part
            below = rest
    w = jnp.concatenate(done, axis=0)
    r, c = iota((128, 128), 0), iota((128, 128), 1)
    diag = jnp.sum(jnp.where(r == c, w, F32(0.0)), axis=1, keepdims=True)
    scale = 1.0 / jnp.sqrt(diag)
    upper = jnp.where(c >= r, w, F32(0.0)) * scale
    inverse = jnp.where(c < r, w, jnp.where(c == r, F32(1.0), F32(0.0))) * scale
    return upper, inverse


def exact(a, b, dims):
    return lax.dot_general(
        a, b, (dims, ((), ())), precision=lax.Precision.HIGHEST, preferred_element_type=F32
    )


def unpack(pieces, left):
    top, bottom = [], []
    for p in range(4):
        a, b = pieces[2 * p], pieces[2 * p + 1]
        top.append(jnp.where(left, a, pltpu.roll(b, 64, 1)))
        bottom.append(jnp.where(left, pltpu.roll(a, 64, 1), b))
    return jnp.concatenate(
        [jnp.concatenate(top, axis=1), jnp.concatenate(bottom, axis=1)], axis=0
    )


def three(a, b, dot):
    return dot(a[0], b[0]) + (dot(a[0], b[1]) + dot(a[1], b[0]))


def remote(src, dst, send, recv, device):
    return pltpu.make_async_remote_copy(
        src_ref=src, dst_ref=dst, send_sem=send, recv_sem=recv, device_id=device,
        device_id_type=pl.DeviceIdType.MESH,
    )


def panel_kernel(
    map_ref, child_ref, front_ref,
    slot_ref, col_ref, acc_ref, panel_ref, got_ref,
    own_ref, cols_ref, inv_ref, ih, il, fh, fl,
    zsend, zrecv, xsend, pan_send, pan_recv, rows_send, rows_recv, piece, swapped, head_send, head_recv, sbuf, w_ref,
    pan_s, pan_r, row_s, row_r, head_s, head_r, own_s, own_r, swap_s, swap_r, piv_s, piv_r,
    fan_s, fan_r, pass_s, loc_s, z_s, z_r, x_s, x_r, flat_ref, far_s,
):
    sub, row, cg = lax.axis_index("sub"), lax.axis_index("row"), lax.axis_index("col")
    rg = sub * 16 + row
    quarter, place = rg // 8, rg % 8
    mate = quarter * 8 + cg
    mate_id = (mate // 16, mate % 16, place)
    moves = place != cg
    twin = (1 - sub, row, cg)

    cmap = map_ref[pl.ds(sub, 1), pl.ds(pl.multiple_of(cg * 1024, 1024), 1024)]
    rmap = map_ref[pl.ds(sub, 1), pl.ds(pl.multiple_of(row * 512, 512), 512)]

    def each(first, last, fn):
        def go(q, carry):
            fn(q)
            return carry

        lax.fori_loop(first, last, go, 0)

    def line(q):
        return (cg + q) % 8

    def plane(q):
        p = (rg + q) % 32
        return p, (p // 16, p % 16, cg)

    def chip(q):
        r = (row + q) % 16
        return r, (sub, r, cg)

    barrier = pltpu.get_barrier_semaphore()

    def greet(device):
        pl.semaphore_signal(barrier, inc=1, device_id=device, device_id_type=pl.DeviceIdType.MESH)

    each(1, 8, lambda q: greet((sub, row, line(q))))
    each(1, 32, lambda q: greet(plane(q)[1]))

    @pl.when(moves)
    def _():
        greet(mate_id)

    pl.semaphore_wait(barrier, jnp.where(moves, 39, 38))

    pan_recv[64:, :] = jnp.zeros((64, 512), F32)

    def to_line(q):
        return remote(
            pan_send.at[q], pan_recv.at[pl.ds(0, 64)], pan_s.at[q], pan_r, (sub, row, q)
        )

    @pl.when(cg == 0)
    def _():
        keep = row * 512 + iota((512, 512), 0) >= iota((512, 512), 1)
        high, low = split(jnp.where(keep, child_ref[:, :512], F32(0.0)))
        n = iota((512, 512), 0)
        nat = (((n >> 5) & 1) * 8 + (n >> 6)) * NB + (n & 31)
        pick = onehot(cmap[:, :512] == nat)
        out = mt(pick, high) + mt(pick, low)
        for q in range(1, 8):
            pan_send[q] = out[q * 64 : q * 64 + 64, :]
            to_line(q).start()
        pan_recv[:64, :] = out[:64, :]

    def bulk(h, q, at):
        return remote(
            zsend.at[h, q], zrecv.at[h, at], z_s.at[h, q], z_r.at[h, at], (sub, row, q)
        )

    keep = row * 512 + iota((512, 1024), 0) >= cg * 1024 + iota((512, 1024), 1)
    high, low = split(jnp.where(keep, child_ref[...], F32(0.0)))
    owner = (cmap >> 5) & 7
    slot = owner * 128 + ranks_of(owner, 8, 16)

    def bulk_half(h, high=high, low=low, slot=slot):
        n = iota((512, 1024), 0)
        pick = onehot(slot == (n >> 6) * 128 + h * 64 + (n & 63))
        out = mt(pick, high) + mt(pick, low)
        for q in range(8):
            zsend[h, q] = out[q * 64 : q * 64 + 64, :]
        zrecv[h, cg] = zsend[h, cg]

    last = row // 2
    for c in range(1, 8):

        @pl.when(c > last)
        def _(c=c):
            zrecv[0, c] = jnp.zeros((64, 512), F32)
            zrecv[1, c] = jnp.zeros((64, 512), F32)

    def bulk_out(h):
        @pl.when(cg <= last)
        def _():
            each(1, 8, lambda q: bulk(h, line(q), cg).start())

    def bulk_in(h):
        def one(c):
            @pl.when(c != cg)
            def _():
                bulk(h, c, c).wait_recv()

        each(0, last + 1, one)

    bulk_half(0)
    owner = (rmap >> 5) & 31
    slot = owner * CAP + ranks_of(owner, 32, 32)
    pick_rows = onehot(slot == iota((32 * CAP, 512), 0))
    index_work(rg, cg, map_ref, slot_ref, col_ref, flat_ref)

    @pl.when(cg != 0)
    def _():
        to_line(cg).wait_recv()

    bulk_out(0)

    high, low = split(pan_recv[...])
    out = mt(pick_rows, high) + mt(pick_rows, low)
    for p in range(32):
        rows_send[p] = out[p * CAP : p * CAP + CAP, :]

    def to_plane(q):
        p, device = plane(q)
        return remote(rows_send.at[p], rows_recv.at[rg], row_s.at[p], row_r.at[rg], device)

    def from_plane(q):
        p, device = plane(q)
        return remote(rows_send.at[p], rows_recv.at[p], row_s.at[p], row_r.at[p], device)

    each(1, 32, lambda q: to_plane(q).start())
    rows_recv[rg] = rows_send[rg]
    bulk_half(1)
    total = jnp.where(natural_lower(rg, cg, 512, 128, 0), front_ref[...], F32(0.0))
    picks = [row_picker(slot_ref[child], 16 * CAP) for child in range(2)]
    each(1, 32, lambda q: from_plane(q).wait_recv())
    for child in range(2):
        got = rows_recv[child * 16 : child * 16 + 16].reshape(16 * CAP, 128)
        high, low = split(got)
        total = total + mm(picks[child], high) + mm(picks[child], low)
    left = iota((64, 128), 1) < 64
    for t in range(4):
        a = total[t * 128 : t * 128 + 64]
        b = total[t * 128 + 64 : t * 128 + 128]
        piece[t * 64 : t * 64 + 64, :] = jnp.where(left, a, pltpu.roll(b, 64, 1))
    head_send[...] = total[:NB, :]

    def head(q, at):
        return remote(
            head_send, head_recv.at[at], head_s.at[q], head_r.at[at], (sub, row, line(q))
        )

    def swap():
        return remote(piece, swapped, swap_s, swap_r, mate_id)

    def own_up(t, at, src):
        return remote(src, own_ref.at[at], own_s.at[t], own_r.at[at], (sub, row, line(1)))

    def own_down(t, at, src):
        return remote(src, own_ref.at[at], own_s.at[4 + t], own_r.at[at], (sub, row, line(7)))

    def ring(t):
        @pl.when(t < 4)
        def _():
            at = (cg + 8 - t) % 8
            own_up(t, at, own_ref.at[at]).wait_recv()
            own_up(t, at, own_ref.at[at]).start()

        @pl.when(t < 3)
        def _():
            at = (cg + t) % 8
            own_down(t, at, own_ref.at[at]).wait_recv()
            own_down(t, at, own_ref.at[at]).start()

    own_local = pltpu.make_async_copy(piece, own_ref.at[cg], loc_s.at[0])

    @pl.when(sub == 0)
    def _():
        each(1, 8, lambda q: head(q, cg).start())

    @pl.when(moves)
    def _():
        swap().start()

    head_recv[cg] = head_send[...]

    def cross(h, p, at, level):
        lanes = pl.ds(0, 128 * (level + 1))
        return remote(
            xsend.at[h, p, :, lanes], got_ref.at[h, at, :, lanes], x_s.at[h, p], x_r.at[h, at],
            (p // 16, p % 16, cg),
        )

    def by_level(fn):
        for level in range(4):

            @pl.when(row // 4 == level)
            def _(level=level):
                each(1, 32, lambda q: fn(plane(q)[0], level))

    def cross_out(h):
        by_level(lambda p, level: cross(h, p, rg, level).start())

    def cross_in(h):
        for level in range(4):

            def one(j):
                p = j // 4 * 16 + level * 4 + j % 4

                @pl.when(p != rg)
                def _():
                    cross(h, p, p, level).wait_recv()

            each(0, 8, one)

    def keep_own(h):
        return pltpu.make_async_copy(xsend.at[h, rg], got_ref.at[h, rg], loc_s.at[2 + h])

    def cross_half(h):
        bulk_in(h)
        high, low = split(zrecv[h].reshape(512, 512))
        out = mt(pick_rows, high) + mt(pick_rows, low)
        for p in range(32):
            xsend[h, p] = out[p * CAP : p * CAP + CAP, :]
        cross_out(h)
        keep_own(h).start()

    def pivot(q, at):
        return remote(sbuf.at[at], sbuf.at[at], piv_s.at[q], piv_r.at[at], chip(q)[1])

    def pivot_twin(at):
        return remote(sbuf.at[at], sbuf.at[at], piv_s.at[16 + at], piv_r.at[at], (1, row, cg))

    @pl.when(sub == 0)
    def _():
        each(1, 8, lambda q: head(q, line(q)).wait_recv())
        half = iota((NB, 128), 1) < 64
        rows = [
            jnp.where(half, head_recv[2 * p], pltpu.roll(head_recv[2 * p + 1], 64, 1))
            for p in range(4)
        ]
        sbuf[row] = jnp.concatenate(rows, axis=1)
        each(1, 16, lambda q: pivot(q, row).start())
        pivot_twin(row).start()

    bulk_out(1)

    @pl.when(moves)
    def _():
        swap().wait_recv()

    @pl.when(jnp.logical_not(moves))
    def _():
        swapped[...] = piece[...]

    gx, gy = row // 4, row % 4

    def xmate(j):
        return (gx + j) % 4 * 4 + gy

    def ymate(j):
        return gx * 4 + (gy + j) % 4

    def fan(k, at, to):
        return remote(swapped, cols_ref.at[at], fan_s.at[k], fan_r.at[0, at], (sub, to, cg))

    def far(half, k, at, to):
        part = cols_ref.at[at, pl.ds(half * 128, 128)]
        return remote(part, part, far_s.at[half, k], fan_r.at[half, at], (sub, to, cg))

    def hand(at, src):
        return remote(src, cols_ref.at[at], pass_s.at[at % 16], fan_r.at[0, at], twin)

    def near(j):
        x, y = xmate(j), ymate(j)
        fan(j, sub * 16 + x, x).wait_recv()
        each(1, 4, lambda i: far(0, j * 4 + i, sub * 16 + x, ymate(i)).start())
        hand(sub * 16 + x, cols_ref.at[sub * 16 + x]).start()
        fan(4 + j, sub * 16 + y, y).wait_recv()
        each(1, 4, lambda i: far(1, j * 4 + i, sub * 16 + y, xmate(i)).start())
        hand(sub * 16 + y, cols_ref.at[sub * 16 + y]).start()

    def corner(i, j):
        at = sub * 16 + (gx + i) % 4 * 4 + (gy + j) % 4
        far(0, 0, at, 0).wait_recv()
        far(1, 0, at, 0).wait_recv()
        hand(at, cols_ref.at[at]).start()

    cols_local = pltpu.make_async_copy(swapped, cols_ref.at[rg], loc_s.at[1])

    def fan_out(j):
        fan(j, rg, xmate(j)).start()
        fan(4 + j, rg, ymate(j)).start()

    each(1, 4, fan_out)
    hand(rg, swapped).start()
    cols_local.start()
    own_up(0, cg, piece).start()
    own_down(0, cg, piece).start()
    own_local.start()

    cross_half(0)

    @pl.when(sub == 0)
    def _():
        def relay(q):
            at = chip(q)[0]
            pivot(q, at).wait_recv()
            pivot_twin(at).start()

        each(1, 16, relay)

    @pl.when(sub == 1)
    def _():
        each(0, 16, lambda q: pivot_twin(q).wait_recv())

    turned = sbuf[...].reshape(PW, PW).T
    for c8 in range(8):
        for half in range(2):
            src = (c8 * 2 + half) * NB
            w_ref[(half * 8 + c8) * NB : (half * 8 + c8 + 1) * NB, :PW] = turned[src : src + NB, :]
    r, c = iota((PW, PW), 0), iota((PW, PW), 1)
    raw = w_ref[:, :PW]
    w_ref[:, :PW] = jnp.where(c >= r, raw, F32(0.0)) + jnp.where(c > r, raw, F32(0.0)).T
    w_ref[:, PW:] = jnp.where(r == c, F32(1.0), F32(0.0))

    def step(kb, carry):
        at = pl.multiple_of(kb * 128, 128)
        upper, inverse = sweep(w_ref[pl.ds(at, 128), pl.ds(at, 128)])
        rows = exact(inverse, w_ref[pl.ds(at, 128), :], ((1,), (0,)))
        lanes = iota((128, PW), 1)
        ahead = jnp.where(lanes >= at + 128, rows[:, :PW], F32(0.0))

        @pl.when(kb < 3)
        def _():
            w_ref[...] = w_ref[...] - exact(ahead, rows, ((0,), (0,)))

        w_ref[pl.ds(at, 128), :] = jnp.concatenate([ahead, rows[:, PW:]], axis=1)
        w_ref[pl.ds(at, 128), pl.ds(at, 128)] = upper

        ring(kb + 1)

        @pl.when(kb == 0)
        def _():
            each(1, 4, near)

        @pl.when(kb > 0)
        def _():
            each(1, 4, lambda j: corner(kb, j))

        @pl.when(kb == 1)
        def _():
            cross_half(1)

        return carry

    lax.fori_loop(0, PW // 128, step, 0)
    turned = w_ref[:, PW:].T
    for c8 in range(8):
        for half in range(2):
            src = (half * 8 + c8) * NB
            inv_ref[(c8 * 2 + half) * NB : (c8 * 2 + half + 1) * NB, :] = turned[src : src + NB, :]
    ih[...], il[...] = split(inv_ref[...])
    w_ref[:, :PW] = w_ref[:, :PW].T
    known = w_ref[pl.ds(pl.multiple_of(jnp.minimum(rg, 15) * NB, NB), NB), :PW]

    own_up(0, line(4), piece).wait_recv()
    own_down(0, line(3), piece).wait_recv()
    own_local.wait()
    for t in range(4):
        tile = unpack([own_ref[c, t * 64 : t * 64 + 64, :] for c in range(8)], left)
        rows = three(split(tile), (ih[...], il[...]), mm)
        if t == 0:
            keep = (iota((128, PW), 0) < NB) & (rg < 16)
            rows = jnp.where(
                keep, jnp.concatenate([known, jnp.zeros((128 - NB, PW), F32)], axis=0), rows
            )
        fh[t * 128 : t * 128 + 128, :], fl[t * 128 : t * 128 + 128, :] = split(rows)
    lane = iota((PW, 128), 1)
    nat = ((lane >> 5) * 8 + cg) * 32 + (lane & 31)
    pick = onehot((nat == iota((PW, 128), 0)) & (lane < 64))
    panel_ref[...] = mm(fh[...], pick) + mm(fl[...], pick)

    each(0, 16, lambda q: hand((1 - sub) * 16 + q, swapped).wait_recv())
    cols_local.wait()
    for v in range(4):
        parts = []
        for i in range(4):
            tile = unpack(
                [cols_ref[i * 8 + c, v * 64 : v * 64 + 64, :] for c in range(8)], left
            )
            parts.append(three(split(tile), (ih[...], il[...]), mm))
        cols = split(
            jnp.concatenate(
                [parts[i][q * NB : q * NB + NB] for q in range(4) for i in range(4)], axis=0
            )
        )
        down = pl.ds(v * 128, 512 - v * 128)
        acc_ref[down, pl.ds(v * 512, 512)] = three((fh[down, :], fl[down, :]), cols, mt)

    each(0, 16, lambda q: hand(sub * 16 + q, swapped).wait_send())

    def sent(j):
        fan(j, rg, xmate(j)).wait_send()
        fan(4 + j, rg, ymate(j)).wait_send()
        each(1, 4, lambda i: far(0, j * 4 + i, rg, ymate(i)).wait_send())
        each(1, 4, lambda i: far(1, j * 4 + i, rg, xmate(i)).wait_send())

    each(1, 4, sent)
    each(0, 4, lambda t: own_up(t, cg, piece).wait_send())
    each(0, 3, lambda t: own_down(t, cg, piece).wait_send())
    each(1, 32, lambda q: to_plane(q).wait_send())
    for h in range(2):

        @pl.when(cg <= last)
        def _(h=h):
            each(1, 8, lambda q: bulk(h, line(q), cg).wait_send())

        cross_in(h)
        by_level(lambda p, level: cross(h, p, rg, level).wait_send())
        keep_own(h).wait()

    @pl.when(cg == 0)
    def _():
        each(1, 8, lambda q: to_line(q).wait_send())

    @pl.when(moves)
    def _():
        swap().wait_send()

    @pl.when(sub == 0)
    def _():
        each(1, 8, lambda q: head(q, cg).wait_send())
        each(1, 16, lambda q: pivot(q, row).wait_send())
        each(0, 16, lambda q: pivot_twin(q).wait_send())


def final_kernel(
    at_ref, slot_ref, col_ref, x_ref, front_ref, acc_ref, panel_ref, o_ref, yh, yl,
):
    rg, cg = at_ref[0], at_ref[1]
    ct = pl.program_id(0)

    @pl.when(ct == 0)
    def _():
        for child in range(2):
            pick = row_picker(slot_ref[child], 16 * CAP)
            for h in range(2):
                got = x_ref[h, child * 16 : child * 16 + 16].reshape(16 * CAP, 512)
                r, lane = iota(got.shape, 0), iota(got.shape, 1)
                limit = jnp.where(r < 4 * CAP, 128, jnp.where(r < 8 * CAP, 256, 384))
                got = jnp.where((lane < limit) | (r >= 12 * CAP), got, F32(0.0))
                high, low = split(got)
                at = pl.ds(h * 512, 512)
                yh[child, :, at], yl[child, :, at] = split(mm(pick, high) + mm(pick, low))

    for v in range(4):

        @pl.when(ct == v)
        def _(v=v):
            top = v * 128
            down = pl.ds(top, 512 - top)
            total = front_ref[down, :] - acc_ref[down, :]
            for child in range(2):
                m = jnp.concatenate(
                    [col_ref[child, v * 4 + j : v * 4 + j + 1, :] for j in range(4)], axis=1
                )
                m = jnp.where(m < 0, -1, ((m >> 6) & 1) * 512 + (m >> 7) * 64 + (m & 63))
                put = onehot(m == iota((1024, 512), 0))
                total = total + mm(yh[child, down, :], put) + mm(yl[child, down, :], put)
            r, c = top + iota(total.shape, 0), v * 512 + iota(total.shape, 1)
            nat_row = ((r >> 5) * 32 + rg) * 32 + (r & 31)
            nat_col = ((c >> 5) * 8 + cg) * 32 + (c & 31)
            total = jnp.where(nat_row >= nat_col, total, F32(0.0))
            if v == 0:
                lane = iota((512, 128), 1)
                value = jnp.where(natural_lower(rg, cg, 512, 128, 0), panel_ref[...], F32(0.0))
                o_ref[:, :128] = jnp.where(lane < 64, value, total[:, :128])
                o_ref[:, 128:] = total[:, 128:]
            else:
                o_ref[:top, :] = jnp.zeros((top, 512), F32)
                o_ref[down, :] = total


def body(front, child_blocks, child_map):
    sub, row, cg = lax.axis_index("sub"), lax.axis_index("row"), lax.axis_index("col")
    rg = sub * 16 + row
    at = jnp.stack([rg, cg]).astype(I32)
    DMA = pltpu.SemaphoreType.DMA
    slots, cols, product, panel, received = pl.pallas_call(
        panel_kernel,
        out_shape=(
            jax.ShapeDtypeStruct((2, NB, 16), I32),
            jax.ShapeDtypeStruct((2, 16, 128), I32),
            jax.ShapeDtypeStruct((512, 2048), F32),
            jax.ShapeDtypeStruct((512, 128), F32),
            jax.ShapeDtypeStruct((2, 32, CAP, 512), F32),
        ),
        grid=(1,),
        in_specs=[
            pl.BlockSpec((2, 8192), lambda i: (0, 0)),
            pl.BlockSpec((512, 1024), lambda i: (0, 0)),
            pl.BlockSpec((512, 128), lambda i: (0, 0)),
        ],
        out_specs=(
            pl.BlockSpec((2, NB, 16), lambda i: (0, 0, 0)),
            pl.BlockSpec((2, 16, 128), lambda i: (0, 0, 0)),
            pl.BlockSpec((512, 2048), lambda i: (0, 0)),
            pl.BlockSpec((512, 128), lambda i: (0, 0)),
            pl.BlockSpec(memory_space=pl.ANY),
        ),
        scratch_shapes=[
            pltpu.VMEM((8, 256, 128), F32),
            pltpu.VMEM((32, 256, 128), F32),
            pltpu.VMEM((PW, PW), F32),
            pltpu.VMEM((PW, PW), BF16),
            pltpu.VMEM((PW, PW), BF16),
            pltpu.VMEM((512, PW), BF16),
            pltpu.VMEM((512, PW), BF16),
            pltpu.VMEM((2, 8, 64, 512), F32),
            pltpu.VMEM((2, 8, 64, 512), F32),
            pltpu.VMEM((2, 32, CAP, 512), F32),
            pltpu.VMEM((8, 64, 512), F32),
            pltpu.VMEM((128, 512), F32),
            pltpu.VMEM((32, CAP, 128), F32),
            pltpu.VMEM((32, CAP, 128), F32),
            pltpu.VMEM((256, 128), F32),
            pltpu.VMEM((256, 128), F32),
            pltpu.VMEM((NB, 128), F32),
            pltpu.VMEM((8, NB, 128), F32),
            pltpu.VMEM((16, NB, PW), F32),
            pltpu.VMEM((PW, 2 * PW), F32),
            DMA((8,)), DMA, DMA((32,)), DMA((32,)), DMA((8,)), DMA((8,)), DMA((8,)), DMA((8,)),
            DMA, DMA, DMA((32,)), DMA((16,)), DMA((8,)), DMA((2, 32)), DMA((16,)), DMA((4,)),
            DMA((2, 8)), DMA((2, 8)), DMA((2, 32)), DMA((2, 32)),
            pltpu.VMEM((64, 128), F32), DMA((2, 16)),
        ],
        name="panel",
        compiler_params=pltpu.CompilerParams(
            collective_id=1, has_side_effects=True, vmem_limit_bytes=56 << 20
        ),
        cost_estimate=pl.CostEstimate(flops=3 * 10**10, bytes_accessed=10**8, transcendentals=0),
    )(child_map, child_blocks[0], front)

    return pl.pallas_call(
        final_kernel,
        out_shape=jax.ShapeDtypeStruct((512, 2048), F32),
        grid=(4,),
        in_specs=[
            SM,
            pl.BlockSpec((2, NB, 16), lambda i: (0, 0, 0)),
            pl.BlockSpec((2, 16, 128), lambda i: (0, 0, 0)),
            pl.BlockSpec((2, 32, CAP, 512), lambda i: (0, 0, 0, 0)),
            pl.BlockSpec((512, 512), lambda i: (0, i)),
            pl.BlockSpec((512, 512), lambda i: (0, i)),
            pl.BlockSpec((512, 128), lambda i: (0, 0)),
        ],
        out_specs=pl.BlockSpec((512, 512), lambda i: (0, i)),
        scratch_shapes=[
            pltpu.VMEM((2, 512, 1024), BF16),
            pltpu.VMEM((2, 512, 1024), BF16),
        ],
        name="final",
        compiler_params=params(60),
    )(
        at,
        slots,
        cols,
        received,
        front,
        product,
        panel,
    )


def solution(mesh):
    return jax.shard_map(
        body,
        mesh=mesh,
        in_specs=(P(("sub", "row"), "col"), P("sub", "row", "col"), P()),
        out_specs=P(("sub", "row"), "col"),
        check_vma=False,
    )
```
